128 devices in a mesh: lon: 16 (over x_hi, y, core), lat: 8 (over x_lo, z).
Axes of the slice: x: 4 (x_hi: 2, x_lo: 2; x = x_hi * 2 + x_lo), y: 4, z: 4, core: 2. Of those that a mesh axis runs over, the one named last changes fastest.
Arguments:
- atmosphere: bfloat16 [256, 1024, 256], P('lat', 'lon'), may hold values from -6 to 6
- conv_weight: float32 [7, 7, 256], replicated, may hold values from -0.875 to 0.875
- atm_gain: float32 [256], replicated, may hold values from 0.1 to 1.9
- atm_up: bfloat16 [256, 1024], replicated, may hold values from -0.375 to 0.375
- atm_down: bfloat16 [1024, 256], replicated, may hold values from -0.1875 to 0.1875
- flux_weight: bfloat16 [256, 256], replicated, may hold values from -0.375 to 0.375
- land_mask: int32 [256, 1024], P('lat', 'lon'), may hold values from 0 to 1, as said below
- tile_owner: int32 [8, 16, 128], P('lat', 'lon'), may hold values from 0 to 127, as said below
- ocean_state: bfloat16 [128, 128, 2, 16, 256], P(('lat', 'lon')), may hold values from -6 to 6
- ocn_gain: float32 [256], replicated, may hold values from 0.1 to 1.9
- ocn_up: bfloat16 [256, 1024], replicated, may hold values from -0.375 to 0.375
- ocn_down: bfloat16 [1024, 256], replicated, may hold values from -0.1875 to 0.1875
Outputs:
- atm_out: bfloat16 [256, 1024, 256], P('lat', 'lon')
- ocean_out: bfloat16 [128, 128, 2, 16, 256], P(('lat', 'lon'))
The draws below stay inside these ranges and needn't reach their ends.
Inputs may be any that keep to these rules, and one draw needn't show every extreme that they name: `tile_owner`: each entry is the index along lat+lon (lat slowest) of the device that owns the tile. No device owns more than 2 tiles of one device's block, and one device owns exactly 2 tiles of every device's block. `land_mask`: no bound on the number of ocean cells of a tile or of a device may be relied on.
All inputs are finite; a program needn't handle non-finite values.
Results may differ from the reference program's by a relative error of at most 0.0056.
Values may be sent and summed in bfloat16 or wider, within the bound.
A program may use at most 64 MiB of HBM per device.

```python
import jax
import jax.numpy as jnp
from jax import lax

C = 256
HID = 1024
KW = 7
CLAT = 32
CLON = 64
CAP = 2
NLAT = 256
NLON = 1024
TPD = 128
TILE = 16
N_LON = 16
N_LAT = 8
DEVICES = 128


def draw_land_mask(key, part):
    key_cells, key_tiles, key_forced = jax.random.split(jax.random.fold_in(key, 7), 3)
    cells = (jax.random.randint(key_cells, (NLAT, NLON), 0, 3) < 2).astype(jnp.int32)
    dry_tiles = jax.random.randint(key_tiles, (N_LAT, N_LON, TPD), 0, 16) == 0
    forced = jax.random.randint(key_forced, (N_LAT, N_LON, 1), 0, TPD)
    dry_tiles = dry_tiles | (jnp.arange(TPD, dtype=jnp.int32)[None, None, :] == forced)
    keep_tiles = jnp.where(dry_tiles, 0, 1).astype(jnp.int32)
    keep_cells = jnp.broadcast_to(keep_tiles[:, :, :, None], (N_LAT, N_LON, TPD, TILE))
    keep_cells = keep_cells.reshape(N_LAT, N_LON, CLAT, CLON).transpose(0, 2, 1, 3).reshape(NLAT, NLON)
    return (cells * keep_cells).astype(jnp.int32)


def draw_tile_owner(key, part):
    blocks = N_LAT * N_LON
    slot_count = DEVICES * CAP
    key_favour, key_penalty, key_jitter, key_shuffle = jax.random.split(key, 4)
    favoured = jax.random.randint(key_favour, (), 0, DEVICES)
    penalty = jax.random.randint(key_penalty, (DEVICES,), 0, 4)
    slot_owner = jnp.arange(slot_count, dtype=jnp.int32) // CAP
    jitter = jax.random.randint(key_jitter, (blocks, slot_count), 0, 3072)
    scores = penalty[slot_owner][None, :] * 1024 + jitter
    scores = jnp.where(slot_owner[None, :] == favoured, -1, scores)
    scores = scores * slot_count + jnp.arange(slot_count, dtype=jnp.int32)[None, :]
    ranking = jnp.argsort(scores, axis=1)
    chosen = slot_owner[ranking[:, :TPD]]
    shuffle = jax.random.randint(key_shuffle, (blocks, TPD), 0, 1 << 20) * TPD + jnp.arange(TPD, dtype=jnp.int32)[None, :]
    chosen = jnp.take_along_axis(chosen, jnp.argsort(shuffle, axis=1), axis=1)
    return chosen.reshape(N_LAT, N_LON, TPD).astype(jnp.int32)


def block_levels(stream_key, dims, pieces, low, top_value):
    def one(dim, blocks):
        draws = jax.random.uniform(jax.random.fold_in(jax.random.fold_in(stream_key, 6), dim), (blocks,), jnp.float32, low / len(pieces), top_value / len(pieces))
        return jnp.repeat(jnp.exp(draws), dims[dim] // blocks).reshape((-1,) + (1,) * (len(dims) - dim - 1))

    gain = one(*pieces[0])
    for cut in pieces[1:]:
        gain = gain * one(*cut)
    return gain


def bell_draw(own_key, extent, scale, most, cuts=(), held_as=jnp.bfloat16):
    values = jax.random.normal(own_key, extent, jnp.float32) * scale
    if len(cuts) > 0:
        values = block_levels(own_key, extent, cuts, -0.22, 0.18) * values
    return jnp.clip(values, min=-most, max=most).astype(held_as)


def setup_inputs(seed: int = 0) -> dict:
    streams_of = jax.random.split(jax.random.key(seed), 13)
    atmosphere = bell_draw(streams_of[0], (NLAT, NLON, C), 1.0, 6.0, ((0, 8), (1, 16)))
    conv_weight = bell_draw(streams_of[1], (KW, KW, C), (KW * KW) ** -0.5, 0.875, (), jnp.float32)
    atm_gain = jnp.clip(1.0 + 0.18 * jax.random.normal(streams_of[2], (C,), jnp.float32), 0.1, 1.9)
    atm_up = bell_draw(streams_of[3], (C, HID), C ** -0.5, 0.375)
    atm_down = bell_draw(streams_of[4], (HID, C), HID ** -0.5, 0.1875)
    flux_weight = bell_draw(streams_of[5], (C, C), C ** -0.5, 0.375)
    land_mask = draw_land_mask(jax.random.fold_in(streams_of[12], 71), 0)
    tile_owner = draw_tile_owner(jax.random.fold_in(streams_of[12], 71), 0)
    ocean_state = bell_draw(streams_of[8], (DEVICES, DEVICES, CAP, TILE, C), 1.0, 6.0, ((0, 128),))
    ocn_gain = jnp.clip(1.0 + 0.18 * jax.random.normal(streams_of[9], (C,), jnp.float32), 0.1, 1.9)
    ocn_up = bell_draw(streams_of[10], (C, HID), C ** -0.5, 0.375)
    ocn_down = bell_draw(streams_of[11], (HID, C), HID ** -0.5, 0.1875)
    return dict(atmosphere=atmosphere, conv_weight=conv_weight, atm_gain=atm_gain, atm_up=atm_up, atm_down=atm_down, flux_weight=flux_weight, land_mask=land_mask, tile_owner=tile_owner, ocean_state=ocean_state, ocn_gain=ocn_gain, ocn_up=ocn_up, ocn_down=ocn_down)


def depthwise(padded, kernel, lat_rows, lon_cols):
    summed = jnp.zeros((lat_rows, lon_cols, padded.shape[2]), jnp.float32)
    for row_off in range(kernel.shape[0]):
        for col_off in range(kernel.shape[1]):
            window = padded[row_off:row_off + lat_rows, col_off:col_off + lon_cols, :].astype(jnp.float32)
            summed = summed + window * kernel[row_off, col_off]
    return summed

def normalize(values, scales):
    average = lax.optimization_barrier(jnp.mean(values, axis=-1, keepdims=True))
    centred = values - average
    spread = lax.optimization_barrier(jnp.mean(centred * centred, axis=-1, keepdims=True))
    return centred * lax.rsqrt(spread + 1e-06) * scales

def channel_mixer(values, scales, w_up, w_down):
    normed = normalize(values, scales).astype(jnp.bfloat16)
    hidden = jax.nn.gelu(jnp.dot(normed, w_up, preferred_element_type=jnp.float32), approximate=True).astype(jnp.bfloat16)
    return jnp.dot(hidden, w_down, preferred_element_type=jnp.float32)

def reference(atmosphere, conv_weight, atm_gain, atm_up, atm_down, flux_weight, land_mask, tile_owner, ocean_state, ocn_gain, ocn_up, ocn_down):
    margin = conv_weight.shape[0] // 2
    lon_padded = jnp.pad(atmosphere, ((0, 0), (margin, margin), (0, 0)), mode='wrap')
    padded = jnp.pad(lon_padded, ((margin, margin), (0, 0), (0, 0)))
    mixed = depthwise(padded, conv_weight, NLAT, NLON)

    def atmos_row(carried):
        mixed_row, atmos_in, mask_row = carried
        branch = channel_mixer(mixed_row, atm_gain, atm_up, atm_down)
        out_row = (atmos_in.astype(jnp.float32) + branch).astype(jnp.bfloat16)
        wet_cells = mask_row.astype(jnp.float32)[:, None]
        flux_row = (jnp.dot(out_row, flux_weight, preferred_element_type=jnp.float32) * wet_cells).astype(jnp.bfloat16)
        return (out_row, flux_row)
    atm_out, fluxes = lax.map(atmos_row, (mixed, atmosphere, land_mask))
    flux_tiles = fluxes.reshape(N_LAT, CLAT, N_LON, CLON, C).transpose(0, 2, 1, 3, 4).reshape(DEVICES, TPD, TILE, C)
    owners = tile_owner.reshape(DEVICES, TPD).astype(jnp.int32)
    member = (owners[:, :, None] == jnp.arange(DEVICES, dtype=jnp.int32)[None, None, :]).astype(jnp.int32)
    tile_rank = (lax.optimization_barrier(jnp.sum(jnp.cumsum(member, axis=1) * member, axis=2)) - 1).astype(jnp.int32)
    sources = jnp.broadcast_to(jnp.arange(DEVICES, dtype=jnp.int32)[:, None], owners.shape)
    gathered = ocean_state[owners, sources, tile_rank]

    def ocean_tiles(carried):
        states_in, flux_in = carried
        states = (states_in.astype(jnp.float32) + flux_in.astype(jnp.float32)).reshape(TPD * TILE, C)
        result = states + channel_mixer(states, ocn_gain, ocn_up, ocn_down)
        return result.astype(jnp.bfloat16).reshape(TPD, TILE, C)
    results = lax.map(ocean_tiles, (gathered, flux_tiles))
    ocean_out = jnp.zeros_like(ocean_state).at[owners, sources, tile_rank].set(results)
    return (atm_out, ocean_out)
```

```python
import jax
import jax.numpy as jnp
from jax import lax
from jax.sharding import PartitionSpec as P

AXES = ("lat", "lon")


def halo_pad(x, width):
    n_lat, n_lon = lax.axis_size("lat"), lax.axis_size("lon")
    rows, cols = x.shape[0], x.shape[1]

    def lin(l, c):
        return c * n_lat + l

    def shift(piece, d_lat, d_lon):
        pairs = []
        for l in range(n_lat):
            for c in range(n_lon):
                tl = l + d_lat
                if 0 <= tl < n_lat:
                    pairs.append((lin(l, c), lin(tl, (c + d_lon) % n_lon)))
        return lax.ppermute(piece, ("lon", "lat"), pairs)

    top_rows = x[:width]
    bottom_rows = x[rows - width:]
    left_cols = x[:, :width]
    right_cols = x[:, cols - width:]
    from_above = shift(bottom_rows, 1, 0)
    from_below = shift(top_rows, -1, 0)
    from_left = shift(right_cols, 0, 1)
    from_right = shift(left_cols, 0, -1)
    c_above_left = shift(x[rows - width:, cols - width:], 1, 1)
    c_above_right = shift(x[rows - width:, :width], 1, -1)
    c_below_left = shift(x[:width, cols - width:], -1, 1)
    c_below_right = shift(x[:width, :width], -1, -1)
    top = jnp.concatenate([c_above_left, from_above, c_above_right], axis=1)
    mid = jnp.concatenate([from_left, x, from_right], axis=1)
    bottom = jnp.concatenate([c_below_left, from_below, c_below_right], axis=1)
    return jnp.concatenate([top, mid, bottom], axis=0)


def depthwise(padded, kernel, lat_rows, lon_cols):
    summed = jnp.zeros((lat_rows, lon_cols, padded.shape[2]), jnp.float32)
    for row_off in range(kernel.shape[0]):
        for col_off in range(kernel.shape[1]):
            window = padded[row_off : row_off + lat_rows, col_off : col_off + lon_cols, :].astype(
                jnp.float32
            )
            summed = summed + window * kernel[row_off, col_off]
    return summed


def normalize(values, scales):
    average = jnp.mean(values, axis=-1, keepdims=True)
    centred = values - average
    spread = jnp.mean(centred * centred, axis=-1, keepdims=True)
    return centred * lax.rsqrt(spread + 1e-06) * scales


def channel_mixer(values, scales, w_up, w_down):
    normed = normalize(values, scales).astype(jnp.bfloat16)
    hidden = jax.nn.gelu(
        jnp.dot(normed, w_up, preferred_element_type=jnp.float32), approximate=True
    ).astype(jnp.bfloat16)
    return jnp.dot(hidden, w_down, preferred_element_type=jnp.float32)


def per_device(
    atmosphere,
    conv_weight,
    atm_gain,
    atm_up,
    atm_down,
    flux_weight,
    land_mask,
    tile_owner,
    ocean_state,
    ocn_gain,
    ocn_up,
    ocn_down,
):
    lat_rows, lon_cols, channels = atmosphere.shape
    margin = conv_weight.shape[0] // 2
    owners = tile_owner.reshape(-1)
    tile_count = owners.shape[0]
    peer_count = ocean_state.shape[1]
    capacity = ocean_state.shape[2]
    tile_cells = ocean_state.shape[3]
    all_owners = lax.all_gather(owners, AXES, axis=0, tiled=False)
    me = lax.axis_index("lat") * lax.axis_size("lon") + lax.axis_index("lon")
    mine = jnp.sum((all_owners == me).astype(jnp.int32), axis=1)
    filled = (jnp.arange(capacity, dtype=jnp.int32)[None, :] < mine[:, None]).astype(jnp.float32)

    padded = halo_pad(atmosphere, margin)
    mixed = depthwise(padded, conv_weight, lat_rows, lon_cols).reshape(
        lat_rows * lon_cols, channels
    )
    branch = channel_mixer(mixed, atm_gain, atm_up, atm_down)
    flat_atmos = atmosphere.reshape(lat_rows * lon_cols, channels)
    atmos_new = (flat_atmos.astype(jnp.float32) + branch).astype(jnp.bfloat16)
    wet_cells = land_mask.reshape(lat_rows * lon_cols, 1).astype(jnp.float32)
    fluxes = (
        jnp.dot(atmos_new, flux_weight, preferred_element_type=jnp.float32) * wet_cells
    ).astype(jnp.bfloat16)
    flux_tiles = fluxes.reshape(tile_count, tile_cells * channels)
    member = (owners[:, None] == jnp.arange(peer_count, dtype=jnp.int32)[None, :]).astype(jnp.int32)
    tile_rank = jnp.sum(jnp.cumsum(member, axis=0) * member, axis=1) - 1
    slot_index = owners * capacity + tile_rank
    onehot = (
        jnp.arange(peer_count * capacity, dtype=jnp.int32)[:, None] == slot_index[None, :]
    ).astype(jnp.bfloat16)
    outgoing = jnp.dot(onehot, flux_tiles, preferred_element_type=jnp.float32).astype(jnp.bfloat16)
    outgoing = outgoing.reshape(peer_count, capacity, tile_cells, channels)
    arrived = lax.all_to_all(outgoing, AXES, split_axis=0, concat_axis=0, tiled=True)
    states = ocean_state[0].astype(jnp.float32) + arrived.astype(jnp.float32)
    flat_states = states.reshape(peer_count * capacity * tile_cells, channels)
    result = flat_states + channel_mixer(flat_states, ocn_gain, ocn_up, ocn_down)
    result = result.reshape(peer_count, capacity, tile_cells, channels) * filled[:, :, None, None]
    ocean_out = result.astype(jnp.bfloat16)[None]
    return (atmos_new.reshape(lat_rows, lon_cols, channels), ocean_out)


def solution(mesh):
    placed = (
        P("lat", "lon", None),
        P(),
        P(),
        P(),
        P(),
        P(),
        P("lat", "lon"),
        P("lat", "lon", None),
        P(("lat", "lon"), None, None, None, None),
        P(),
        P(),
        P(),
    )
    return jax.shard_map(
        per_device,
        mesh=mesh,
        in_specs=placed,
        out_specs=(P("lat", "lon", None), P(("lat", "lon"), None, None, None, None)),
        check_vma=False,
    )
```

```python
import jax
import jax.numpy as jnp
from jax import lax
from jax.sharding import PartitionSpec as P

AXES = ("lat", "lon")


def padded_2(x, sides, width, wrap):
    for axis, dim in sides:
        devices, length = (lax.axis_size(axis), x.shape[dim])
        up = [(i, (i + 1) % devices) for i in range(devices if wrap else devices - 1)]
        down = [(j, i) for i, j in up]
        last = lax.slice_in_dim(x, length - width, length, axis=dim)
        leading = lax.slice_in_dim(x, 0, width, axis=dim)
        before = lax.ppermute(last, axis, up)
        after = lax.ppermute(leading, axis, down)
        x = jnp.concatenate([before, x, after], axis=dim)
    return x


def depthwise(padded, kernel, lat_rows, lon_cols):
    summed = jnp.zeros((lat_rows, lon_cols, padded.shape[2]), jnp.float32)
    for row_off in range(kernel.shape[0]):
        for col_off in range(kernel.shape[1]):
            window = padded[row_off : row_off + lat_rows, col_off : col_off + lon_cols, :].astype(
                jnp.float32
            )
            summed = summed + window * kernel[row_off, col_off]
    return summed


def normalize(values, scales):
    average = jnp.mean(values, axis=-1, keepdims=True)
    centred = values - average
    spread = jnp.mean(centred * centred, axis=-1, keepdims=True)
    return centred * lax.rsqrt(spread + 1e-06) * scales


def channel_mixer(values, scales, w_up, w_down):
    normed = normalize(values, scales).astype(jnp.bfloat16)
    hidden = jax.nn.gelu(
        jnp.dot(normed, w_up, preferred_element_type=jnp.float32), approximate=True
    ).astype(jnp.bfloat16)
    return jnp.dot(hidden, w_down, preferred_element_type=jnp.float32)


def per_device(
    atmosphere,
    conv_weight,
    atm_gain,
    atm_up,
    atm_down,
    flux_weight,
    land_mask,
    tile_owner,
    ocean_state,
    ocn_gain,
    ocn_up,
    ocn_down,
):
    lat_rows, lon_cols, channels = atmosphere.shape
    margin = conv_weight.shape[0] // 2
    owners = tile_owner.reshape(-1)
    tile_count = owners.shape[0]
    peer_count = ocean_state.shape[1]
    capacity = ocean_state.shape[2]
    tile_cells = ocean_state.shape[3]
    lon_padded = padded_2(atmosphere, (("lon", 1),), margin, True)
    padded = padded_2(lon_padded, (("lat", 0),), margin, False)
    mixed = depthwise(padded, conv_weight, lat_rows, lon_cols).reshape(
        lat_rows * lon_cols, channels
    )
    branch = channel_mixer(mixed, atm_gain, atm_up, atm_down)
    flat_atmos = atmosphere.reshape(lat_rows * lon_cols, channels)
    atmos_new = (flat_atmos.astype(jnp.float32) + branch).astype(jnp.bfloat16)
    wet_cells = land_mask.reshape(lat_rows * lon_cols, 1).astype(jnp.float32)
    fluxes = (
        jnp.dot(atmos_new, flux_weight, preferred_element_type=jnp.float32) * wet_cells
    ).astype(jnp.bfloat16)
    flux_tiles = fluxes.reshape(tile_count, tile_cells * channels)
    member = (owners[:, None] == jnp.arange(peer_count, dtype=jnp.int32)[None, :]).astype(jnp.int32)
    tile_rank = jnp.sum(jnp.cumsum(member, axis=0) * member, axis=1) - 1
    slot_index = owners * capacity + tile_rank
    onehot = (
        jnp.arange(peer_count * capacity, dtype=jnp.int32)[:, None] == slot_index[None, :]
    ).astype(jnp.bfloat16)
    outgoing = jnp.dot(onehot, flux_tiles, preferred_element_type=jnp.float32).astype(jnp.bfloat16)
    used = jnp.sum(onehot.astype(jnp.float32), axis=1) > 0
    outgoing = jnp.where(used[:, None], outgoing, jnp.nan).astype(jnp.bfloat16)
    outgoing = outgoing.reshape(peer_count, capacity, tile_cells, channels)
    arrived = lax.all_to_all(outgoing, AXES, split_axis=0, concat_axis=0, tiled=True)
    filled = arrived[:, :, 0, 0] == arrived[:, :, 0, 0]
    states = ocean_state[0].astype(jnp.float32) + arrived.astype(jnp.float32)
    flat_states = states.reshape(peer_count * capacity * tile_cells, channels)
    result = flat_states + channel_mixer(flat_states, ocn_gain, ocn_up, ocn_down)
    result = jnp.where(filled[:, :, None, None], result.reshape(peer_count, capacity, tile_cells, channels), 0.0)
    ocean_out = result.astype(jnp.bfloat16)[None]
    return (atmos_new.reshape(lat_rows, lon_cols, channels), ocean_out)


def solution(mesh):
    placed = (
        P("lat", "lon", None),
        P(),
        P(),
        P(),
        P(),
        P(),
        P("lat", "lon"),
        P("lat", "lon", None),
        P(("lat", "lon"), None, None, None, None),
        P(),
        P(),
        P(),
    )
    return jax.shard_map(
        per_device,
        mesh=mesh,
        in_specs=placed,
        out_specs=(P("lat", "lon", None), P(("lat", "lon"), None, None, None, None)),
        check_vma=False,
    )
```

```python
import functools

import jax
import jax.numpy as jnp
from jax import lax
from jax.experimental import pallas as pl
from jax.experimental.pallas import tpu as pltpu
from jax.sharding import PartitionSpec as P

MESH = pl.DeviceIdType.MESH

AXES = ("lat", "lon")


def padded_2(x, sides, width, wrap):
    for axis, dim in sides:
        devices, length = (lax.axis_size(axis), x.shape[dim])
        up = [(i, (i + 1) % devices) for i in range(devices if wrap else devices - 1)]
        down = [(j, i) for i, j in up]
        last = lax.slice_in_dim(x, length - width, length, axis=dim)
        leading = lax.slice_in_dim(x, 0, width, axis=dim)
        before = lax.ppermute(last, axis, up)
        after = lax.ppermute(leading, axis, down)
        x = jnp.concatenate([before, x, after], axis=dim)
    return x


def a2a_body(n_lon, n, out_ref, recv_ref, send_sems, recv_sems):
    me = lax.axis_index("lat") * n_lon + lax.axis_index("lon")

    def coords(d):
        return (lax.rem(d, n_lon), lax.div(d, n_lon))

    barrier = pltpu.get_barrier_semaphore()

    @pl.loop(1, n)
    def _(j):
        pl.semaphore_signal(barrier, inc=1, device_id=coords(lax.rem(me + j, n)), device_id_type=MESH)

    pl.semaphore_wait(barrier, n - 1)

    def send_copy(j):
        peer = lax.rem(me + j, n)
        return pltpu.make_async_remote_copy(
            src_ref=out_ref.at[peer],
            dst_ref=recv_ref.at[me],
            send_sem=send_sems.at[j],
            recv_sem=recv_sems.at[j],
            device_id=coords(peer),
            device_id_type=MESH,
        )

    def recv_copy(j):
        source = lax.rem(me - j + n, n)
        return pltpu.make_async_remote_copy(
            src_ref=out_ref.at[source],
            dst_ref=recv_ref.at[source],
            send_sem=send_sems.at[j],
            recv_sem=recv_sems.at[j],
            device_id=coords(source),
            device_id_type=MESH,
        )

    @pl.loop(1, n)
    def _(j):
        send_copy(j).start()

    recv_ref[me] = out_ref[me]

    @pl.loop(1, n)
    def _(j):
        send_copy(j).wait_send()
        recv_copy(j).wait_recv()


def all_to_all_kernel(outgoing):
    n_lon = lax.axis_size("lon")
    n = n_lon * lax.axis_size("lat")
    return pl.pallas_call(
        functools.partial(a2a_body, n_lon, n),
        out_shape=jax.ShapeDtypeStruct(outgoing.shape, outgoing.dtype),
        in_specs=[pl.BlockSpec(memory_space=pltpu.VMEM)],
        out_specs=pl.BlockSpec(memory_space=pltpu.VMEM),
        scratch_shapes=[pltpu.SemaphoreType.DMA((n,)), pltpu.SemaphoreType.DMA((n,))],
        compiler_params=pltpu.CompilerParams(collective_id=0, has_side_effects=True),
    )(outgoing)


def depthwise(padded, kernel, lat_rows, lon_cols):
    summed = jnp.zeros((lat_rows, lon_cols, padded.shape[2]), jnp.float32)
    for row_off in range(kernel.shape[0]):
        for col_off in range(kernel.shape[1]):
            window = padded[row_off : row_off + lat_rows, col_off : col_off + lon_cols, :].astype(
                jnp.float32
            )
            summed = summed + window * kernel[row_off, col_off]
    return summed


def normalize(values, scales):
    average = jnp.mean(values, axis=-1, keepdims=True)
    centred = values - average
    spread = jnp.mean(centred * centred, axis=-1, keepdims=True)
    return centred * lax.rsqrt(spread + 1e-06) * scales


def channel_mixer(values, scales, w_up, w_down):
    normed = normalize(values, scales).astype(jnp.bfloat16)
    hidden = jax.nn.gelu(
        jnp.dot(normed, w_up, preferred_element_type=jnp.float32), approximate=True
    ).astype(jnp.bfloat16)
    return jnp.dot(hidden, w_down, preferred_element_type=jnp.float32)


def per_device(
    atmosphere,
    conv_weight,
    atm_gain,
    atm_up,
    atm_down,
    flux_weight,
    land_mask,
    tile_owner,
    ocean_state,
    ocn_gain,
    ocn_up,
    ocn_down,
):
    lat_rows, lon_cols, channels = atmosphere.shape
    margin = conv_weight.shape[0] // 2
    owners = tile_owner.reshape(-1)
    tile_count = owners.shape[0]
    peer_count = ocean_state.shape[1]
    capacity = ocean_state.shape[2]
    tile_cells = ocean_state.shape[3]
    lon_padded = padded_2(atmosphere, (("lon", 1),), margin, True)
    padded = padded_2(lon_padded, (("lat", 0),), margin, False)
    mixed = depthwise(padded, conv_weight, lat_rows, lon_cols).reshape(
        lat_rows * lon_cols, channels
    )
    branch = channel_mixer(mixed, atm_gain, atm_up, atm_down)
    flat_atmos = atmosphere.reshape(lat_rows * lon_cols, channels)
    atmos_new = (flat_atmos.astype(jnp.float32) + branch).astype(jnp.bfloat16)
    wet_cells = land_mask.reshape(lat_rows * lon_cols, 1).astype(jnp.float32)
    fluxes = (
        jnp.dot(atmos_new, flux_weight, preferred_element_type=jnp.float32) * wet_cells
    ).astype(jnp.bfloat16)
    flux_tiles = fluxes.reshape(tile_count, tile_cells * channels)
    member = (owners[:, None] == jnp.arange(peer_count, dtype=jnp.int32)[None, :]).astype(jnp.int32)
    tile_rank = jnp.sum(jnp.cumsum(member, axis=0) * member, axis=1) - 1
    slot_index = owners * capacity + tile_rank
    onehot = (
        jnp.arange(peer_count * capacity, dtype=jnp.int32)[:, None] == slot_index[None, :]
    ).astype(jnp.bfloat16)
    outgoing = jnp.dot(onehot, flux_tiles, preferred_element_type=jnp.float32).astype(jnp.bfloat16)
    used = jnp.sum(onehot.astype(jnp.float32), axis=1) > 0
    outgoing = jnp.where(used[:, None], outgoing, jnp.nan).astype(jnp.bfloat16)
    outgoing = outgoing.reshape(peer_count, capacity, tile_cells, channels)
    arrived = all_to_all_kernel(outgoing)
    filled = arrived[:, :, 0, 0] == arrived[:, :, 0, 0]
    states = ocean_state[0].astype(jnp.float32) + arrived.astype(jnp.float32)
    flat_states = states.reshape(peer_count * capacity * tile_cells, channels)
    result = flat_states + channel_mixer(flat_states, ocn_gain, ocn_up, ocn_down)
    result = jnp.where(filled[:, :, None, None], result.reshape(peer_count, capacity, tile_cells, channels), 0.0)
    ocean_out = result.astype(jnp.bfloat16)[None]
    return (atmos_new.reshape(lat_rows, lon_cols, channels), ocean_out)


def solution(mesh):
    placed = (
        P("lat", "lon", None),
        P(),
        P(),
        P(),
        P(),
        P(),
        P("lat", "lon"),
        P("lat", "lon", None),
        P(("lat", "lon"), None, None, None, None),
        P(),
        P(),
        P(),
    )
    return jax.shard_map(
        per_device,
        mesh=mesh,
        in_specs=placed,
        out_specs=(P("lat", "lon", None), P(("lat", "lon"), None, None, None, None)),
        check_vma=False,
    )
```

```python
import functools

import jax
import jax.numpy as jnp
from jax import lax
from jax.experimental import pallas as pl
from jax.experimental.pallas import tpu as pltpu
from jax.sharding import PartitionSpec as P

MESH = pl.DeviceIdType.MESH

AXES = ("lat", "lon")


def padded_2(x, sides, width, wrap):
    for axis, dim in sides:
        devices, length = (lax.axis_size(axis), x.shape[dim])
        up = [(i, (i + 1) % devices) for i in range(devices if wrap else devices - 1)]
        down = [(j, i) for i, j in up]
        last = lax.slice_in_dim(x, length - width, length, axis=dim)
        leading = lax.slice_in_dim(x, 0, width, axis=dim)
        before = lax.ppermute(last, axis, up)
        after = lax.ppermute(leading, axis, down)
        x = jnp.concatenate([before, x, after], axis=dim)
    return x


def exchange_body(n_lon, n, group, out_ref, state_ref, gain_ref, up_ref, down_ref,
                  res_ref, recv_ref, stage_ref, send_sems, recv_sems):
    me = lax.axis_index("lat") * n_lon + lax.axis_index("lon")

    def coords(d):
        return (lax.rem(d, n_lon), lax.div(d, n_lon))

    barrier = pltpu.get_barrier_semaphore()

    @pl.loop(1, n)
    def _(j):
        pl.semaphore_signal(barrier, inc=1, device_id=coords(lax.rem(me + j, n)), device_id_type=MESH)

    pl.semaphore_wait(barrier, n - 1)

    def send_copy(j):
        peer = lax.rem(me + j, n)
        return pltpu.make_async_remote_copy(
            src_ref=out_ref.at[peer],
            dst_ref=recv_ref.at[j],
            send_sem=send_sems.at[j],
            recv_sem=recv_sems.at[j],
            device_id=coords(peer),
            device_id_type=MESH,
        )

    def recv_copy(j):
        source = lax.rem(me - j + n, n)
        return pltpu.make_async_remote_copy(
            src_ref=out_ref.at[source],
            dst_ref=recv_ref.at[j],
            send_sem=send_sems.at[j],
            recv_sem=recv_sems.at[j],
            device_id=coords(source),
            device_id_type=MESH,
        )

    @pl.loop(1, n)
    def _(j):
        send_copy(j).start()

    recv_ref[0] = out_ref[me]
    slots, cells, channels = out_ref.shape[1], out_ref.shape[2], out_ref.shape[3]
    rows = group * slots * cells

    @pl.loop(0, n // group)
    def _(g):
        base = g * group

        @pl.loop(0, group)
        def _(i):
            j = base + i

            @pl.when(j > 0)
            def _():
                recv_copy(j).wait_recv()

            stage_ref[i] = state_ref[lax.rem(me - j + n, n)]

        fluxes = recv_ref[pl.ds(base, group)]
        used = fluxes[:, :, 0:1, 0:1] == fluxes[:, :, 0:1, 0:1]
        states = (stage_ref[...].astype(jnp.float32) + fluxes.astype(jnp.float32)).reshape(rows, channels)
        average = jnp.mean(states, axis=-1, keepdims=True)
        centred = states - average
        spread = jnp.mean(centred * centred, axis=-1, keepdims=True)
        normed = (centred * lax.rsqrt(spread + 1e-06) * gain_ref[...]).astype(jnp.bfloat16)
        hidden = jax.nn.gelu(
            jnp.dot(normed, up_ref[...], preferred_element_type=jnp.float32), approximate=True
        ).astype(jnp.bfloat16)
        result = states + jnp.dot(hidden, down_ref[...], preferred_element_type=jnp.float32)
        result = result.reshape(group, slots, cells, channels)
        stage_ref[...] = jnp.where(used, result, 0.0).astype(jnp.bfloat16)

        @pl.loop(0, group)
        def _(i):
            res_ref[lax.rem(me - base - i + n, n)] = stage_ref[i]

    @pl.loop(1, n)
    def _(j):
        send_copy(j).wait_send()


def exchange_and_ocean(outgoing, state, gain, w_up, w_down):
    n_lon = lax.axis_size("lon")
    n = n_lon * lax.axis_size("lat")
    group = 16
    rows = outgoing.shape[0] * outgoing.shape[1] * outgoing.shape[2]
    channels, hid = w_up.shape
    vmem = pl.BlockSpec(memory_space=pltpu.VMEM)
    return pl.pallas_call(
        functools.partial(exchange_body, n_lon, n, group),
        out_shape=jax.ShapeDtypeStruct(outgoing.shape, outgoing.dtype),
        in_specs=[vmem] * 5,
        out_specs=vmem,
        scratch_shapes=[
            pltpu.VMEM(outgoing.shape, outgoing.dtype),
            pltpu.VMEM((group,) + outgoing.shape[1:], outgoing.dtype),
            pltpu.SemaphoreType.DMA((n,)),
            pltpu.SemaphoreType.DMA((n,)),
        ],
        compiler_params=pltpu.CompilerParams(
            collective_id=0, has_side_effects=True, vmem_limit_bytes=48 * 1024 * 1024
        ),
        cost_estimate=pl.CostEstimate(
            flops=4 * rows * channels * hid, transcendentals=rows * hid, bytes_accessed=4 * rows * channels * 2
        ),
    )(outgoing, state, gain.reshape(1, channels), w_up, w_down)


def depthwise(padded, kernel, lat_rows, lon_cols):
    summed = jnp.zeros((lat_rows, lon_cols, padded.shape[2]), jnp.float32)
    for row_off in range(kernel.shape[0]):
        for col_off in range(kernel.shape[1]):
            window = padded[row_off : row_off + lat_rows, col_off : col_off + lon_cols, :].astype(
                jnp.float32
            )
            summed = summed + window * kernel[row_off, col_off]
    return summed


def normalize(values, scales):
    average = jnp.mean(values, axis=-1, keepdims=True)
    centred = values - average
    spread = jnp.mean(centred * centred, axis=-1, keepdims=True)
    return centred * lax.rsqrt(spread + 1e-06) * scales


def channel_mixer(values, scales, w_up, w_down):
    normed = normalize(values, scales).astype(jnp.bfloat16)
    hidden = jax.nn.gelu(
        jnp.dot(normed, w_up, preferred_element_type=jnp.float32), approximate=True
    ).astype(jnp.bfloat16)
    return jnp.dot(hidden, w_down, preferred_element_type=jnp.float32)


def per_device(
    atmosphere,
    conv_weight,
    atm_gain,
    atm_up,
    atm_down,
    flux_weight,
    land_mask,
    tile_owner,
    ocean_state,
    ocn_gain,
    ocn_up,
    ocn_down,
):
    lat_rows, lon_cols, channels = atmosphere.shape
    margin = conv_weight.shape[0] // 2
    owners = tile_owner.reshape(-1)
    tile_count = owners.shape[0]
    peer_count = ocean_state.shape[1]
    capacity = ocean_state.shape[2]
    tile_cells = ocean_state.shape[3]
    lon_padded = padded_2(atmosphere, (("lon", 1),), margin, True)
    padded = padded_2(lon_padded, (("lat", 0),), margin, False)
    mixed = depthwise(padded, conv_weight, lat_rows, lon_cols).reshape(
        lat_rows * lon_cols, channels
    )
    branch = channel_mixer(mixed, atm_gain, atm_up, atm_down)
    flat_atmos = atmosphere.reshape(lat_rows * lon_cols, channels)
    atmos_new = (flat_atmos.astype(jnp.float32) + branch).astype(jnp.bfloat16)
    wet_cells = land_mask.reshape(lat_rows * lon_cols, 1).astype(jnp.float32)
    fluxes = (
        jnp.dot(atmos_new, flux_weight, preferred_element_type=jnp.float32) * wet_cells
    ).astype(jnp.bfloat16)
    flux_tiles = fluxes.reshape(tile_count, tile_cells * channels)
    member = (owners[:, None] == jnp.arange(peer_count, dtype=jnp.int32)[None, :]).astype(jnp.int32)
    tile_rank = jnp.sum(jnp.cumsum(member, axis=0) * member, axis=1) - 1
    slot_index = owners * capacity + tile_rank
    onehot = (
        jnp.arange(peer_count * capacity, dtype=jnp.int32)[:, None] == slot_index[None, :]
    ).astype(jnp.bfloat16)
    outgoing = jnp.dot(onehot, flux_tiles, preferred_element_type=jnp.float32).astype(jnp.bfloat16)
    used = jnp.sum(onehot.astype(jnp.float32), axis=1) > 0
    outgoing = jnp.where(used[:, None], outgoing, jnp.nan).astype(jnp.bfloat16)
    outgoing = outgoing.reshape(peer_count, capacity, tile_cells, channels)
    ocean_out = exchange_and_ocean(outgoing, ocean_state[0], ocn_gain, ocn_up, ocn_down)[None]
    return (atmos_new.reshape(lat_rows, lon_cols, channels), ocean_out)


def solution(mesh):
    placed = (
        P("lat", "lon", None),
        P(),
        P(),
        P(),
        P(),
        P(),
        P("lat", "lon"),
        P("lat", "lon", None),
        P(("lat", "lon"), None, None, None, None),
        P(),
        P(),
        P(),
    )
    return jax.shard_map(
        per_device,
        mesh=mesh,
        in_specs=placed,
        out_specs=(P("lat", "lon", None), P(("lat", "lon"), None, None, None, None)),
        check_vma=False,
    )
```

```python
import functools

import jax
import jax.numpy as jnp
from jax import lax
from jax.experimental import pallas as pl
from jax.experimental.pallas import tpu as pltpu
from jax.sharding import PartitionSpec as P

MESH = pl.DeviceIdType.MESH

AXES = ("lat", "lon")


HALO_MOVES = ((1, 0), (-1, 0), (0, 1), (0, -1), (1, 1), (1, -1), (-1, 1), (-1, -1))


def halo_body(n_lat, n_lon, *refs):
    pieces, got, send_sems, recv_sems = refs[:8], refs[8:16], refs[16], refs[17]
    lat, lon = lax.axis_index("lat"), lax.axis_index("lon")
    has_up = lat > 0
    has_down = lat < n_lat - 1

    def exists(d_lat):
        return has_down if d_lat > 0 else (has_up if d_lat < 0 else lat >= 0)

    def exists_from(d_lat):
        return has_up if d_lat > 0 else (has_down if d_lat < 0 else lat >= 0)

    def target(d_lat, d_lon):
        return (lax.rem(lon + d_lon + n_lon, n_lon), lat + d_lat)

    barrier = pltpu.get_barrier_semaphore()
    for d_lat, d_lon in HALO_MOVES:
        @pl.when(exists(d_lat))
        def _():
            pl.semaphore_signal(barrier, inc=1, device_id=target(d_lat, d_lon), device_id_type=MESH)

    pl.semaphore_wait(barrier, 2 + 3 * has_up.astype(jnp.int32) + 3 * has_down.astype(jnp.int32))

    def copy(p):
        d_lat, d_lon = HALO_MOVES[p]
        return pltpu.make_async_remote_copy(
            src_ref=pieces[p],
            dst_ref=got[p],
            send_sem=send_sems.at[p],
            recv_sem=recv_sems.at[p],
            device_id=target(d_lat, d_lon),
            device_id_type=MESH,
        )

    for p, (d_lat, d_lon) in enumerate(HALO_MOVES):
        @pl.when(exists(d_lat))
        def _():
            copy(p).start()

    for p, (d_lat, d_lon) in enumerate(HALO_MOVES):
        @pl.when(exists_from(d_lat))
        def _():
            copy(p).wait_recv()

        @pl.when(jnp.logical_not(exists_from(d_lat)))
        def _():
            got[p][...] = jnp.zeros(got[p].shape, got[p].dtype)

    for p, (d_lat, d_lon) in enumerate(HALO_MOVES):
        @pl.when(exists(d_lat))
        def _():
            copy(p).wait_send()


def halo_pad(x, w):
    rows, cols = x.shape[0], x.shape[1]
    pieces = (
        x[rows - w:], x[:w], x[:, cols - w:], x[:, :w],
        x[rows - w:, cols - w:], x[rows - w:, :w], x[:w, cols - w:], x[:w, :w],
    )
    vmem = pl.BlockSpec(memory_space=pltpu.VMEM)
    got = pl.pallas_call(
        functools.partial(halo_body, lax.axis_size("lat"), lax.axis_size("lon")),
        out_shape=tuple(jax.ShapeDtypeStruct(p.shape, p.dtype) for p in pieces),
        in_specs=[vmem] * 8,
        out_specs=tuple([vmem] * 8),
        scratch_shapes=[pltpu.SemaphoreType.DMA((8,)), pltpu.SemaphoreType.DMA((8,))],
        compiler_params=pltpu.CompilerParams(collective_id=1, has_side_effects=True),
    )(*pieces)
    above, below, left, right, above_left, above_right, below_left, below_right = got
    top = jnp.concatenate([above_left, above, above_right], axis=1)
    mid = jnp.concatenate([left, x, right], axis=1)
    bottom = jnp.concatenate([below_left, below, below_right], axis=1)
    return jnp.concatenate([top, mid, bottom], axis=0)


def exchange_body(n_lon, n, group, out_ref, state_ref, gain_ref, up_ref, down_ref,
                  res_ref, recv_ref, stage_ref, send_sems, recv_sems):
    me = lax.axis_index("lat") * n_lon + lax.axis_index("lon")

    def coords(d):
        return (lax.rem(d, n_lon), lax.div(d, n_lon))

    barrier = pltpu.get_barrier_semaphore()

    @pl.loop(1, n)
    def _(j):
        pl.semaphore_signal(barrier, inc=1, device_id=coords(lax.rem(me + j, n)), device_id_type=MESH)

    pl.semaphore_wait(barrier, n - 1)

    def send_copy(j):
        peer = lax.rem(me + j, n)
        return pltpu.make_async_remote_copy(
            src_ref=out_ref.at[peer],
            dst_ref=recv_ref.at[j],
            send_sem=send_sems.at[j],
            recv_sem=recv_sems.at[j],
            device_id=coords(peer),
            device_id_type=MESH,
        )

    def recv_copy(j):
        source = lax.rem(me - j + n, n)
        return pltpu.make_async_remote_copy(
            src_ref=out_ref.at[source],
            dst_ref=recv_ref.at[j],
            send_sem=send_sems.at[j],
            recv_sem=recv_sems.at[j],
            device_id=coords(source),
            device_id_type=MESH,
        )

    @pl.loop(1, n)
    def _(j):
        send_copy(j).start()

    recv_ref[0] = out_ref[me]
    slots, cells, channels = out_ref.shape[1], out_ref.shape[2], out_ref.shape[3]
    rows = group * slots * cells

    @pl.loop(0, n // group)
    def _(g):
        base = g * group

        @pl.loop(0, group)
        def _(i):
            j = base + i

            @pl.when(j > 0)
            def _():
                recv_copy(j).wait_recv()

            stage_ref[i] = state_ref[lax.rem(me - j + n, n)]

        fluxes = recv_ref[pl.ds(base, group)]
        used = fluxes[:, :, 0:1, 0:1] == fluxes[:, :, 0:1, 0:1]
        states = (stage_ref[...].astype(jnp.float32) + fluxes.astype(jnp.float32)).reshape(rows, channels)
        average = jnp.mean(states, axis=-1, keepdims=True)
        centred = states - average
        spread = jnp.mean(centred * centred, axis=-1, keepdims=True)
        normed = (centred * lax.rsqrt(spread + 1e-06) * gain_ref[...]).astype(jnp.bfloat16)
        hidden = jax.nn.gelu(
            jnp.dot(normed, up_ref[...], preferred_element_type=jnp.float32), approximate=True
        ).astype(jnp.bfloat16)
        result = states + jnp.dot(hidden, down_ref[...], preferred_element_type=jnp.float32)
        result = result.reshape(group, slots, cells, channels)
        stage_ref[...] = jnp.where(used, result, 0.0).astype(jnp.bfloat16)

        @pl.loop(0, group)
        def _(i):
            res_ref[lax.rem(me - base - i + n, n)] = stage_ref[i]

    @pl.loop(1, n)
    def _(j):
        send_copy(j).wait_send()


def exchange_and_ocean(outgoing, state, gain, w_up, w_down):
    n_lon = lax.axis_size("lon")
    n = n_lon * lax.axis_size("lat")
    group = 16
    rows = outgoing.shape[0] * outgoing.shape[1] * outgoing.shape[2]
    channels, hid = w_up.shape
    vmem = pl.BlockSpec(memory_space=pltpu.VMEM)
    return pl.pallas_call(
        functools.partial(exchange_body, n_lon, n, group),
        out_shape=jax.ShapeDtypeStruct(outgoing.shape, outgoing.dtype),
        in_specs=[vmem] * 5,
        out_specs=vmem,
        scratch_shapes=[
            pltpu.VMEM(outgoing.shape, outgoing.dtype),
            pltpu.VMEM((group,) + outgoing.shape[1:], outgoing.dtype),
            pltpu.SemaphoreType.DMA((n,)),
            pltpu.SemaphoreType.DMA((n,)),
        ],
        compiler_params=pltpu.CompilerParams(
            collective_id=0, has_side_effects=True, vmem_limit_bytes=48 * 1024 * 1024
        ),
        cost_estimate=pl.CostEstimate(
            flops=4 * rows * channels * hid, transcendentals=rows * hid, bytes_accessed=4 * rows * channels * 2
        ),
    )(outgoing, state, gain.reshape(1, channels), w_up, w_down)


def depthwise(padded, kernel, lat_rows, lon_cols):
    summed = jnp.zeros((lat_rows, lon_cols, padded.shape[2]), jnp.float32)
    for row_off in range(kernel.shape[0]):
        for col_off in range(kernel.shape[1]):
            window = padded[row_off : row_off + lat_rows, col_off : col_off + lon_cols, :].astype(
                jnp.float32
            )
            summed = summed + window * kernel[row_off, col_off]
    return summed


def normalize(values, scales):
    average = jnp.mean(values, axis=-1, keepdims=True)
    centred = values - average
    spread = jnp.mean(centred * centred, axis=-1, keepdims=True)
    return centred * lax.rsqrt(spread + 1e-06) * scales


def channel_mixer(values, scales, w_up, w_down):
    normed = normalize(values, scales).astype(jnp.bfloat16)
    hidden = jax.nn.gelu(
        jnp.dot(normed, w_up, preferred_element_type=jnp.float32), approximate=True
    ).astype(jnp.bfloat16)
    return jnp.dot(hidden, w_down, preferred_element_type=jnp.float32)


def per_device(
    atmosphere,
    conv_weight,
    atm_gain,
    atm_up,
    atm_down,
    flux_weight,
    land_mask,
    tile_owner,
    ocean_state,
    ocn_gain,
    ocn_up,
    ocn_down,
):
    lat_rows, lon_cols, channels = atmosphere.shape
    margin = conv_weight.shape[0] // 2
    owners = tile_owner.reshape(-1)
    tile_count = owners.shape[0]
    peer_count = ocean_state.shape[1]
    capacity = ocean_state.shape[2]
    tile_cells = ocean_state.shape[3]
    padded = halo_pad(atmosphere, margin)
    mixed = depthwise(padded, conv_weight, lat_rows, lon_cols).reshape(
        lat_rows * lon_cols, channels
    )
    branch = channel_mixer(mixed, atm_gain, atm_up, atm_down)
    flat_atmos = atmosphere.reshape(lat_rows * lon_cols, channels)
    atmos_new = (flat_atmos.astype(jnp.float32) + branch).astype(jnp.bfloat16)
    wet_cells = land_mask.reshape(lat_rows * lon_cols, 1).astype(jnp.float32)
    fluxes = (
        jnp.dot(atmos_new, flux_weight, preferred_element_type=jnp.float32) * wet_cells
    ).astype(jnp.bfloat16)
    flux_tiles = fluxes.reshape(tile_count, tile_cells * channels)
    member = (owners[:, None] == jnp.arange(peer_count, dtype=jnp.int32)[None, :]).astype(jnp.int32)
    tile_rank = jnp.sum(jnp.cumsum(member, axis=0) * member, axis=1) - 1
    slot_index = owners * capacity + tile_rank
    onehot = (
        jnp.arange(peer_count * capacity, dtype=jnp.int32)[:, None] == slot_index[None, :]
    ).astype(jnp.bfloat16)
    outgoing = jnp.dot(onehot, flux_tiles, preferred_element_type=jnp.float32).astype(jnp.bfloat16)
    used = jnp.sum(onehot.astype(jnp.float32), axis=1) > 0
    outgoing = jnp.where(used[:, None], outgoing, jnp.nan).astype(jnp.bfloat16)
    outgoing = outgoing.reshape(peer_count, capacity, tile_cells, channels)
    ocean_out = exchange_and_ocean(outgoing, ocean_state[0], ocn_gain, ocn_up, ocn_down)[None]
    return (atmos_new.reshape(lat_rows, lon_cols, channels), ocean_out)


def solution(mesh):
    placed = (
        P("lat", "lon", None),
        P(),
        P(),
        P(),
        P(),
        P(),
        P("lat", "lon"),
        P("lat", "lon", None),
        P(("lat", "lon"), None, None, None, None),
        P(),
        P(),
        P(),
    )
    return jax.shard_map(
        per_device,
        mesh=mesh,
        in_specs=placed,
        out_specs=(P("lat", "lon", None), P(("lat", "lon"), None, None, None, None)),
        check_vma=False,
    )
```

```python
import functools

import jax
import jax.numpy as jnp
from jax import lax
from jax.experimental import pallas as pl
from jax.experimental.pallas import tpu as pltpu
from jax.sharding import PartitionSpec as P

MESH = pl.DeviceIdType.MESH

AXES = ("lat", "lon")


HALO_MOVES = ((1, 0), (-1, 0), (0, 1), (0, -1), (1, 1), (1, -1), (-1, 1), (-1, -1))


def halo_body(n_lat, n_lon, *refs):
    pieces, got, send_sems, recv_sems = refs[:8], refs[8:16], refs[16], refs[17]
    lat, lon = lax.axis_index("lat"), lax.axis_index("lon")
    has_up = lat > 0
    has_down = lat < n_lat - 1

    def exists(d_lat):
        return has_down if d_lat > 0 else (has_up if d_lat < 0 else lat >= 0)

    def exists_from(d_lat):
        return has_up if d_lat > 0 else (has_down if d_lat < 0 else lat >= 0)

    def target(d_lat, d_lon):
        return (lax.rem(lon + d_lon + n_lon, n_lon), lat + d_lat)

    barrier = pltpu.get_barrier_semaphore()
    for d_lat, d_lon in HALO_MOVES:
        @pl.when(exists(d_lat))
        def _():
            pl.semaphore_signal(barrier, inc=1, device_id=target(d_lat, d_lon), device_id_type=MESH)

    pl.semaphore_wait(barrier, 2 + 3 * has_up.astype(jnp.int32) + 3 * has_down.astype(jnp.int32))

    def copy(p):
        d_lat, d_lon = HALO_MOVES[p]
        return pltpu.make_async_remote_copy(
            src_ref=pieces[p],
            dst_ref=got[p],
            send_sem=send_sems.at[p],
            recv_sem=recv_sems.at[p],
            device_id=target(d_lat, d_lon),
            device_id_type=MESH,
        )

    for p, (d_lat, d_lon) in enumerate(HALO_MOVES):
        @pl.when(exists(d_lat))
        def _():
            copy(p).start()

    for p, (d_lat, d_lon) in enumerate(HALO_MOVES):
        @pl.when(exists_from(d_lat))
        def _():
            copy(p).wait_recv()

        @pl.when(jnp.logical_not(exists_from(d_lat)))
        def _():
            got[p][...] = jnp.zeros(got[p].shape, got[p].dtype)

    for p, (d_lat, d_lon) in enumerate(HALO_MOVES):
        @pl.when(exists(d_lat))
        def _():
            copy(p).wait_send()


def halo_pad(x, w):
    rows, cols = x.shape[0], x.shape[1]
    pieces = (
        x[rows - w:], x[:w], x[:, cols - w:], x[:, :w],
        x[rows - w:, cols - w:], x[rows - w:, :w], x[:w, cols - w:], x[:w, :w],
    )
    vmem = pl.BlockSpec(memory_space=pltpu.VMEM)
    got = pl.pallas_call(
        functools.partial(halo_body, lax.axis_size("lat"), lax.axis_size("lon")),
        out_shape=tuple(jax.ShapeDtypeStruct(p.shape, p.dtype) for p in pieces),
        in_specs=[vmem] * 8,
        out_specs=tuple([vmem] * 8),
        scratch_shapes=[pltpu.SemaphoreType.DMA((8,)), pltpu.SemaphoreType.DMA((8,))],
        compiler_params=pltpu.CompilerParams(collective_id=1, has_side_effects=True),
    )(*pieces)
    above, below, left, right, above_left, above_right, below_left, below_right = got
    top = jnp.concatenate([above_left, above, above_right], axis=1)
    mid = jnp.concatenate([left, x, right], axis=1)
    bottom = jnp.concatenate([below_left, below, below_right], axis=1)
    return jnp.concatenate([top, mid, bottom], axis=0)


def exchange_body(n_lon, n, group, out_ref, state_ref, gain_ref, up_ref, down_ref,
                  res_ref, recv_ref, stage_ref, send_sems, recv_sems):
    me = lax.axis_index("lat") * n_lon + lax.axis_index("lon")

    def coords(d):
        return (lax.rem(d, n_lon), lax.div(d, n_lon))

    barrier = pltpu.get_barrier_semaphore()

    @pl.loop(1, n)
    def _(j):
        pl.semaphore_signal(barrier, inc=1, device_id=coords(lax.rem(me + j, n)), device_id_type=MESH)

    pl.semaphore_wait(barrier, n - 1)

    def send_copy(j):
        peer = lax.rem(me + j, n)
        return pltpu.make_async_remote_copy(
            src_ref=out_ref.at[peer],
            dst_ref=recv_ref.at[j],
            send_sem=send_sems.at[j],
            recv_sem=recv_sems.at[j],
            device_id=coords(peer),
            device_id_type=MESH,
        )

    def recv_copy(j):
        source = lax.rem(me - j + n, n)
        return pltpu.make_async_remote_copy(
            src_ref=out_ref.at[source],
            dst_ref=recv_ref.at[j],
            send_sem=send_sems.at[j],
            recv_sem=recv_sems.at[j],
            device_id=coords(source),
            device_id_type=MESH,
        )

    @pl.loop(1, n)
    def _(j):
        send_copy(j).start()

    recv_ref[0] = out_ref[me]
    slots, cells, channels = out_ref.shape[1], out_ref.shape[2], out_ref.shape[3]
    rows = group * slots * cells

    @pl.loop(0, n // group)
    def _(g):
        base = g * group

        @pl.loop(0, group)
        def _(i):
            j = base + i

            @pl.when(j > 0)
            def _():
                recv_copy(j).wait_recv()

            stage_ref[i] = state_ref[lax.rem(me - j + n, n)]

        fluxes = recv_ref[pl.ds(base, group)]
        used = fluxes[:, :, 0:1, 0:1] == fluxes[:, :, 0:1, 0:1]
        states = (stage_ref[...].astype(jnp.float32) + fluxes.astype(jnp.float32)).reshape(rows, channels)
        average = jnp.mean(states, axis=-1, keepdims=True)
        centred = states - average
        spread = jnp.mean(centred * centred, axis=-1, keepdims=True)
        normed = (centred * lax.rsqrt(spread + 1e-06) * gain_ref[...]).astype(jnp.bfloat16)
        hidden = jax.nn.gelu(
            jnp.dot(normed, up_ref[...], preferred_element_type=jnp.float32), approximate=True
        ).astype(jnp.bfloat16)
        result = states + jnp.dot(hidden, down_ref[...], preferred_element_type=jnp.float32)
        result = result.reshape(group, slots, cells, channels)
        stage_ref[...] = jnp.where(used, result, 0.0).astype(jnp.bfloat16)

        @pl.loop(0, group)
        def _(i):
            res_ref[lax.rem(me - base - i + n, n)] = stage_ref[i]

    @pl.loop(1, n)
    def _(j):
        send_copy(j).wait_send()


def exchange_and_ocean(outgoing, state, gain, w_up, w_down):
    n_lon = lax.axis_size("lon")
    n = n_lon * lax.axis_size("lat")
    group = 16
    rows = outgoing.shape[0] * outgoing.shape[1] * outgoing.shape[2]
    channels, hid = w_up.shape
    vmem = pl.BlockSpec(memory_space=pltpu.VMEM)
    return pl.pallas_call(
        functools.partial(exchange_body, n_lon, n, group),
        out_shape=jax.ShapeDtypeStruct(outgoing.shape, outgoing.dtype),
        in_specs=[vmem] * 5,
        out_specs=vmem,
        scratch_shapes=[
            pltpu.VMEM(outgoing.shape, outgoing.dtype),
            pltpu.VMEM((group,) + outgoing.shape[1:], outgoing.dtype),
            pltpu.SemaphoreType.DMA((n,)),
            pltpu.SemaphoreType.DMA((n,)),
        ],
        compiler_params=pltpu.CompilerParams(
            collective_id=0, has_side_effects=True, vmem_limit_bytes=48 * 1024 * 1024
        ),
        cost_estimate=pl.CostEstimate(
            flops=4 * rows * channels * hid, transcendentals=rows * hid, bytes_accessed=4 * rows * channels * 2
        ),
    )(outgoing, state, gain.reshape(1, channels), w_up, w_down)


def atmos_body(kw, band, pad_ref, w_ref, atm_ref, gain_ref, up_ref, down_ref, fw_ref, wet_ref,
               out_ref, flux_ref, xf_ref, mixed_ref):
    rows, cols, channels = atm_ref.shape
    xf_ref[:, : pad_ref.shape[1], :] = pad_ref[...].astype(jnp.float32)

    @pl.loop(0, rows // band)
    def _(b):
        r0 = b * band
        for cb in range(channels // 128):
            lanes = pl.ds(cb * 128, 128)
            acc = [jnp.zeros((cols, 128), jnp.float32) for _ in range(band)]
            for q in range(kw):
                for i in range(band + kw - 1):
                    line = xf_ref[r0 + i, pl.ds(q, cols), lanes]
                    for p in range(kw):
                        r = i - p
                        if 0 <= r < band:
                            acc[r] = acc[r] + line * w_ref[p, pl.ds(q, 1), lanes]
            for r in range(band):
                mixed_ref[r0 + r, :, lanes] = acc[r]

    chunk = 8

    @pl.loop(0, rows // chunk)
    def _(k):
        cells = chunk * cols
        mixed = mixed_ref[pl.ds(k * chunk, chunk)].reshape(cells, channels)
        average = jnp.mean(mixed, axis=-1, keepdims=True)
        centred = mixed - average
        spread = jnp.mean(centred * centred, axis=-1, keepdims=True)
        normed = (centred * lax.rsqrt(spread + 1e-06) * gain_ref[...]).astype(jnp.bfloat16)
        hidden = jax.nn.gelu(
            jnp.dot(normed, up_ref[...], preferred_element_type=jnp.float32), approximate=True
        ).astype(jnp.bfloat16)
        branch = jnp.dot(hidden, down_ref[...], preferred_element_type=jnp.float32)
        atmos = atm_ref[pl.ds(k * chunk, chunk)].reshape(cells, channels).astype(jnp.float32)
        new = (atmos + branch).astype(jnp.bfloat16)
        out_ref[pl.ds(k * chunk, chunk)] = new.reshape(chunk, cols, channels)
        flux = jnp.dot(new, fw_ref[...], preferred_element_type=jnp.float32) * wet_ref[pl.ds(k * cells, cells)]
        flux_ref[pl.ds(k * cells, cells)] = flux.astype(jnp.bfloat16)


def atmosphere_block(padded, conv_weight, atmosphere, gain, w_up, w_down, flux_weight, wet):
    rows, cols, channels = atmosphere.shape
    kw = conv_weight.shape[0]
    hid = w_up.shape[1]
    vmem = pl.BlockSpec(memory_space=pltpu.VMEM)
    cells = rows * cols
    return pl.pallas_call(
        functools.partial(atmos_body, kw, 4),
        out_shape=(
            jax.ShapeDtypeStruct(atmosphere.shape, atmosphere.dtype),
            jax.ShapeDtypeStruct((cells, channels), jnp.bfloat16),
        ),
        in_specs=[vmem] * 8,
        out_specs=(vmem, vmem),
        scratch_shapes=[
            pltpu.VMEM((padded.shape[0], -(-padded.shape[1] // 8) * 8, channels), jnp.float32),
            pltpu.VMEM((rows, cols, channels), jnp.float32),
        ],
        compiler_params=pltpu.CompilerParams(vmem_limit_bytes=48 * 1024 * 1024),
        cost_estimate=pl.CostEstimate(
            flops=2 * cells * channels * (kw * kw + 2 * hid + channels),
            transcendentals=cells * hid,
            bytes_accessed=cells * channels * 8,
        ),
    )(padded, conv_weight, atmosphere, gain.reshape(1, channels), w_up, w_down, flux_weight, wet)


def normalize(values, scales):
    average = jnp.mean(values, axis=-1, keepdims=True)
    centred = values - average
    spread = jnp.mean(centred * centred, axis=-1, keepdims=True)
    return centred * lax.rsqrt(spread + 1e-06) * scales


def channel_mixer(values, scales, w_up, w_down):
    normed = normalize(values, scales).astype(jnp.bfloat16)
    hidden = jax.nn.gelu(
        jnp.dot(normed, w_up, preferred_element_type=jnp.float32), approximate=True
    ).astype(jnp.bfloat16)
    return jnp.dot(hidden, w_down, preferred_element_type=jnp.float32)


def per_device(
    atmosphere,
    conv_weight,
    atm_gain,
    atm_up,
    atm_down,
    flux_weight,
    land_mask,
    tile_owner,
    ocean_state,
    ocn_gain,
    ocn_up,
    ocn_down,
):
    lat_rows, lon_cols, channels = atmosphere.shape
    margin = conv_weight.shape[0] // 2
    owners = tile_owner.reshape(-1)
    tile_count = owners.shape[0]
    peer_count = ocean_state.shape[1]
    capacity = ocean_state.shape[2]
    tile_cells = ocean_state.shape[3]
    padded = halo_pad(atmosphere, margin)
    wet_cells = land_mask.reshape(lat_rows * lon_cols, 1).astype(jnp.float32)
    atmos_new, fluxes = atmosphere_block(
        padded, conv_weight, atmosphere, atm_gain, atm_up, atm_down, flux_weight, wet_cells
    )
    flux_tiles = fluxes.reshape(tile_count, tile_cells * channels)
    member = (owners[:, None] == jnp.arange(peer_count, dtype=jnp.int32)[None, :]).astype(jnp.int32)
    tile_rank = jnp.sum(jnp.cumsum(member, axis=0) * member, axis=1) - 1
    slot_index = owners * capacity + tile_rank
    onehot = (
        jnp.arange(peer_count * capacity, dtype=jnp.int32)[:, None] == slot_index[None, :]
    ).astype(jnp.bfloat16)
    outgoing = jnp.dot(onehot, flux_tiles, preferred_element_type=jnp.float32).astype(jnp.bfloat16)
    used = jnp.sum(onehot.astype(jnp.float32), axis=1) > 0
    outgoing = jnp.where(used[:, None], outgoing, jnp.nan).astype(jnp.bfloat16)
    outgoing = outgoing.reshape(peer_count, capacity, tile_cells, channels)
    ocean_out = exchange_and_ocean(outgoing, ocean_state[0], ocn_gain, ocn_up, ocn_down)[None]
    return (atmos_new, ocean_out)


def solution(mesh):
    placed = (
        P("lat", "lon", None),
        P(),
        P(),
        P(),
        P(),
        P(),
        P("lat", "lon"),
        P("lat", "lon", None),
        P(("lat", "lon"), None, None, None, None),
        P(),
        P(),
        P(),
    )
    return jax.shard_map(
        per_device,
        mesh=mesh,
        in_specs=placed,
        out_specs=(P("lat", "lon", None), P(("lat", "lon"), None, None, None, None)),
        check_vma=False,
    )
```

```python
import functools

import jax
import jax.numpy as jnp
from jax import lax
from jax.experimental import pallas as pl
from jax.experimental.pallas import tpu as pltpu
from jax.sharding import PartitionSpec as P

MESH = pl.DeviceIdType.MESH

AXES = ("lat", "lon")


HALO_MOVES = ((1, 0), (-1, 0), (0, 1), (0, -1), (1, 1), (1, -1), (-1, 1), (-1, -1))


def halo_body(n_lat, n_lon, *refs):
    pieces, got, send_sems, recv_sems = refs[:8], refs[8:16], refs[16], refs[17]
    lat, lon = lax.axis_index("lat"), lax.axis_index("lon")
    has_up = lat > 0
    has_down = lat < n_lat - 1

    def exists(d_lat):
        return has_down if d_lat > 0 else (has_up if d_lat < 0 else lat >= 0)

    def exists_from(d_lat):
        return has_up if d_lat > 0 else (has_down if d_lat < 0 else lat >= 0)

    def target(d_lat, d_lon):
        return (lax.rem(lon + d_lon + n_lon, n_lon), lat + d_lat)

    barrier = pltpu.get_barrier_semaphore()
    for d_lat, d_lon in HALO_MOVES:
        @pl.when(exists(d_lat))
        def _():
            pl.semaphore_signal(barrier, inc=1, device_id=target(d_lat, d_lon), device_id_type=MESH)

    pl.semaphore_wait(barrier, 2 + 3 * has_up.astype(jnp.int32) + 3 * has_down.astype(jnp.int32))

    def copy(p):
        d_lat, d_lon = HALO_MOVES[p]
        return pltpu.make_async_remote_copy(
            src_ref=pieces[p],
            dst_ref=got[p],
            send_sem=send_sems.at[p],
            recv_sem=recv_sems.at[p],
            device_id=target(d_lat, d_lon),
            device_id_type=MESH,
        )

    for p, (d_lat, d_lon) in enumerate(HALO_MOVES):
        @pl.when(exists(d_lat))
        def _():
            copy(p).start()

    for p, (d_lat, d_lon) in enumerate(HALO_MOVES):
        @pl.when(exists_from(d_lat))
        def _():
            copy(p).wait_recv()

        @pl.when(jnp.logical_not(exists_from(d_lat)))
        def _():
            got[p][...] = jnp.zeros(got[p].shape, got[p].dtype)

    for p, (d_lat, d_lon) in enumerate(HALO_MOVES):
        @pl.when(exists(d_lat))
        def _():
            copy(p).wait_send()


def halo_pad(x, w):
    rows, cols = x.shape[0], x.shape[1]
    pieces = (
        x[rows - w:], x[:w], x[:, cols - w:], x[:, :w],
        x[rows - w:, cols - w:], x[rows - w:, :w], x[:w, cols - w:], x[:w, :w],
    )
    vmem = pl.BlockSpec(memory_space=pltpu.VMEM)
    got = pl.pallas_call(
        functools.partial(halo_body, lax.axis_size("lat"), lax.axis_size("lon")),
        out_shape=tuple(jax.ShapeDtypeStruct(p.shape, p.dtype) for p in pieces),
        in_specs=[vmem] * 8,
        out_specs=tuple([vmem] * 8),
        scratch_shapes=[pltpu.SemaphoreType.DMA((8,)), pltpu.SemaphoreType.DMA((8,))],
        compiler_params=pltpu.CompilerParams(collective_id=1, has_side_effects=True),
    )(*pieces)
    above, below, left, right, above_left, above_right, below_left, below_right = got
    top = jnp.concatenate([above_left, above, above_right], axis=1)
    mid = jnp.concatenate([left, x, right], axis=1)
    bottom = jnp.concatenate([below_left, below, below_right], axis=1)
    return jnp.concatenate([top, mid, bottom], axis=0)


def exchange_body(n_lon, n, group, out_ref, state_ref, gain_ref, up_ref, down_ref,
                  res_ref, recv_ref, stage_ref, send_sems, recv_sems):
    me = lax.axis_index("lat") * n_lon + lax.axis_index("lon")

    def coords(d):
        return (lax.rem(d, n_lon), lax.div(d, n_lon))

    barrier = pltpu.get_barrier_semaphore()

    @pl.loop(1, n)
    def _(j):
        pl.semaphore_signal(barrier, inc=1, device_id=coords(lax.rem(me + j, n)), device_id_type=MESH)

    pl.semaphore_wait(barrier, n - 1)

    def send_copy(j):
        peer = lax.rem(me + j, n)
        return pltpu.make_async_remote_copy(
            src_ref=out_ref.at[peer],
            dst_ref=recv_ref.at[j],
            send_sem=send_sems.at[j],
            recv_sem=recv_sems.at[j],
            device_id=coords(peer),
            device_id_type=MESH,
        )

    def recv_copy(j):
        source = lax.rem(me - j + n, n)
        return pltpu.make_async_remote_copy(
            src_ref=out_ref.at[source],
            dst_ref=recv_ref.at[j],
            send_sem=send_sems.at[j],
            recv_sem=recv_sems.at[j],
            device_id=coords(source),
            device_id_type=MESH,
        )

    @pl.loop(1, n)
    def _(j):
        send_copy(j).start()

    recv_ref[0] = out_ref[me]
    slots, cells, channels = out_ref.shape[1], out_ref.shape[2], out_ref.shape[3]
    rows = group * slots * cells

    @pl.loop(0, n // group)
    def _(g):
        base = g * group

        @pl.loop(0, group)
        def _(i):
            j = base + i

            @pl.when(j > 0)
            def _():
                recv_copy(j).wait_recv()

            stage_ref[i] = state_ref[lax.rem(me - j + n, n)]

        fluxes = recv_ref[pl.ds(base, group)]
        used = fluxes[:, :, 0:1, 0:1] == fluxes[:, :, 0:1, 0:1]
        states = (stage_ref[...].astype(jnp.float32) + fluxes.astype(jnp.float32)).reshape(rows, channels)
        average = jnp.mean(states, axis=-1, keepdims=True)
        centred = states - average
        spread = jnp.mean(centred * centred, axis=-1, keepdims=True)
        normed = (centred * lax.rsqrt(spread + 1e-06) * gain_ref[...]).astype(jnp.bfloat16)
        hidden = jax.nn.gelu(
            jnp.dot(normed, up_ref[...], preferred_element_type=jnp.float32), approximate=True
        ).astype(jnp.bfloat16)
        result = states + jnp.dot(hidden, down_ref[...], preferred_element_type=jnp.float32)
        result = result.reshape(group, slots, cells, channels)
        stage_ref[...] = jnp.where(used, result, 0.0).astype(jnp.bfloat16)

        @pl.loop(0, group)
        def _(i):
            res_ref[lax.rem(me - base - i + n, n)] = stage_ref[i]

    @pl.loop(1, n)
    def _(j):
        send_copy(j).wait_send()


def exchange_and_ocean(outgoing, state, gain, w_up, w_down):
    n_lon = lax.axis_size("lon")
    n = n_lon * lax.axis_size("lat")
    group = 16
    rows = outgoing.shape[0] * outgoing.shape[1] * outgoing.shape[2]
    channels, hid = w_up.shape
    vmem = pl.BlockSpec(memory_space=pltpu.VMEM)
    return pl.pallas_call(
        functools.partial(exchange_body, n_lon, n, group),
        out_shape=jax.ShapeDtypeStruct(outgoing.shape, outgoing.dtype),
        in_specs=[vmem] * 5,
        out_specs=vmem,
        scratch_shapes=[
            pltpu.VMEM(outgoing.shape, outgoing.dtype),
            pltpu.VMEM((group,) + outgoing.shape[1:], outgoing.dtype),
            pltpu.SemaphoreType.DMA((n,)),
            pltpu.SemaphoreType.DMA((n,)),
        ],
        compiler_params=pltpu.CompilerParams(
            collective_id=0, has_side_effects=True, vmem_limit_bytes=48 * 1024 * 1024
        ),
        cost_estimate=pl.CostEstimate(
            flops=4 * rows * channels * hid, transcendentals=rows * hid, bytes_accessed=4 * rows * channels * 2
        ),
    )(outgoing, state, gain.reshape(1, channels), w_up, w_down)


def atmos_body(kw, band, pad_ref, w_ref, atm_ref, gain_ref, up_hbm, down_hbm, fw_hbm, wet_ref,
               out_ref, flux_ref, xf_ref, xs_ref, mixed_ref, up_ref, down_ref, fw_ref, sems):
    rows, cols, channels = atm_ref.shape
    weights = [
        pltpu.make_async_copy(up_hbm, up_ref, sems.at[0]),
        pltpu.make_async_copy(down_hbm, down_ref, sems.at[1]),
        pltpu.make_async_copy(fw_hbm, fw_ref, sems.at[2]),
    ]
    for copy in weights:
        copy.start()
    xf_ref[:, : pad_ref.shape[1], :] = pad_ref[...].astype(jnp.float32)

    @pl.loop(0, pad_ref.shape[0])
    def _(i):
        for q in range(kw):
            xs_ref[q, i] = xf_ref[i, pl.ds(q, cols), :]

    @pl.loop(0, rows // band)
    def _(b):
        r0 = b * band
        for cb in range(channels // 128):
            lanes = pl.ds(cb * 128, 128)
            acc = [jnp.zeros((cols, 128), jnp.float32) for _ in range(band)]
            for q in range(kw):
                for i in range(band + kw - 1):
                    line = xs_ref[q, r0 + i, :, lanes]
                    for p in range(kw):
                        r = i - p
                        if 0 <= r < band:
                            acc[r] = acc[r] + line * w_ref[p, pl.ds(q, 1), lanes]
            for r in range(band):
                mixed_ref[r0 + r, :, lanes] = acc[r]

    for copy in weights:
        copy.wait()

    chunk = 8

    @pl.loop(0, rows // chunk)
    def _(k):
        cells = chunk * cols
        mixed = mixed_ref[pl.ds(k * chunk, chunk)].reshape(cells, channels)
        average = jnp.mean(mixed, axis=-1, keepdims=True)
        centred = mixed - average
        spread = jnp.mean(centred * centred, axis=-1, keepdims=True)
        normed = (centred * lax.rsqrt(spread + 1e-06) * gain_ref[...]).astype(jnp.bfloat16)
        hidden = jax.nn.gelu(
            jnp.dot(normed, up_ref[...], preferred_element_type=jnp.float32), approximate=True
        ).astype(jnp.bfloat16)
        branch = jnp.dot(hidden, down_ref[...], preferred_element_type=jnp.float32)
        atmos = atm_ref[pl.ds(k * chunk, chunk)].reshape(cells, channels).astype(jnp.float32)
        new = (atmos + branch).astype(jnp.bfloat16)
        out_ref[pl.ds(k * chunk, chunk)] = new.reshape(chunk, cols, channels)
        flux = jnp.dot(new, fw_ref[...], preferred_element_type=jnp.float32) * wet_ref[pl.ds(k * cells, cells)]
        flux_ref[pl.ds(k * cells, cells)] = flux.astype(jnp.bfloat16)


def atmosphere_block(padded, conv_weight, atmosphere, gain, w_up, w_down, flux_weight, wet):
    rows, cols, channels = atmosphere.shape
    kw = conv_weight.shape[0]
    hid = w_up.shape[1]
    vmem = pl.BlockSpec(memory_space=pltpu.VMEM)
    hbm = pl.BlockSpec(memory_space=pl.ANY)
    cells = rows * cols
    return pl.pallas_call(
        functools.partial(atmos_body, kw, 4),
        out_shape=(
            jax.ShapeDtypeStruct(atmosphere.shape, atmosphere.dtype),
            jax.ShapeDtypeStruct((cells, channels), jnp.bfloat16),
        ),
        in_specs=[vmem] * 4 + [hbm] * 3 + [vmem],
        out_specs=(vmem, vmem),
        scratch_shapes=[
            pltpu.VMEM((padded.shape[0], -(-padded.shape[1] // 8) * 8, channels), jnp.float32),
            pltpu.VMEM((kw, padded.shape[0], cols, channels), jnp.float32),
            pltpu.VMEM((rows, cols, channels), jnp.float32),
            pltpu.VMEM(w_up.shape, w_up.dtype),
            pltpu.VMEM(w_down.shape, w_down.dtype),
            pltpu.VMEM(flux_weight.shape, flux_weight.dtype),
            pltpu.SemaphoreType.DMA((3,)),
        ],
        compiler_params=pltpu.CompilerParams(vmem_limit_bytes=56 * 1024 * 1024),
        cost_estimate=pl.CostEstimate(
            flops=2 * cells * channels * (kw * kw + 2 * hid + channels),
            transcendentals=cells * hid,
            bytes_accessed=cells * channels * 8,
        ),
    )(padded, conv_weight, atmosphere, gain.reshape(1, channels), w_up, w_down, flux_weight, wet)


def normalize(values, scales):
    average = jnp.mean(values, axis=-1, keepdims=True)
    centred = values - average
    spread = jnp.mean(centred * centred, axis=-1, keepdims=True)
    return centred * lax.rsqrt(spread + 1e-06) * scales


def channel_mixer(values, scales, w_up, w_down):
    normed = normalize(values, scales).astype(jnp.bfloat16)
    hidden = jax.nn.gelu(
        jnp.dot(normed, w_up, preferred_element_type=jnp.float32), approximate=True
    ).astype(jnp.bfloat16)
    return jnp.dot(hidden, w_down, preferred_element_type=jnp.float32)


def per_device(
    atmosphere,
    conv_weight,
    atm_gain,
    atm_up,
    atm_down,
    flux_weight,
    land_mask,
    tile_owner,
    ocean_state,
    ocn_gain,
    ocn_up,
    ocn_down,
):
    lat_rows, lon_cols, channels = atmosphere.shape
    margin = conv_weight.shape[0] // 2
    owners = tile_owner.reshape(-1)
    tile_count = owners.shape[0]
    peer_count = ocean_state.shape[1]
    capacity = ocean_state.shape[2]
    tile_cells = ocean_state.shape[3]
    padded = halo_pad(atmosphere, margin)
    wet_cells = land_mask.reshape(lat_rows * lon_cols, 1).astype(jnp.float32)
    atmos_new, fluxes = atmosphere_block(
        padded, conv_weight, atmosphere, atm_gain, atm_up, atm_down, flux_weight, wet_cells
    )
    flux_tiles = fluxes.reshape(tile_count, tile_cells * channels)
    member = (owners[:, None] == jnp.arange(peer_count, dtype=jnp.int32)[None, :]).astype(jnp.int32)
    tile_rank = jnp.sum(jnp.cumsum(member, axis=0) * member, axis=1) - 1
    slot_index = owners * capacity + tile_rank
    onehot = (
        jnp.arange(peer_count * capacity, dtype=jnp.int32)[:, None] == slot_index[None, :]
    ).astype(jnp.bfloat16)
    outgoing = jnp.dot(onehot, flux_tiles, preferred_element_type=jnp.float32).astype(jnp.bfloat16)
    used = jnp.sum(onehot.astype(jnp.float32), axis=1) > 0
    outgoing = jnp.where(used[:, None], outgoing, jnp.nan).astype(jnp.bfloat16)
    outgoing = outgoing.reshape(peer_count, capacity, tile_cells, channels)
    ocean_out = exchange_and_ocean(outgoing, ocean_state[0], ocn_gain, ocn_up, ocn_down)[None]
    return (atmos_new, ocean_out)


def solution(mesh):
    placed = (
        P("lat", "lon", None),
        P(),
        P(),
        P(),
        P(),
        P(),
        P("lat", "lon"),
        P("lat", "lon", None),
        P(("lat", "lon"), None, None, None, None),
        P(),
        P(),
        P(),
    )
    return jax.shard_map(
        per_device,
        mesh=mesh,
        in_specs=placed,
        out_specs=(P("lat", "lon", None), P(("lat", "lon"), None, None, None, None)),
        check_vma=False,
    )
```

```python
import functools

import jax
import jax.numpy as jnp
from jax import lax
from jax.experimental import pallas as pl
from jax.experimental.pallas import tpu as pltpu
from jax.sharding import PartitionSpec as P

MESH = pl.DeviceIdType.MESH

AXES = ("lat", "lon")


HALO_MOVES = ((1, 0), (-1, 0), (0, 1), (0, -1), (1, 1), (1, -1), (-1, 1), (-1, -1))


def halo_body(n_lat, n_lon, *refs):
    pieces, got, send_sems, recv_sems = refs[:8], refs[8:16], refs[16], refs[17]
    lat, lon = lax.axis_index("lat"), lax.axis_index("lon")
    has_up = lat > 0
    has_down = lat < n_lat - 1

    def exists(d_lat):
        return has_down if d_lat > 0 else (has_up if d_lat < 0 else lat >= 0)

    def exists_from(d_lat):
        return has_up if d_lat > 0 else (has_down if d_lat < 0 else lat >= 0)

    def target(d_lat, d_lon):
        return (lax.rem(lon + d_lon + n_lon, n_lon), lat + d_lat)

    barrier = pltpu.get_barrier_semaphore()
    for d_lat, d_lon in HALO_MOVES:
        @pl.when(exists(d_lat))
        def _():
            pl.semaphore_signal(barrier, inc=1, device_id=target(d_lat, d_lon), device_id_type=MESH)

    pl.semaphore_wait(barrier, 2 + 3 * has_up.astype(jnp.int32) + 3 * has_down.astype(jnp.int32))

    def copy(p):
        d_lat, d_lon = HALO_MOVES[p]
        return pltpu.make_async_remote_copy(
            src_ref=pieces[p],
            dst_ref=got[p],
            send_sem=send_sems.at[p],
            recv_sem=recv_sems.at[p],
            device_id=target(d_lat, d_lon),
            device_id_type=MESH,
        )

    for p, (d_lat, d_lon) in enumerate(HALO_MOVES):
        @pl.when(exists(d_lat))
        def _():
            copy(p).start()

    for p, (d_lat, d_lon) in enumerate(HALO_MOVES):
        @pl.when(exists_from(d_lat))
        def _():
            copy(p).wait_recv()

        @pl.when(jnp.logical_not(exists_from(d_lat)))
        def _():
            got[p][...] = jnp.zeros(got[p].shape, got[p].dtype)

    for p, (d_lat, d_lon) in enumerate(HALO_MOVES):
        @pl.when(exists(d_lat))
        def _():
            copy(p).wait_send()


def halo_pad(x, w):
    rows, cols = x.shape[0], x.shape[1]
    pieces = (
        x[rows - w:], x[:w], x[:, cols - w:], x[:, :w],
        x[rows - w:, cols - w:], x[rows - w:, :w], x[:w, cols - w:], x[:w, :w],
    )
    vmem = pl.BlockSpec(memory_space=pltpu.VMEM)
    got = pl.pallas_call(
        functools.partial(halo_body, lax.axis_size("lat"), lax.axis_size("lon")),
        out_shape=tuple(jax.ShapeDtypeStruct(p.shape, p.dtype) for p in pieces),
        in_specs=[vmem] * 8,
        out_specs=tuple([vmem] * 8),
        scratch_shapes=[pltpu.SemaphoreType.DMA((8,)), pltpu.SemaphoreType.DMA((8,))],
        compiler_params=pltpu.CompilerParams(collective_id=1, has_side_effects=True),
    )(*pieces)
    above, below, left, right, above_left, above_right, below_left, below_right = got
    top = jnp.concatenate([above_left, above, above_right], axis=1)
    mid = jnp.concatenate([left, x, right], axis=1)
    bottom = jnp.concatenate([below_left, below, below_right], axis=1)
    return jnp.concatenate([top, mid, bottom], axis=0)


def exchange_body(n_lon, n, group, out_ref, state_ref, gain_ref, up_ref, down_ref,
                  res_ref, recv_ref, stage_ref, send_sems, recv_sems):
    me = lax.axis_index("lat") * n_lon + lax.axis_index("lon")

    def coords(d):
        return (lax.rem(d, n_lon), lax.div(d, n_lon))

    barrier = pltpu.get_barrier_semaphore()

    @pl.loop(1, n)
    def _(j):
        pl.semaphore_signal(barrier, inc=1, device_id=coords(lax.rem(me + j, n)), device_id_type=MESH)

    pl.semaphore_wait(barrier, n - 1)

    def send_copy(j):
        peer = lax.rem(me + j, n)
        return pltpu.make_async_remote_copy(
            src_ref=out_ref.at[peer],
            dst_ref=recv_ref.at[j],
            send_sem=send_sems.at[j],
            recv_sem=recv_sems.at[j],
            device_id=coords(peer),
            device_id_type=MESH,
        )

    def recv_copy(j):
        source = lax.rem(me - j + n, n)
        return pltpu.make_async_remote_copy(
            src_ref=out_ref.at[source],
            dst_ref=recv_ref.at[j],
            send_sem=send_sems.at[j],
            recv_sem=recv_sems.at[j],
            device_id=coords(source),
            device_id_type=MESH,
        )

    @pl.loop(1, n)
    def _(j):
        send_copy(j).start()

    recv_ref[0] = out_ref[me]
    slots, cells, channels = out_ref.shape[1], out_ref.shape[2], out_ref.shape[3]
    rows = group * slots * cells

    @pl.loop(0, n // group)
    def _(g):
        base = g * group

        @pl.loop(0, group)
        def _(i):
            j = base + i

            @pl.when(j > 0)
            def _():
                recv_copy(j).wait_recv()

            stage_ref[i] = state_ref[lax.rem(me - j + n, n)]

        fluxes = recv_ref[pl.ds(base, group)]
        used = fluxes[:, :, 0:1, 0:1] == fluxes[:, :, 0:1, 0:1]
        states = (stage_ref[...].astype(jnp.float32) + fluxes.astype(jnp.float32)).reshape(rows, channels)
        average = jnp.mean(states, axis=-1, keepdims=True)
        centred = states - average
        spread = jnp.mean(centred * centred, axis=-1, keepdims=True)
        normed = (centred * lax.rsqrt(spread + 1e-06) * gain_ref[...]).astype(jnp.bfloat16)
        hidden = jax.nn.gelu(
            jnp.dot(normed, up_ref[...], preferred_element_type=jnp.float32), approximate=True
        ).astype(jnp.bfloat16)
        result = states + jnp.dot(hidden, down_ref[...], preferred_element_type=jnp.float32)
        result = result.reshape(group, slots, cells, channels)
        stage_ref[...] = jnp.where(used, result, 0.0).astype(jnp.bfloat16)

        @pl.loop(0, group)
        def _(i):
            res_ref[lax.rem(me - base - i + n, n)] = stage_ref[i]

    @pl.loop(1, n)
    def _(j):
        send_copy(j).wait_send()


def exchange_and_ocean(outgoing, state, gain, w_up, w_down):
    n_lon = lax.axis_size("lon")
    n = n_lon * lax.axis_size("lat")
    group = 16
    rows = outgoing.shape[0] * outgoing.shape[1] * outgoing.shape[2]
    channels, hid = w_up.shape
    vmem = pl.BlockSpec(memory_space=pltpu.VMEM)
    return pl.pallas_call(
        functools.partial(exchange_body, n_lon, n, group),
        out_shape=jax.ShapeDtypeStruct(outgoing.shape, outgoing.dtype),
        in_specs=[vmem] * 5,
        out_specs=vmem,
        scratch_shapes=[
            pltpu.VMEM(outgoing.shape, outgoing.dtype),
            pltpu.VMEM((group,) + outgoing.shape[1:], outgoing.dtype),
            pltpu.SemaphoreType.DMA((n,)),
            pltpu.SemaphoreType.DMA((n,)),
        ],
        compiler_params=pltpu.CompilerParams(
            collective_id=0, has_side_effects=True, vmem_limit_bytes=48 * 1024 * 1024
        ),
        cost_estimate=pl.CostEstimate(
            flops=4 * rows * channels * hid, transcendentals=rows * hid, bytes_accessed=4 * rows * channels * 2
        ),
    )(outgoing, state, gain.reshape(1, channels), w_up, w_down)


def atmos_body(kw, band, pad_ref, w_ref, atm_ref, gain_ref, up_hbm, down_hbm, fw_hbm, wet_ref, tile_ref, used_ref,
               out_ref, slots_ref, flux_ref, xf_ref, xs_ref, mixed_ref, up_ref, down_ref, fw_ref, sems):
    rows, cols, channels = atm_ref.shape
    weights = [
        pltpu.make_async_copy(up_hbm, up_ref, sems.at[0]),
        pltpu.make_async_copy(down_hbm, down_ref, sems.at[1]),
        pltpu.make_async_copy(fw_hbm, fw_ref, sems.at[2]),
    ]
    for copy in weights:
        copy.start()
    xf_ref[:, : pad_ref.shape[1], :] = pad_ref[...].astype(jnp.float32)

    @pl.loop(0, pad_ref.shape[0])
    def _(i):
        for q in range(kw):
            xs_ref[q, i] = xf_ref[i, pl.ds(q, cols), :]

    @pl.loop(0, rows // band)
    def _(b):
        r0 = b * band
        for cb in range(channels // 128):
            lanes = pl.ds(cb * 128, 128)
            acc = [jnp.zeros((cols, 128), jnp.float32) for _ in range(band)]
            for q in range(kw):
                for i in range(band + kw - 1):
                    line = xs_ref[q, r0 + i, :, lanes]
                    for p in range(kw):
                        r = i - p
                        if 0 <= r < band:
                            acc[r] = acc[r] + line * w_ref[p, pl.ds(q, 1), lanes]
            for r in range(band):
                mixed_ref[r0 + r, :, lanes] = acc[r]

    for copy in weights:
        copy.wait()

    chunk = 8

    @pl.loop(0, rows // chunk)
    def _(k):
        cells = chunk * cols
        mixed = mixed_ref[pl.ds(k * chunk, chunk)].reshape(cells, channels)
        average = jnp.mean(mixed, axis=-1, keepdims=True)
        centred = mixed - average
        spread = jnp.mean(centred * centred, axis=-1, keepdims=True)
        normed = (centred * lax.rsqrt(spread + 1e-06) * gain_ref[...]).astype(jnp.bfloat16)
        hidden = jax.nn.gelu(
            jnp.dot(normed, up_ref[...], preferred_element_type=jnp.float32), approximate=True
        ).astype(jnp.bfloat16)
        branch = jnp.dot(hidden, down_ref[...], preferred_element_type=jnp.float32)
        atmos = atm_ref[pl.ds(k * chunk, chunk)].reshape(cells, channels).astype(jnp.float32)
        new = (atmos + branch).astype(jnp.bfloat16)
        out_ref[pl.ds(k * chunk, chunk)] = new.reshape(chunk, cols, channels)
        flux = jnp.dot(new, fw_ref[...], preferred_element_type=jnp.float32) * wet_ref[pl.ds(k * cells, cells)]
        flux_ref[pl.ds(k * cells, cells)] = flux.astype(jnp.bfloat16)

    capacity, tile_cells = slots_ref.shape[1], slots_ref.shape[2]

    @pl.loop(0, slots_ref.shape[0] * capacity)
    def _(t):
        start = pl.multiple_of(tile_ref[t] * tile_cells, tile_cells)
        cells_of_tile = flux_ref[pl.ds(start, tile_cells)]
        keep = jnp.full(cells_of_tile.shape, used_ref[t], jnp.int32) > 0
        slots_ref[t // capacity, t % capacity] = jnp.where(keep, cells_of_tile, jnp.nan).astype(jnp.bfloat16)


def atmosphere_block(padded, conv_weight, atmosphere, gain, w_up, w_down, flux_weight, wet, tile_of_slot, used,
                     slot_shape):
    rows, cols, channels = atmosphere.shape
    kw = conv_weight.shape[0]
    hid = w_up.shape[1]
    vmem = pl.BlockSpec(memory_space=pltpu.VMEM)
    hbm = pl.BlockSpec(memory_space=pl.ANY)
    cells = rows * cols
    return pl.pallas_call(
        functools.partial(atmos_body, kw, 4),
        out_shape=(
            jax.ShapeDtypeStruct(atmosphere.shape, atmosphere.dtype),
            jax.ShapeDtypeStruct(slot_shape, jnp.bfloat16),
        ),
        in_specs=[vmem] * 4 + [hbm] * 3 + [vmem] + [pl.BlockSpec(memory_space=pltpu.SMEM)] * 2,
        out_specs=(vmem, vmem),
        scratch_shapes=[
            pltpu.VMEM((cells, channels), jnp.bfloat16),
            pltpu.VMEM((padded.shape[0], -(-padded.shape[1] // 8) * 8, channels), jnp.float32),
            pltpu.VMEM((kw, padded.shape[0], cols, channels), jnp.float32),
            pltpu.VMEM((rows, cols, channels), jnp.float32),
            pltpu.VMEM(w_up.shape, w_up.dtype),
            pltpu.VMEM(w_down.shape, w_down.dtype),
            pltpu.VMEM(flux_weight.shape, flux_weight.dtype),
            pltpu.SemaphoreType.DMA((3,)),
        ],
        compiler_params=pltpu.CompilerParams(vmem_limit_bytes=56 * 1024 * 1024),
        cost_estimate=pl.CostEstimate(
            flops=2 * cells * channels * (kw * kw + 2 * hid + channels),
            transcendentals=cells * hid,
            bytes_accessed=cells * channels * 8,
        ),
    )(padded, conv_weight, atmosphere, gain.reshape(1, channels), w_up, w_down, flux_weight, wet, tile_of_slot, used)


def normalize(values, scales):
    average = jnp.mean(values, axis=-1, keepdims=True)
    centred = values - average
    spread = jnp.mean(centred * centred, axis=-1, keepdims=True)
    return centred * lax.rsqrt(spread + 1e-06) * scales


def channel_mixer(values, scales, w_up, w_down):
    normed = normalize(values, scales).astype(jnp.bfloat16)
    hidden = jax.nn.gelu(
        jnp.dot(normed, w_up, preferred_element_type=jnp.float32), approximate=True
    ).astype(jnp.bfloat16)
    return jnp.dot(hidden, w_down, preferred_element_type=jnp.float32)


def per_device(
    atmosphere,
    conv_weight,
    atm_gain,
    atm_up,
    atm_down,
    flux_weight,
    land_mask,
    tile_owner,
    ocean_state,
    ocn_gain,
    ocn_up,
    ocn_down,
):
    lat_rows, lon_cols, channels = atmosphere.shape
    margin = conv_weight.shape[0] // 2
    padded = halo_pad(atmosphere, margin)
    owners = tile_owner.reshape(-1)
    tile_count = owners.shape[0]
    peer_count, capacity, tile_cells = ocean_state.shape[1], ocean_state.shape[2], ocean_state.shape[3]
    order = jnp.arange(tile_count, dtype=jnp.int32)
    earlier_same = (owners[:, None] == owners[None, :]) & (order[None, :] < order[:, None])
    tile_rank = jnp.sum(earlier_same.astype(jnp.int32), axis=1)
    slot_index = owners * capacity + tile_rank
    hits = jnp.arange(peer_count * capacity, dtype=jnp.int32)[:, None] == slot_index[None, :]
    used = jnp.sum(hits.astype(jnp.int32), axis=1)
    tile_of_slot = jnp.sum(jnp.where(hits, order[None, :], 0), axis=1)
    wet_cells = land_mask.reshape(lat_rows * lon_cols, 1).astype(jnp.float32)
    atmos_new, outgoing = atmosphere_block(
        padded, conv_weight, atmosphere, atm_gain, atm_up, atm_down, flux_weight, wet_cells,
        tile_of_slot, used, (peer_count, capacity, tile_cells, channels),
    )
    ocean_out = exchange_and_ocean(outgoing, ocean_state[0], ocn_gain, ocn_up, ocn_down)[None]
    return (atmos_new, ocean_out)


def solution(mesh):
    placed = (
        P("lat", "lon", None),
        P(),
        P(),
        P(),
        P(),
        P(),
        P("lat", "lon"),
        P("lat", "lon", None),
        P(("lat", "lon"), None, None, None, None),
        P(),
        P(),
        P(),
    )
    return jax.shard_map(
        per_device,
        mesh=mesh,
        in_specs=placed,
        out_specs=(P("lat", "lon", None), P(("lat", "lon"), None, None, None, None)),
        check_vma=False,
    )
```

```python
import functools

import jax
import jax.numpy as jnp
from jax import lax
from jax.experimental import pallas as pl
from jax.experimental.pallas import tpu as pltpu
from jax.sharding import PartitionSpec as P

MESH = pl.DeviceIdType.MESH

AXES = ("lat", "lon")


HALO_MOVES = ((1, 0), (-1, 0), (0, 1), (0, -1), (1, 1), (1, -1), (-1, 1), (-1, -1))


def halo_body(n_lat, n_lon, w, side, x_ref, *refs):
    got, send_sems, recv_sems = refs[:8], refs[8], refs[9]
    rows, cols = x_ref.shape[0], x_ref.shape[1]
    lat, lon = lax.axis_index("lat"), lax.axis_index("lon")
    has_up = lat > 0
    has_down = lat < n_lat - 1
    row_part = {1: pl.ds(rows - w, w), -1: pl.ds(0, w), 0: pl.ds(0, rows)}
    col_part = {1: pl.ds(cols - side, side), -1: pl.ds(0, side), 0: pl.ds(0, cols)}

    def exists(d_lat):
        return has_down if d_lat > 0 else (has_up if d_lat < 0 else lat >= 0)

    def exists_from(d_lat):
        return has_up if d_lat > 0 else (has_down if d_lat < 0 else lat >= 0)

    def target(d_lat, d_lon):
        return (lax.rem(lon + d_lon + n_lon, n_lon), lat + d_lat)

    barrier = pltpu.get_barrier_semaphore()
    for d_lat, d_lon in HALO_MOVES:
        @pl.when(exists(d_lat))
        def _():
            pl.semaphore_signal(barrier, inc=1, device_id=target(d_lat, d_lon), device_id_type=MESH)

    pl.semaphore_wait(barrier, 2 + 3 * has_up.astype(jnp.int32) + 3 * has_down.astype(jnp.int32))

    def copy(p):
        d_lat, d_lon = HALO_MOVES[p]
        return pltpu.make_async_remote_copy(
            src_ref=x_ref.at[row_part[d_lat], col_part[d_lon]],
            dst_ref=got[p],
            send_sem=send_sems.at[p],
            recv_sem=recv_sems.at[p],
            device_id=target(d_lat, d_lon),
            device_id_type=MESH,
        )

    for p, (d_lat, d_lon) in enumerate(HALO_MOVES):
        @pl.when(exists(d_lat))
        def _():
            copy(p).start()

    for p, (d_lat, d_lon) in enumerate(HALO_MOVES):
        @pl.when(exists_from(d_lat))
        def _():
            copy(p).wait_recv()

        @pl.when(jnp.logical_not(exists_from(d_lat)))
        def _():
            got[p][...] = jnp.zeros(got[p].shape, got[p].dtype)

    for p, (d_lat, d_lon) in enumerate(HALO_MOVES):
        @pl.when(exists(d_lat))
        def _():
            copy(p).wait_send()


def halo_pad(x, w):
    rows, cols, channels = x.shape
    side = 8
    shapes = []
    for d_lat, d_lon in HALO_MOVES:
        shapes.append((w if d_lat else rows, side if d_lon else cols, channels))
    vmem = pl.BlockSpec(memory_space=pltpu.VMEM)
    got = pl.pallas_call(
        functools.partial(halo_body, lax.axis_size("lat"), lax.axis_size("lon"), w, side),
        out_shape=tuple(jax.ShapeDtypeStruct(sh, x.dtype) for sh in shapes),
        in_specs=[pl.BlockSpec(memory_space=pl.ANY)],
        out_specs=tuple([vmem] * 8),
        scratch_shapes=[pltpu.SemaphoreType.DMA((8,)), pltpu.SemaphoreType.DMA((8,))],
        compiler_params=pltpu.CompilerParams(collective_id=1, has_side_effects=True),
    )(x)
    above, below, left, right, above_left, above_right, below_left, below_right = got
    left, above_left, below_left = (a[:, side - w:] for a in (left, above_left, below_left))
    right, above_right, below_right = (a[:, :w] for a in (right, above_right, below_right))
    top = jnp.concatenate([above_left, above, above_right], axis=1)
    mid = jnp.concatenate([left, x, right], axis=1)
    bottom = jnp.concatenate([below_left, below, below_right], axis=1)
    return jnp.concatenate([top, mid, bottom], axis=0)


def exchange_body(n_lon, n, group, out_ref, state_ref, gain_ref, up_ref, down_ref,
                  res_ref, recv_ref, stage_ref, send_sems, recv_sems):
    me = lax.axis_index("lat") * n_lon + lax.axis_index("lon")

    def coords(d):
        return (lax.rem(d, n_lon), lax.div(d, n_lon))

    barrier = pltpu.get_barrier_semaphore()

    @pl.loop(1, n)
    def _(j):
        pl.semaphore_signal(barrier, inc=1, device_id=coords(lax.rem(me + j, n)), device_id_type=MESH)

    pl.semaphore_wait(barrier, n - 1)

    def send_copy(j):
        peer = lax.rem(me + j, n)
        return pltpu.make_async_remote_copy(
            src_ref=out_ref.at[peer],
            dst_ref=recv_ref.at[j],
            send_sem=send_sems.at[j],
            recv_sem=recv_sems.at[j],
            device_id=coords(peer),
            device_id_type=MESH,
        )

    def recv_copy(j):
        source = lax.rem(me - j + n, n)
        return pltpu.make_async_remote_copy(
            src_ref=out_ref.at[source],
            dst_ref=recv_ref.at[j],
            send_sem=send_sems.at[j],
            recv_sem=recv_sems.at[j],
            device_id=coords(source),
            device_id_type=MESH,
        )

    @pl.loop(1, n)
    def _(j):
        send_copy(j).start()

    recv_ref[0] = out_ref[me]
    slots, cells, channels = out_ref.shape[1], out_ref.shape[2], out_ref.shape[3]
    rows = group * slots * cells

    @pl.loop(0, n // group)
    def _(g):
        base = g * group

        @pl.loop(0, group)
        def _(i):
            j = base + i

            @pl.when(j > 0)
            def _():
                recv_copy(j).wait_recv()

            stage_ref[i] = state_ref[lax.rem(me - j + n, n)]

        fluxes = recv_ref[pl.ds(base, group)]
        used = fluxes[:, :, 0:1, 0:1] == fluxes[:, :, 0:1, 0:1]
        states = (stage_ref[...].astype(jnp.float32) + fluxes.astype(jnp.float32)).reshape(rows, channels)
        average = jnp.mean(states, axis=-1, keepdims=True)
        centred = states - average
        spread = jnp.mean(centred * centred, axis=-1, keepdims=True)
        normed = (centred * lax.rsqrt(spread + 1e-06) * gain_ref[...]).astype(jnp.bfloat16)
        hidden = jax.nn.gelu(
            jnp.dot(normed, up_ref[...], preferred_element_type=jnp.float32), approximate=True
        ).astype(jnp.bfloat16)
        result = states + jnp.dot(hidden, down_ref[...], preferred_element_type=jnp.float32)
        result = result.reshape(group, slots, cells, channels)
        stage_ref[...] = jnp.where(used, result, 0.0).astype(jnp.bfloat16)

        @pl.loop(0, group)
        def _(i):
            res_ref[lax.rem(me - base - i + n, n)] = stage_ref[i]

    @pl.loop(1, n)
    def _(j):
        send_copy(j).wait_send()


def exchange_and_ocean(outgoing, state, gain, w_up, w_down):
    n_lon = lax.axis_size("lon")
    n = n_lon * lax.axis_size("lat")
    group = 16
    rows = outgoing.shape[0] * outgoing.shape[1] * outgoing.shape[2]
    channels, hid = w_up.shape
    vmem = pl.BlockSpec(memory_space=pltpu.VMEM)
    return pl.pallas_call(
        functools.partial(exchange_body, n_lon, n, group),
        out_shape=jax.ShapeDtypeStruct(outgoing.shape, outgoing.dtype),
        in_specs=[vmem] * 5,
        out_specs=vmem,
        scratch_shapes=[
            pltpu.VMEM(outgoing.shape, outgoing.dtype),
            pltpu.VMEM((group,) + outgoing.shape[1:], outgoing.dtype),
            pltpu.SemaphoreType.DMA((n,)),
            pltpu.SemaphoreType.DMA((n,)),
        ],
        compiler_params=pltpu.CompilerParams(
            collective_id=0, has_side_effects=True, vmem_limit_bytes=48 * 1024 * 1024
        ),
        cost_estimate=pl.CostEstimate(
            flops=4 * rows * channels * hid, transcendentals=rows * hid, bytes_accessed=4 * rows * channels * 2
        ),
    )(outgoing, state, gain.reshape(1, channels), w_up, w_down)


def atmos_body(kw, band, pad_ref, w_ref, atm_ref, gain_ref, up_hbm, down_hbm, fw_hbm,
               out_ref, flux_ref, xf_ref, xs_ref, mixed_ref, up_ref, down_ref, fw_ref, sems):
    rows, cols, channels = atm_ref.shape
    weights = [
        pltpu.make_async_copy(up_hbm, up_ref, sems.at[0]),
        pltpu.make_async_copy(down_hbm, down_ref, sems.at[1]),
        pltpu.make_async_copy(fw_hbm, fw_ref, sems.at[2]),
    ]
    for copy in weights:
        copy.start()
    xf_ref[:, : pad_ref.shape[1], :] = pad_ref[...].astype(jnp.float32)

    @pl.loop(0, pad_ref.shape[0])
    def _(i):
        for q in range(kw):
            xs_ref[q, i] = xf_ref[i, pl.ds(q, cols), :]

    @pl.loop(0, rows // band)
    def _(b):
        r0 = b * band
        for cb in range(channels // 128):
            lanes = pl.ds(cb * 128, 128)
            acc = [jnp.zeros((cols, 128), jnp.float32) for _ in range(band)]
            for q in range(kw):
                for i in range(band + kw - 1):
                    line = xs_ref[q, r0 + i, :, lanes]
                    for p in range(kw):
                        r = i - p
                        if 0 <= r < band:
                            acc[r] = acc[r] + line * w_ref[p, pl.ds(q, 1), lanes]
            for r in range(band):
                mixed_ref[r0 + r, :, lanes] = acc[r]

    for copy in weights:
        copy.wait()

    chunk = 8

    @pl.loop(0, rows // chunk)
    def _(k):
        cells = chunk * cols
        mixed = mixed_ref[pl.ds(k * chunk, chunk)].reshape(cells, channels)
        average = jnp.mean(mixed, axis=-1, keepdims=True)
        centred = mixed - average
        spread = jnp.mean(centred * centred, axis=-1, keepdims=True)
        normed = (centred * lax.rsqrt(spread + 1e-06) * gain_ref[...]).astype(jnp.bfloat16)
        hidden = jax.nn.gelu(
            jnp.dot(normed, up_ref[...], preferred_element_type=jnp.float32), approximate=True
        ).astype(jnp.bfloat16)
        branch = jnp.dot(hidden, down_ref[...], preferred_element_type=jnp.float32)
        atmos = atm_ref[pl.ds(k * chunk, chunk)].reshape(cells, channels).astype(jnp.float32)
        new = (atmos + branch).astype(jnp.bfloat16)
        out_ref[pl.ds(k * chunk, chunk)] = new.reshape(chunk, cols, channels)
        flux = jnp.dot(new, fw_ref[...], preferred_element_type=jnp.float32)
        flux_ref[pl.ds(k * cells, cells)] = flux.astype(jnp.bfloat16)


def atmosphere_block(padded, conv_weight, atmosphere, gain, w_up, w_down, flux_weight):
    rows, cols, channels = atmosphere.shape
    kw = conv_weight.shape[0]
    hid = w_up.shape[1]
    vmem = pl.BlockSpec(memory_space=pltpu.VMEM)
    hbm = pl.BlockSpec(memory_space=pl.ANY)
    cells = rows * cols
    return pl.pallas_call(
        functools.partial(atmos_body, kw, 4),
        out_shape=(
            jax.ShapeDtypeStruct(atmosphere.shape, atmosphere.dtype),
            jax.ShapeDtypeStruct((cells, channels), jnp.bfloat16),
        ),
        in_specs=[vmem] * 4 + [hbm] * 3,
        out_specs=(vmem, vmem),
        scratch_shapes=[
            pltpu.VMEM((padded.shape[0], -(-padded.shape[1] // 8) * 8, channels), jnp.float32),
            pltpu.VMEM((kw, padded.shape[0], cols, channels), jnp.float32),
            pltpu.VMEM((rows, cols, channels), jnp.float32),
            pltpu.VMEM(w_up.shape, w_up.dtype),
            pltpu.VMEM(w_down.shape, w_down.dtype),
            pltpu.VMEM(flux_weight.shape, flux_weight.dtype),
            pltpu.SemaphoreType.DMA((3,)),
        ],
        compiler_params=pltpu.CompilerParams(vmem_limit_bytes=56 * 1024 * 1024),
        cost_estimate=pl.CostEstimate(
            flops=2 * cells * channels * (kw * kw + 2 * hid + channels),
            transcendentals=cells * hid,
            bytes_accessed=cells * channels * 8,
        ),
    )(padded, conv_weight, atmosphere, gain.reshape(1, channels), w_up, w_down, flux_weight)


def normalize(values, scales):
    average = jnp.mean(values, axis=-1, keepdims=True)
    centred = values - average
    spread = jnp.mean(centred * centred, axis=-1, keepdims=True)
    return centred * lax.rsqrt(spread + 1e-06) * scales


def channel_mixer(values, scales, w_up, w_down):
    normed = normalize(values, scales).astype(jnp.bfloat16)
    hidden = jax.nn.gelu(
        jnp.dot(normed, w_up, preferred_element_type=jnp.float32), approximate=True
    ).astype(jnp.bfloat16)
    return jnp.dot(hidden, w_down, preferred_element_type=jnp.float32)


def per_device(
    atmosphere,
    conv_weight,
    atm_gain,
    atm_up,
    atm_down,
    flux_weight,
    land_mask,
    tile_owner,
    ocean_state,
    ocn_gain,
    ocn_up,
    ocn_down,
):
    lat_rows, lon_cols, channels = atmosphere.shape
    margin = conv_weight.shape[0] // 2
    owners = tile_owner.reshape(-1)
    tile_count = owners.shape[0]
    peer_count = ocean_state.shape[1]
    capacity = ocean_state.shape[2]
    tile_cells = ocean_state.shape[3]
    padded = halo_pad(atmosphere, margin)
    atmos_new, fluxes = atmosphere_block(padded, conv_weight, atmosphere, atm_gain, atm_up, atm_down, flux_weight)
    wet = land_mask.reshape(tile_count, tile_cells, 1).astype(jnp.bfloat16)
    flux_tiles = (fluxes.reshape(tile_count, tile_cells, channels) * wet).reshape(tile_count, tile_cells * channels)
    member = (owners[:, None] == jnp.arange(peer_count, dtype=jnp.int32)[None, :]).astype(jnp.int32)
    tile_rank = jnp.sum(jnp.cumsum(member, axis=0) * member, axis=1) - 1
    slot_index = owners * capacity + tile_rank
    onehot = (
        jnp.arange(peer_count * capacity, dtype=jnp.int32)[:, None] == slot_index[None, :]
    ).astype(jnp.bfloat16)
    outgoing = jnp.dot(onehot, flux_tiles, preferred_element_type=jnp.float32).astype(jnp.bfloat16)
    used = jnp.sum(onehot.astype(jnp.float32), axis=1) > 0
    outgoing = jnp.where(used[:, None], outgoing, jnp.nan).astype(jnp.bfloat16)
    outgoing = outgoing.reshape(peer_count, capacity, tile_cells, channels)
    ocean_out = exchange_and_ocean(outgoing, ocean_state[0], ocn_gain, ocn_up, ocn_down)[None]
    return (atmos_new, ocean_out)


def solution(mesh):
    placed = (
        P("lat", "lon", None),
        P(),
        P(),
        P(),
        P(),
        P(),
        P("lat", "lon"),
        P("lat", "lon", None),
        P(("lat", "lon"), None, None, None, None),
        P(),
        P(),
        P(),
    )
    return jax.shard_map(
        per_device,
        mesh=mesh,
        in_specs=placed,
        out_specs=(P("lat", "lon", None), P(("lat", "lon"), None, None, None, None)),
        check_vma=False,
    )
```

```python
import functools

import jax
import jax.numpy as jnp
from jax import lax
from jax.experimental import pallas as pl
from jax.experimental.pallas import tpu as pltpu
from jax.sharding import PartitionSpec as P

MESH = pl.DeviceIdType.MESH

AXES = ("lat", "lon")


HALO_MOVES = ((1, 0), (-1, 0), (0, 1), (0, -1), (1, 1), (1, -1), (-1, 1), (-1, -1))


def halo_body(n_lat, n_lon, w, side, x_ref, *refs):
    got, send_sems, recv_sems = refs[:8], refs[8], refs[9]
    rows, cols = x_ref.shape[0], x_ref.shape[1]
    lat, lon = lax.axis_index("lat"), lax.axis_index("lon")
    has_up = lat > 0
    has_down = lat < n_lat - 1
    row_part = {1: pl.ds(rows - w, w), -1: pl.ds(0, w), 0: pl.ds(0, rows)}
    col_part = {1: pl.ds(cols - side, side), -1: pl.ds(0, side), 0: pl.ds(0, cols)}

    def exists(d_lat):
        return has_down if d_lat > 0 else (has_up if d_lat < 0 else lat >= 0)

    def exists_from(d_lat):
        return has_up if d_lat > 0 else (has_down if d_lat < 0 else lat >= 0)

    def target(d_lat, d_lon):
        return (lax.rem(lon + d_lon + n_lon, n_lon), lat + d_lat)

    barrier = pltpu.get_barrier_semaphore()
    for d_lat, d_lon in HALO_MOVES:
        @pl.when(exists(d_lat))
        def _():
            pl.semaphore_signal(barrier, inc=1, device_id=target(d_lat, d_lon), device_id_type=MESH)

    pl.semaphore_wait(barrier, 2 + 3 * has_up.astype(jnp.int32) + 3 * has_down.astype(jnp.int32))

    def copy(p):
        d_lat, d_lon = HALO_MOVES[p]
        return pltpu.make_async_remote_copy(
            src_ref=x_ref.at[row_part[d_lat], col_part[d_lon]],
            dst_ref=got[p],
            send_sem=send_sems.at[p],
            recv_sem=recv_sems.at[p],
            device_id=target(d_lat, d_lon),
            device_id_type=MESH,
        )

    for p, (d_lat, d_lon) in enumerate(HALO_MOVES):
        @pl.when(exists(d_lat))
        def _():
            copy(p).start()

    for p, (d_lat, d_lon) in enumerate(HALO_MOVES):
        @pl.when(exists_from(d_lat))
        def _():
            copy(p).wait_recv()

        @pl.when(jnp.logical_not(exists_from(d_lat)))
        def _():
            got[p][...] = jnp.zeros(got[p].shape, got[p].dtype)

    for p, (d_lat, d_lon) in enumerate(HALO_MOVES):
        @pl.when(exists(d_lat))
        def _():
            copy(p).wait_send()


def halo_pad(x, w):
    rows, cols, channels = x.shape
    side = 8
    shapes = []
    for d_lat, d_lon in HALO_MOVES:
        shapes.append((w if d_lat else rows, side if d_lon else cols, channels))
    vmem = pl.BlockSpec(memory_space=pltpu.VMEM)
    got = pl.pallas_call(
        functools.partial(halo_body, lax.axis_size("lat"), lax.axis_size("lon"), w, side),
        out_shape=tuple(jax.ShapeDtypeStruct(sh, x.dtype) for sh in shapes),
        in_specs=[pl.BlockSpec(memory_space=pl.ANY)],
        out_specs=tuple([vmem] * 8),
        scratch_shapes=[pltpu.SemaphoreType.DMA((8,)), pltpu.SemaphoreType.DMA((8,))],
        compiler_params=pltpu.CompilerParams(collective_id=1, has_side_effects=True),
    )(x)
    return got


def exchange_body(n_lon, n, group, out_ref, state_ref, gain_ref, up_ref, down_ref,
                  res_ref, recv_ref, stage_ref, send_sems, recv_sems):
    me = lax.axis_index("lat") * n_lon + lax.axis_index("lon")

    def coords(d):
        return (lax.rem(d, n_lon), lax.div(d, n_lon))

    barrier = pltpu.get_barrier_semaphore()

    @pl.loop(1, n)
    def _(j):
        pl.semaphore_signal(barrier, inc=1, device_id=coords(lax.rem(me + j, n)), device_id_type=MESH)

    pl.semaphore_wait(barrier, n - 1)

    def send_copy(j):
        peer = lax.rem(me + j, n)
        return pltpu.make_async_remote_copy(
            src_ref=out_ref.at[peer],
            dst_ref=recv_ref.at[j],
            send_sem=send_sems.at[j],
            recv_sem=recv_sems.at[j],
            device_id=coords(peer),
            device_id_type=MESH,
        )

    def recv_copy(j):
        source = lax.rem(me - j + n, n)
        return pltpu.make_async_remote_copy(
            src_ref=out_ref.at[source],
            dst_ref=recv_ref.at[j],
            send_sem=send_sems.at[j],
            recv_sem=recv_sems.at[j],
            device_id=coords(source),
            device_id_type=MESH,
        )

    @pl.loop(1, n)
    def _(j):
        send_copy(j).start()

    recv_ref[0] = out_ref[me]
    slots, cells, channels = out_ref.shape[1], out_ref.shape[2], out_ref.shape[3]
    rows = group * slots * cells

    @pl.loop(0, n // group)
    def _(g):
        base = g * group

        @pl.loop(0, group)
        def _(i):
            j = base + i

            @pl.when(j > 0)
            def _():
                recv_copy(j).wait_recv()

            stage_ref[i] = state_ref[lax.rem(me - j + n, n)]

        fluxes = recv_ref[pl.ds(base, group)]
        used = fluxes[:, :, 0:1, 0:1] == fluxes[:, :, 0:1, 0:1]
        states = (stage_ref[...].astype(jnp.float32) + fluxes.astype(jnp.float32)).reshape(rows, channels)
        average = jnp.mean(states, axis=-1, keepdims=True)
        centred = states - average
        spread = jnp.mean(centred * centred, axis=-1, keepdims=True)
        normed = (centred * lax.rsqrt(spread + 1e-06) * gain_ref[...]).astype(jnp.bfloat16)
        hidden = jax.nn.gelu(
            jnp.dot(normed, up_ref[...], preferred_element_type=jnp.float32), approximate=True
        ).astype(jnp.bfloat16)
        result = states + jnp.dot(hidden, down_ref[...], preferred_element_type=jnp.float32)
        result = result.reshape(group, slots, cells, channels)
        stage_ref[...] = jnp.where(used, result, 0.0).astype(jnp.bfloat16)

        @pl.loop(0, group)
        def _(i):
            res_ref[lax.rem(me - base - i + n, n)] = stage_ref[i]

    @pl.loop(1, n)
    def _(j):
        send_copy(j).wait_send()


def exchange_and_ocean(outgoing, state, gain, w_up, w_down):
    n_lon = lax.axis_size("lon")
    n = n_lon * lax.axis_size("lat")
    group = 16
    rows = outgoing.shape[0] * outgoing.shape[1] * outgoing.shape[2]
    channels, hid = w_up.shape
    vmem = pl.BlockSpec(memory_space=pltpu.VMEM)
    return pl.pallas_call(
        functools.partial(exchange_body, n_lon, n, group),
        out_shape=jax.ShapeDtypeStruct(outgoing.shape, outgoing.dtype),
        in_specs=[vmem] * 5,
        out_specs=vmem,
        scratch_shapes=[
            pltpu.VMEM(outgoing.shape, outgoing.dtype),
            pltpu.VMEM((group,) + outgoing.shape[1:], outgoing.dtype),
            pltpu.SemaphoreType.DMA((n,)),
            pltpu.SemaphoreType.DMA((n,)),
        ],
        compiler_params=pltpu.CompilerParams(
            collective_id=0, has_side_effects=True, vmem_limit_bytes=48 * 1024 * 1024
        ),
        cost_estimate=pl.CostEstimate(
            flops=4 * rows * channels * hid, transcendentals=rows * hid, bytes_accessed=4 * rows * channels * 2
        ),
    )(outgoing, state, gain.reshape(1, channels), w_up, w_down)


def atmos_body(kw, band, side, w_ref, atm_ref, gain_ref, up_hbm, down_hbm, fw_hbm,
               above, below, left, right, above_left, above_right, below_left, below_right,
               out_ref, flux_ref, xf_ref, xs_ref, mixed_ref, up_ref, down_ref, fw_ref, sems):
    rows, cols, channels = atm_ref.shape
    weights = [
        pltpu.make_async_copy(up_hbm, up_ref, sems.at[0]),
        pltpu.make_async_copy(down_hbm, down_ref, sems.at[1]),
        pltpu.make_async_copy(fw_hbm, fw_ref, sems.at[2]),
    ]
    for copy in weights:
        copy.start()
    m = kw // 2
    for r0, r1, l_ref, c_ref, r_ref in (
        (0, m, above_left, above, above_right),
        (m, m + rows, left, atm_ref, right),
        (m + rows, 2 * m + rows, below_left, below, below_right),
    ):
        xf_ref[r0:r1, 0:side, :] = l_ref[...].astype(jnp.float32)
        xf_ref[r0:r1, side:side + cols, :] = c_ref[...].astype(jnp.float32)
        xf_ref[r0:r1, side + cols:, :] = r_ref[...].astype(jnp.float32)

    @pl.loop(0, rows + 2 * m)
    def _(i):
        for q in range(kw):
            xs_ref[q, i] = xf_ref[i, pl.ds(side - m + q, cols), :]

    @pl.loop(0, rows // band)
    def _(b):
        r0 = b * band
        for cb in range(channels // 128):
            lanes = pl.ds(cb * 128, 128)
            acc = [jnp.zeros((cols, 128), jnp.float32) for _ in range(band)]
            for q in range(kw):
                for i in range(band + kw - 1):
                    line = xs_ref[q, r0 + i, :, lanes]
                    for p in range(kw):
                        r = i - p
                        if 0 <= r < band:
                            acc[r] = acc[r] + line * w_ref[p, pl.ds(q, 1), lanes]
            for r in range(band):
                mixed_ref[r0 + r, :, lanes] = acc[r]

    for copy in weights:
        copy.wait()

    chunk = 8

    @pl.loop(0, rows // chunk)
    def _(k):
        cells = chunk * cols
        mixed = mixed_ref[pl.ds(k * chunk, chunk)].reshape(cells, channels)
        average = jnp.mean(mixed, axis=-1, keepdims=True)
        centred = mixed - average
        spread = jnp.mean(centred * centred, axis=-1, keepdims=True)
        normed = (centred * lax.rsqrt(spread + 1e-06) * gain_ref[...]).astype(jnp.bfloat16)
        hidden = jax.nn.gelu(
            jnp.dot(normed, up_ref[...], preferred_element_type=jnp.float32), approximate=True
        ).astype(jnp.bfloat16)
        branch = jnp.dot(hidden, down_ref[...], preferred_element_type=jnp.float32)
        atmos = atm_ref[pl.ds(k * chunk, chunk)].reshape(cells, channels).astype(jnp.float32)
        new = (atmos + branch).astype(jnp.bfloat16)
        out_ref[pl.ds(k * chunk, chunk)] = new.reshape(chunk, cols, channels)
        flux = jnp.dot(new, fw_ref[...], preferred_element_type=jnp.float32)
        flux_ref[pl.ds(k * cells, cells)] = flux.astype(jnp.bfloat16)


def atmosphere_block(pieces, conv_weight, atmosphere, gain, w_up, w_down, flux_weight):
    rows, cols, channels = atmosphere.shape
    kw = conv_weight.shape[0]
    hid = w_up.shape[1]
    vmem = pl.BlockSpec(memory_space=pltpu.VMEM)
    hbm = pl.BlockSpec(memory_space=pl.ANY)
    cells = rows * cols
    return pl.pallas_call(
        functools.partial(atmos_body, kw, 4, pieces[2].shape[1]),
        out_shape=(
            jax.ShapeDtypeStruct(atmosphere.shape, atmosphere.dtype),
            jax.ShapeDtypeStruct((cells, channels), jnp.bfloat16),
        ),
        in_specs=[vmem] * 3 + [hbm] * 3 + [vmem] * 8,
        out_specs=(vmem, vmem),
        scratch_shapes=[
            pltpu.VMEM((rows + kw - 1, cols + 2 * pieces[2].shape[1], channels), jnp.float32),
            pltpu.VMEM((kw, rows + kw - 1, cols, channels), jnp.float32),
            pltpu.VMEM((rows, cols, channels), jnp.float32),
            pltpu.VMEM(w_up.shape, w_up.dtype),
            pltpu.VMEM(w_down.shape, w_down.dtype),
            pltpu.VMEM(flux_weight.shape, flux_weight.dtype),
            pltpu.SemaphoreType.DMA((3,)),
        ],
        compiler_params=pltpu.CompilerParams(vmem_limit_bytes=56 * 1024 * 1024),
        cost_estimate=pl.CostEstimate(
            flops=2 * cells * channels * (kw * kw + 2 * hid + channels),
            transcendentals=cells * hid,
            bytes_accessed=cells * channels * 8,
        ),
    )(conv_weight, atmosphere, gain.reshape(1, channels), w_up, w_down, flux_weight, *pieces)


def normalize(values, scales):
    average = jnp.mean(values, axis=-1, keepdims=True)
    centred = values - average
    spread = jnp.mean(centred * centred, axis=-1, keepdims=True)
    return centred * lax.rsqrt(spread + 1e-06) * scales


def channel_mixer(values, scales, w_up, w_down):
    normed = normalize(values, scales).astype(jnp.bfloat16)
    hidden = jax.nn.gelu(
        jnp.dot(normed, w_up, preferred_element_type=jnp.float32), approximate=True
    ).astype(jnp.bfloat16)
    return jnp.dot(hidden, w_down, preferred_element_type=jnp.float32)


def per_device(
    atmosphere,
    conv_weight,
    atm_gain,
    atm_up,
    atm_down,
    flux_weight,
    land_mask,
    tile_owner,
    ocean_state,
    ocn_gain,
    ocn_up,
    ocn_down,
):
    lat_rows, lon_cols, channels = atmosphere.shape
    margin = conv_weight.shape[0] // 2
    owners = tile_owner.reshape(-1)
    tile_count = owners.shape[0]
    peer_count = ocean_state.shape[1]
    capacity = ocean_state.shape[2]
    tile_cells = ocean_state.shape[3]
    pieces = halo_pad(atmosphere, margin)
    atmos_new, fluxes = atmosphere_block(pieces, conv_weight, atmosphere, atm_gain, atm_up, atm_down, flux_weight)
    wet = land_mask.reshape(tile_count, tile_cells, 1).astype(jnp.bfloat16)
    flux_tiles = (fluxes.reshape(tile_count, tile_cells, channels) * wet).reshape(tile_count, tile_cells * channels)
    member = (owners[:, None] == jnp.arange(peer_count, dtype=jnp.int32)[None, :]).astype(jnp.int32)
    tile_rank = jnp.sum(jnp.cumsum(member, axis=0) * member, axis=1) - 1
    slot_index = owners * capacity + tile_rank
    onehot = (
        jnp.arange(peer_count * capacity, dtype=jnp.int32)[:, None] == slot_index[None, :]
    ).astype(jnp.bfloat16)
    outgoing = jnp.dot(onehot, flux_tiles, preferred_element_type=jnp.float32).astype(jnp.bfloat16)
    used = jnp.sum(onehot.astype(jnp.float32), axis=1) > 0
    outgoing = jnp.where(used[:, None], outgoing, jnp.nan).astype(jnp.bfloat16)
    outgoing = outgoing.reshape(peer_count, capacity, tile_cells, channels)
    ocean_out = exchange_and_ocean(outgoing, ocean_state[0], ocn_gain, ocn_up, ocn_down)[None]
    return (atmos_new, ocean_out)


def solution(mesh):
    placed = (
        P("lat", "lon", None),
        P(),
        P(),
        P(),
        P(),
        P(),
        P("lat", "lon"),
        P("lat", "lon", None),
        P(("lat", "lon"), None, None, None, None),
        P(),
        P(),
        P(),
    )
    return jax.shard_map(
        per_device,
        mesh=mesh,
        in_specs=placed,
        out_specs=(P("lat", "lon", None), P(("lat", "lon"), None, None, None, None)),
        check_vma=False,
    )
```

```python
import functools

import jax
import jax.numpy as jnp
from jax import lax
from jax.experimental import pallas as pl
from jax.experimental.pallas import tpu as pltpu
from jax.sharding import PartitionSpec as P

MESH = pl.DeviceIdType.MESH

AXES = ("lat", "lon")


HALO_MOVES = ((1, 0), (-1, 0), (0, 1), (0, -1), (1, 1), (1, -1), (-1, 1), (-1, -1))


def halo_body(n_lat, n_lon, w, side, x_ref, *refs):
    got, send_sems, recv_sems = refs[:8], refs[8], refs[9]
    rows, cols = x_ref.shape[0], x_ref.shape[1]
    lat, lon = lax.axis_index("lat"), lax.axis_index("lon")
    has_up = lat > 0
    has_down = lat < n_lat - 1
    row_part = {1: pl.ds(rows - w, w), -1: pl.ds(0, w), 0: pl.ds(0, rows)}
    col_part = {1: pl.ds(cols - side, side), -1: pl.ds(0, side), 0: pl.ds(0, cols)}

    def exists(d_lat):
        return has_down if d_lat > 0 else (has_up if d_lat < 0 else lat >= 0)

    def exists_from(d_lat):
        return has_up if d_lat > 0 else (has_down if d_lat < 0 else lat >= 0)

    def target(d_lat, d_lon):
        return (lax.rem(lon + d_lon + n_lon, n_lon), lat + d_lat)

    barrier = pltpu.get_barrier_semaphore()
    for d_lat, d_lon in HALO_MOVES:
        @pl.when(exists(d_lat))
        def _():
            pl.semaphore_signal(barrier, inc=1, device_id=target(d_lat, d_lon), device_id_type=MESH)

    pl.semaphore_wait(barrier, 2 + 3 * has_up.astype(jnp.int32) + 3 * has_down.astype(jnp.int32))

    def copy(p):
        d_lat, d_lon = HALO_MOVES[p]
        return pltpu.make_async_remote_copy(
            src_ref=x_ref.at[row_part[d_lat], col_part[d_lon]],
            dst_ref=got[p],
            send_sem=send_sems.at[p],
            recv_sem=recv_sems.at[p],
            device_id=target(d_lat, d_lon),
            device_id_type=MESH,
        )

    for p, (d_lat, d_lon) in enumerate(HALO_MOVES):
        @pl.when(exists(d_lat))
        def _():
            copy(p).start()

    for p, (d_lat, d_lon) in enumerate(HALO_MOVES):
        @pl.when(exists_from(d_lat))
        def _():
            copy(p).wait_recv()

        @pl.when(jnp.logical_not(exists_from(d_lat)))
        def _():
            got[p][...] = jnp.zeros(got[p].shape, got[p].dtype)

    for p, (d_lat, d_lon) in enumerate(HALO_MOVES):
        @pl.when(exists(d_lat))
        def _():
            copy(p).wait_send()


def halo_pad(x, w):
    rows, cols, channels = x.shape
    side = 8
    shapes = []
    for d_lat, d_lon in HALO_MOVES:
        shapes.append((w if d_lat else rows, side if d_lon else cols, channels))
    vmem = pl.BlockSpec(memory_space=pltpu.VMEM)
    got = pl.pallas_call(
        functools.partial(halo_body, lax.axis_size("lat"), lax.axis_size("lon"), w, side),
        out_shape=tuple(jax.ShapeDtypeStruct(sh, x.dtype) for sh in shapes),
        in_specs=[pl.BlockSpec(memory_space=pl.ANY)],
        out_specs=tuple([vmem] * 8),
        scratch_shapes=[pltpu.SemaphoreType.DMA((8,)), pltpu.SemaphoreType.DMA((8,))],
        compiler_params=pltpu.CompilerParams(collective_id=1, has_side_effects=True),
    )(x)
    return got


def partner(a, b, n):
    total = 0
    bit = 1
    while bit < n:
        total = total + lax.rem(lax.div(a, bit) + lax.div(b, bit), 2) * bit
        bit *= 2
    return total


def exchange_body(n_lon, n, group, out_ref, state_ref, gain_ref, up_ref, down_ref,
                  res_ref, recv_ref, stage_ref, send_sems, recv_sems):
    me = lax.axis_index("lat") * n_lon + lax.axis_index("lon")

    def coords(d):
        return (lax.rem(d, n_lon), lax.div(d, n_lon))

    barrier = pltpu.get_barrier_semaphore()

    @pl.loop(1, n)
    def _(j):
        pl.semaphore_signal(barrier, inc=1, device_id=coords(partner(me, j, n)), device_id_type=MESH)

    pl.semaphore_wait(barrier, n - 1)

    def send_copy(j):
        peer = partner(me, j, n)
        return pltpu.make_async_remote_copy(
            src_ref=out_ref.at[peer],
            dst_ref=recv_ref.at[j],
            send_sem=send_sems.at[j],
            recv_sem=recv_sems.at[j],
            device_id=coords(peer),
            device_id_type=MESH,
        )

    def recv_copy(j):
        source = partner(me, j, n)
        return pltpu.make_async_remote_copy(
            src_ref=out_ref.at[source],
            dst_ref=recv_ref.at[j],
            send_sem=send_sems.at[j],
            recv_sem=recv_sems.at[j],
            device_id=coords(source),
            device_id_type=MESH,
        )

    @pl.loop(1, n)
    def _(j):
        send_copy(j).start()

    recv_ref[0] = out_ref[me]
    slots, cells, channels = out_ref.shape[1], out_ref.shape[2], out_ref.shape[3]
    rows = group * slots * cells

    @pl.loop(0, n // group)
    def _(g):
        base = g * group

        @pl.loop(0, group)
        def _(i):
            j = base + i

            @pl.when(j > 0)
            def _():
                recv_copy(j).wait_recv()

            stage_ref[i] = state_ref[partner(me, j, n)]

        fluxes = recv_ref[pl.ds(base, group)]
        used = fluxes[:, :, 0:1, 0:1] == fluxes[:, :, 0:1, 0:1]
        states = (stage_ref[...].astype(jnp.float32) + fluxes.astype(jnp.float32)).reshape(rows, channels)
        average = jnp.mean(states, axis=-1, keepdims=True)
        centred = states - average
        spread = jnp.mean(centred * centred, axis=-1, keepdims=True)
        normed = (centred * lax.rsqrt(spread + 1e-06) * gain_ref[...]).astype(jnp.bfloat16)
        hidden = jax.nn.gelu(
            jnp.dot(normed, up_ref[...], preferred_element_type=jnp.float32), approximate=True
        ).astype(jnp.bfloat16)
        result = states + jnp.dot(hidden, down_ref[...], preferred_element_type=jnp.float32)
        result = result.reshape(group, slots, cells, channels)
        stage_ref[...] = jnp.where(used, result, 0.0).astype(jnp.bfloat16)

        @pl.loop(0, group)
        def _(i):
            res_ref[partner(me, base + i, n)] = stage_ref[i]

    @pl.loop(1, n)
    def _(j):
        send_copy(j).wait_send()


def exchange_and_ocean(outgoing, state, gain, w_up, w_down):
    n_lon = lax.axis_size("lon")
    n = n_lon * lax.axis_size("lat")
    assert n & (n - 1) == 0
    group = 16
    rows = outgoing.shape[0] * outgoing.shape[1] * outgoing.shape[2]
    channels, hid = w_up.shape
    vmem = pl.BlockSpec(memory_space=pltpu.VMEM)
    return pl.pallas_call(
        functools.partial(exchange_body, n_lon, n, group),
        out_shape=jax.ShapeDtypeStruct(outgoing.shape, outgoing.dtype),
        in_specs=[vmem] * 5,
        out_specs=vmem,
        scratch_shapes=[
            pltpu.VMEM(outgoing.shape, outgoing.dtype),
            pltpu.VMEM((group,) + outgoing.shape[1:], outgoing.dtype),
            pltpu.SemaphoreType.DMA((n,)),
            pltpu.SemaphoreType.DMA((n,)),
        ],
        compiler_params=pltpu.CompilerParams(
            collective_id=0, has_side_effects=True, vmem_limit_bytes=48 * 1024 * 1024
        ),
        cost_estimate=pl.CostEstimate(
            flops=4 * rows * channels * hid, transcendentals=rows * hid, bytes_accessed=4 * rows * channels * 2
        ),
    )(outgoing, state, gain.reshape(1, channels), w_up, w_down)


def atmos_body(kw, band, side, w_ref, atm_ref, gain_ref, up_hbm, down_hbm, fw_hbm,
               above, below, left, right, above_left, above_right, below_left, below_right,
               out_ref, flux_ref, xf_ref, xs_ref, mixed_ref, up_ref, down_ref, fw_ref, sems):
    rows, cols, channels = atm_ref.shape
    weights = [
        pltpu.make_async_copy(up_hbm, up_ref, sems.at[0]),
        pltpu.make_async_copy(down_hbm, down_ref, sems.at[1]),
        pltpu.make_async_copy(fw_hbm, fw_ref, sems.at[2]),
    ]
    for copy in weights:
        copy.start()
    m = kw // 2
    for r0, r1, l_ref, c_ref, r_ref in (
        (0, m, above_left, above, above_right),
        (m, m + rows, left, atm_ref, right),
        (m + rows, 2 * m + rows, below_left, below, below_right),
    ):
        xf_ref[r0:r1, 0:side, :] = l_ref[...].astype(jnp.float32)
        xf_ref[r0:r1, side:side + cols, :] = c_ref[...].astype(jnp.float32)
        xf_ref[r0:r1, side + cols:, :] = r_ref[...].astype(jnp.float32)

    @pl.loop(0, rows + 2 * m)
    def _(i):
        for q in range(kw):
            xs_ref[q, i] = xf_ref[i, pl.ds(side - m + q, cols), :]

    @pl.loop(0, rows // band)
    def _(b):
        r0 = b * band
        for cb in range(channels // 128):
            lanes = pl.ds(cb * 128, 128)
            acc = [jnp.zeros((cols, 128), jnp.float32) for _ in range(band)]
            for q in range(kw):
                for i in range(band + kw - 1):
                    line = xs_ref[q, r0 + i, :, lanes]
                    for p in range(kw):
                        r = i - p
                        if 0 <= r < band:
                            acc[r] = acc[r] + line * w_ref[p, pl.ds(q, 1), lanes]
            for r in range(band):
                mixed_ref[r0 + r, :, lanes] = acc[r]

    for copy in weights:
        copy.wait()

    chunk = 8

    @pl.loop(0, rows // chunk)
    def _(k):
        cells = chunk * cols
        mixed = mixed_ref[pl.ds(k * chunk, chunk)].reshape(cells, channels)
        average = jnp.mean(mixed, axis=-1, keepdims=True)
        centred = mixed - average
        spread = jnp.mean(centred * centred, axis=-1, keepdims=True)
        normed = (centred * lax.rsqrt(spread + 1e-06) * gain_ref[...]).astype(jnp.bfloat16)
        hidden = jax.nn.gelu(
            jnp.dot(normed, up_ref[...], preferred_element_type=jnp.float32), approximate=True
        ).astype(jnp.bfloat16)
        branch = jnp.dot(hidden, down_ref[...], preferred_element_type=jnp.float32)
        atmos = atm_ref[pl.ds(k * chunk, chunk)].reshape(cells, channels).astype(jnp.float32)
        new = (atmos + branch).astype(jnp.bfloat16)
        out_ref[pl.ds(k * chunk, chunk)] = new.reshape(chunk, cols, channels)
        flux = jnp.dot(new, fw_ref[...], preferred_element_type=jnp.float32)
        flux_ref[pl.ds(k * cells, cells)] = flux.astype(jnp.bfloat16)


def atmosphere_block(pieces, conv_weight, atmosphere, gain, w_up, w_down, flux_weight):
    rows, cols, channels = atmosphere.shape
    kw = conv_weight.shape[0]
    hid = w_up.shape[1]
    vmem = pl.BlockSpec(memory_space=pltpu.VMEM)
    hbm = pl.BlockSpec(memory_space=pl.ANY)
    cells = rows * cols
    return pl.pallas_call(
        functools.partial(atmos_body, kw, 4, pieces[2].shape[1]),
        out_shape=(
            jax.ShapeDtypeStruct(atmosphere.shape, atmosphere.dtype),
            jax.ShapeDtypeStruct((cells, channels), jnp.bfloat16),
        ),
        in_specs=[vmem] * 3 + [hbm] * 3 + [vmem] * 8,
        out_specs=(vmem, vmem),
        scratch_shapes=[
            pltpu.VMEM((rows + kw - 1, cols + 2 * pieces[2].shape[1], channels), jnp.float32),
            pltpu.VMEM((kw, rows + kw - 1, cols, channels), jnp.float32),
            pltpu.VMEM((rows, cols, channels), jnp.float32),
            pltpu.VMEM(w_up.shape, w_up.dtype),
            pltpu.VMEM(w_down.shape, w_down.dtype),
            pltpu.VMEM(flux_weight.shape, flux_weight.dtype),
            pltpu.SemaphoreType.DMA((3,)),
        ],
        compiler_params=pltpu.CompilerParams(vmem_limit_bytes=56 * 1024 * 1024),
        cost_estimate=pl.CostEstimate(
            flops=2 * cells * channels * (kw * kw + 2 * hid + channels),
            transcendentals=cells * hid,
            bytes_accessed=cells * channels * 8,
        ),
    )(conv_weight, atmosphere, gain.reshape(1, channels), w_up, w_down, flux_weight, *pieces)


def normalize(values, scales):
    average = jnp.mean(values, axis=-1, keepdims=True)
    centred = values - average
    spread = jnp.mean(centred * centred, axis=-1, keepdims=True)
    return centred * lax.rsqrt(spread + 1e-06) * scales


def channel_mixer(values, scales, w_up, w_down):
    normed = normalize(values, scales).astype(jnp.bfloat16)
    hidden = jax.nn.gelu(
        jnp.dot(normed, w_up, preferred_element_type=jnp.float32), approximate=True
    ).astype(jnp.bfloat16)
    return jnp.dot(hidden, w_down, preferred_element_type=jnp.float32)


def per_device(
    atmosphere,
    conv_weight,
    atm_gain,
    atm_up,
    atm_down,
    flux_weight,
    land_mask,
    tile_owner,
    ocean_state,
    ocn_gain,
    ocn_up,
    ocn_down,
):
    lat_rows, lon_cols, channels = atmosphere.shape
    margin = conv_weight.shape[0] // 2
    owners = tile_owner.reshape(-1)
    tile_count = owners.shape[0]
    peer_count = ocean_state.shape[1]
    capacity = ocean_state.shape[2]
    tile_cells = ocean_state.shape[3]
    pieces = halo_pad(atmosphere, margin)
    atmos_new, fluxes = atmosphere_block(pieces, conv_weight, atmosphere, atm_gain, atm_up, atm_down, flux_weight)
    wet = land_mask.reshape(tile_count, tile_cells, 1).astype(jnp.bfloat16)
    flux_tiles = (fluxes.reshape(tile_count, tile_cells, channels) * wet).reshape(tile_count, tile_cells * channels)
    member = (owners[:, None] == jnp.arange(peer_count, dtype=jnp.int32)[None, :]).astype(jnp.int32)
    tile_rank = jnp.sum(jnp.cumsum(member, axis=0) * member, axis=1) - 1
    slot_index = owners * capacity + tile_rank
    onehot = (
        jnp.arange(peer_count * capacity, dtype=jnp.int32)[:, None] == slot_index[None, :]
    ).astype(jnp.bfloat16)
    outgoing = jnp.dot(onehot, flux_tiles, preferred_element_type=jnp.float32).astype(jnp.bfloat16)
    used = jnp.sum(onehot.astype(jnp.float32), axis=1) > 0
    outgoing = jnp.where(used[:, None], outgoing, jnp.nan).astype(jnp.bfloat16)
    outgoing = outgoing.reshape(peer_count, capacity, tile_cells, channels)
    ocean_out = exchange_and_ocean(outgoing, ocean_state[0], ocn_gain, ocn_up, ocn_down)[None]
    return (atmos_new, ocean_out)


def solution(mesh):
    placed = (
        P("lat", "lon", None),
        P(),
        P(),
        P(),
        P(),
        P(),
        P("lat", "lon"),
        P("lat", "lon", None),
        P(("lat", "lon"), None, None, None, None),
        P(),
        P(),
        P(),
    )
    return jax.shard_map(
        per_device,
        mesh=mesh,
        in_specs=placed,
        out_specs=(P("lat", "lon", None), P(("lat", "lon"), None, None, None, None)),
        check_vma=False,
    )
```

```python
import functools

import jax
import jax.numpy as jnp
from jax import lax
from jax.experimental import pallas as pl
from jax.experimental.pallas import tpu as pltpu
from jax.sharding import PartitionSpec as P

MESH = pl.DeviceIdType.MESH

AXES = ("lat", "lon")


HALO_MOVES = ((1, 0), (-1, 0), (0, 1), (0, -1), (1, 1), (1, -1), (-1, 1), (-1, -1))


def halo_body(n_lat, n_lon, w, side, x_ref, *refs):
    got, send_sems, recv_sems = refs[:8], refs[8], refs[9]
    rows, cols = x_ref.shape[0], x_ref.shape[1]
    lat, lon = lax.axis_index("lat"), lax.axis_index("lon")
    has_up = lat > 0
    has_down = lat < n_lat - 1
    row_part = {1: pl.ds(rows - w, w), -1: pl.ds(0, w), 0: pl.ds(0, rows)}
    col_part = {1: pl.ds(cols - side, side), -1: pl.ds(0, side), 0: pl.ds(0, cols)}

    def exists(d_lat):
        return has_down if d_lat > 0 else (has_up if d_lat < 0 else lat >= 0)

    def exists_from(d_lat):
        return has_up if d_lat > 0 else (has_down if d_lat < 0 else lat >= 0)

    def target(d_lat, d_lon):
        return (lax.rem(lon + d_lon + n_lon, n_lon), lat + d_lat)

    barrier = pltpu.get_barrier_semaphore()
    for d_lat, d_lon in HALO_MOVES:
        @pl.when(exists(d_lat))
        def _():
            pl.semaphore_signal(barrier, inc=1, device_id=target(d_lat, d_lon), device_id_type=MESH)

    pl.semaphore_wait(barrier, 2 + 3 * has_up.astype(jnp.int32) + 3 * has_down.astype(jnp.int32))

    def copy(p):
        d_lat, d_lon = HALO_MOVES[p]
        return pltpu.make_async_remote_copy(
            src_ref=x_ref.at[row_part[d_lat], col_part[d_lon]],
            dst_ref=got[p],
            send_sem=send_sems.at[p],
            recv_sem=recv_sems.at[p],
            device_id=target(d_lat, d_lon),
            device_id_type=MESH,
        )

    for p, (d_lat, d_lon) in enumerate(HALO_MOVES):
        @pl.when(exists(d_lat))
        def _():
            copy(p).start()

    for p, (d_lat, d_lon) in enumerate(HALO_MOVES):
        @pl.when(exists_from(d_lat))
        def _():
            copy(p).wait_recv()

        @pl.when(jnp.logical_not(exists_from(d_lat)))
        def _():
            got[p][...] = jnp.zeros(got[p].shape, got[p].dtype)

    for p, (d_lat, d_lon) in enumerate(HALO_MOVES):
        @pl.when(exists(d_lat))
        def _():
            copy(p).wait_send()


def halo_pad(x, w):
    rows, cols, channels = x.shape
    side = 8
    shapes = []
    for d_lat, d_lon in HALO_MOVES:
        shapes.append((w if d_lat else rows, side if d_lon else cols, channels))
    vmem = pl.BlockSpec(memory_space=pltpu.VMEM)
    got = pl.pallas_call(
        functools.partial(halo_body, lax.axis_size("lat"), lax.axis_size("lon"), w, side),
        out_shape=tuple(jax.ShapeDtypeStruct(sh, x.dtype) for sh in shapes),
        in_specs=[pl.BlockSpec(memory_space=pl.ANY)],
        out_specs=tuple([vmem] * 8),
        scratch_shapes=[pltpu.SemaphoreType.DMA((8,)), pltpu.SemaphoreType.DMA((8,))],
        compiler_params=pltpu.CompilerParams(collective_id=1, has_side_effects=True),
    )(x)
    return got


def exchange_body(n_lon, n, group, out_ref, state_ref, gain_ref, up_ref, down_ref,
                  res_ref, recv_ref, stage_ref, send_sems, recv_sems):
    me = lax.axis_index("lat") * n_lon + lax.axis_index("lon")

    def coords(d):
        return (lax.rem(d, n_lon), lax.div(d, n_lon))

    barrier = pltpu.get_barrier_semaphore()

    @pl.loop(1, n)
    def _(j):
        pl.semaphore_signal(barrier, inc=1, device_id=coords(lax.rem(me + j, n)), device_id_type=MESH)

    pl.semaphore_wait(barrier, n - 1)

    def send_copy(j):
        peer = lax.rem(me + j, n)
        return pltpu.make_async_remote_copy(
            src_ref=out_ref.at[peer],
            dst_ref=recv_ref.at[j],
            send_sem=send_sems.at[j],
            recv_sem=recv_sems.at[j],
            device_id=coords(peer),
            device_id_type=MESH,
        )

    def recv_copy(j):
        source = lax.rem(me - j + n, n)
        return pltpu.make_async_remote_copy(
            src_ref=out_ref.at[source],
            dst_ref=recv_ref.at[j],
            send_sem=send_sems.at[j],
            recv_sem=recv_sems.at[j],
            device_id=coords(source),
            device_id_type=MESH,
        )

    @pl.loop(1, n)
    def _(t):
        half = lax.div(t + 1, 2)
        odd = lax.rem(t, 2)
        send_copy(odd * half + (1 - odd) * (n - half)).start()

    recv_ref[0] = out_ref[me]
    slots, cells, channels = out_ref.shape[1], out_ref.shape[2], out_ref.shape[3]
    rows = group * slots * cells

    groups = n // group

    @pl.loop(0, groups)
    def _(gi):
        odd = lax.rem(gi, 2)
        g = odd * (groups - 1 - lax.div(gi, 2)) + (1 - odd) * lax.div(gi, 2)
        base = g * group

        @pl.loop(0, group)
        def _(i):
            j = base + i

            @pl.when(j > 0)
            def _():
                recv_copy(j).wait_recv()

            stage_ref[i] = state_ref[lax.rem(me - j + n, n)]

        fluxes = recv_ref[pl.ds(base, group)]
        used = fluxes[:, :, 0:1, 0:1] == fluxes[:, :, 0:1, 0:1]
        states = (stage_ref[...].astype(jnp.float32) + fluxes.astype(jnp.float32)).reshape(rows, channels)
        average = jnp.mean(states, axis=-1, keepdims=True)
        centred = states - average
        spread = jnp.mean(centred * centred, axis=-1, keepdims=True)
        normed = (centred * lax.rsqrt(spread + 1e-06) * gain_ref[...]).astype(jnp.bfloat16)
        hidden = jax.nn.gelu(
            jnp.dot(normed, up_ref[...], preferred_element_type=jnp.float32), approximate=True
        ).astype(jnp.bfloat16)
        result = states + jnp.dot(hidden, down_ref[...], preferred_element_type=jnp.float32)
        result = result.reshape(group, slots, cells, channels)
        stage_ref[...] = jnp.where(used, result, 0.0).astype(jnp.bfloat16)

        @pl.loop(0, group)
        def _(i):
            res_ref[lax.rem(me - base - i + n, n)] = stage_ref[i]

    @pl.loop(1, n)
    def _(j):
        send_copy(j).wait_send()


def exchange_and_ocean(outgoing, state, gain, w_up, w_down):
    n_lon = lax.axis_size("lon")
    n = n_lon * lax.axis_size("lat")
    group = 16
    rows = outgoing.shape[0] * outgoing.shape[1] * outgoing.shape[2]
    channels, hid = w_up.shape
    vmem = pl.BlockSpec(memory_space=pltpu.VMEM)
    return pl.pallas_call(
        functools.partial(exchange_body, n_lon, n, group),
        out_shape=jax.ShapeDtypeStruct(outgoing.shape, outgoing.dtype),
        in_specs=[vmem] * 5,
        out_specs=vmem,
        scratch_shapes=[
            pltpu.VMEM(outgoing.shape, outgoing.dtype),
            pltpu.VMEM((group,) + outgoing.shape[1:], outgoing.dtype),
            pltpu.SemaphoreType.DMA((n,)),
            pltpu.SemaphoreType.DMA((n,)),
        ],
        compiler_params=pltpu.CompilerParams(
            collective_id=0, has_side_effects=True, vmem_limit_bytes=48 * 1024 * 1024
        ),
        cost_estimate=pl.CostEstimate(
            flops=4 * rows * channels * hid, transcendentals=rows * hid, bytes_accessed=4 * rows * channels * 2
        ),
    )(outgoing, state, gain.reshape(1, channels), w_up, w_down)


def atmos_body(kw, band, side, w_ref, atm_ref, gain_ref, up_hbm, down_hbm, fw_hbm,
               above, below, left, right, above_left, above_right, below_left, below_right,
               out_ref, flux_ref, xf_ref, xs_ref, mixed_ref, up_ref, down_ref, fw_ref, sems):
    rows, cols, channels = atm_ref.shape
    weights = [
        pltpu.make_async_copy(up_hbm, up_ref, sems.at[0]),
        pltpu.make_async_copy(down_hbm, down_ref, sems.at[1]),
        pltpu.make_async_copy(fw_hbm, fw_ref, sems.at[2]),
    ]
    for copy in weights:
        copy.start()
    m = kw // 2
    for r0, r1, l_ref, c_ref, r_ref in (
        (0, m, above_left, above, above_right),
        (m, m + rows, left, atm_ref, right),
        (m + rows, 2 * m + rows, below_left, below, below_right),
    ):
        xf_ref[r0:r1, 0:side, :] = l_ref[...].astype(jnp.float32)
        xf_ref[r0:r1, side:side + cols, :] = c_ref[...].astype(jnp.float32)
        xf_ref[r0:r1, side + cols:, :] = r_ref[...].astype(jnp.float32)

    @pl.loop(0, rows + 2 * m)
    def _(i):
        for q in range(kw):
            xs_ref[q, i] = xf_ref[i, pl.ds(side - m + q, cols), :]

    @pl.loop(0, rows // band)
    def _(b):
        r0 = b * band
        for cb in range(channels // 128):
            lanes = pl.ds(cb * 128, 128)
            acc = [jnp.zeros((cols, 128), jnp.float32) for _ in range(band)]
            for q in range(kw):
                for i in range(band + kw - 1):
                    line = xs_ref[q, r0 + i, :, lanes]
                    for p in range(kw):
                        r = i - p
                        if 0 <= r < band:
                            acc[r] = acc[r] + line * w_ref[p, pl.ds(q, 1), lanes]
            for r in range(band):
                mixed_ref[r0 + r, :, lanes] = acc[r]

    for copy in weights:
        copy.wait()

    chunk = 8

    @pl.loop(0, rows // chunk)
    def _(k):
        cells = chunk * cols
        mixed = mixed_ref[pl.ds(k * chunk, chunk)].reshape(cells, channels)
        average = jnp.mean(mixed, axis=-1, keepdims=True)
        centred = mixed - average
        spread = jnp.mean(centred * centred, axis=-1, keepdims=True)
        normed = (centred * lax.rsqrt(spread + 1e-06) * gain_ref[...]).astype(jnp.bfloat16)
        hidden = jax.nn.gelu(
            jnp.dot(normed, up_ref[...], preferred_element_type=jnp.float32), approximate=True
        ).astype(jnp.bfloat16)
        branch = jnp.dot(hidden, down_ref[...], preferred_element_type=jnp.float32)
        atmos = atm_ref[pl.ds(k * chunk, chunk)].reshape(cells, channels).astype(jnp.float32)
        new = (atmos + branch).astype(jnp.bfloat16)
        out_ref[pl.ds(k * chunk, chunk)] = new.reshape(chunk, cols, channels)
        flux = jnp.dot(new, fw_ref[...], preferred_element_type=jnp.float32)
        flux_ref[pl.ds(k * cells, cells)] = flux.astype(jnp.bfloat16)


def atmosphere_block(pieces, conv_weight, atmosphere, gain, w_up, w_down, flux_weight):
    rows, cols, channels = atmosphere.shape
    kw = conv_weight.shape[0]
    hid = w_up.shape[1]
    vmem = pl.BlockSpec(memory_space=pltpu.VMEM)
    hbm = pl.BlockSpec(memory_space=pl.ANY)
    cells = rows * cols
    return pl.pallas_call(
        functools.partial(atmos_body, kw, 4, pieces[2].shape[1]),
        out_shape=(
            jax.ShapeDtypeStruct(atmosphere.shape, atmosphere.dtype),
            jax.ShapeDtypeStruct((cells, channels), jnp.bfloat16),
        ),
        in_specs=[vmem] * 3 + [hbm] * 3 + [vmem] * 8,
        out_specs=(vmem, vmem),
        scratch_shapes=[
            pltpu.VMEM((rows + kw - 1, cols + 2 * pieces[2].shape[1], channels), jnp.float32),
            pltpu.VMEM((kw, rows + kw - 1, cols, channels), jnp.float32),
            pltpu.VMEM((rows, cols, channels), jnp.float32),
            pltpu.VMEM(w_up.shape, w_up.dtype),
            pltpu.VMEM(w_down.shape, w_down.dtype),
            pltpu.VMEM(flux_weight.shape, flux_weight.dtype),
            pltpu.SemaphoreType.DMA((3,)),
        ],
        compiler_params=pltpu.CompilerParams(vmem_limit_bytes=56 * 1024 * 1024),
        cost_estimate=pl.CostEstimate(
            flops=2 * cells * channels * (kw * kw + 2 * hid + channels),
            transcendentals=cells * hid,
            bytes_accessed=cells * channels * 8,
        ),
    )(conv_weight, atmosphere, gain.reshape(1, channels), w_up, w_down, flux_weight, *pieces)


def normalize(values, scales):
    average = jnp.mean(values, axis=-1, keepdims=True)
    centred = values - average
    spread = jnp.mean(centred * centred, axis=-1, keepdims=True)
    return centred * lax.rsqrt(spread + 1e-06) * scales


def channel_mixer(values, scales, w_up, w_down):
    normed = normalize(values, scales).astype(jnp.bfloat16)
    hidden = jax.nn.gelu(
        jnp.dot(normed, w_up, preferred_element_type=jnp.float32), approximate=True
    ).astype(jnp.bfloat16)
    return jnp.dot(hidden, w_down, preferred_element_type=jnp.float32)


def per_device(
    atmosphere,
    conv_weight,
    atm_gain,
    atm_up,
    atm_down,
    flux_weight,
    land_mask,
    tile_owner,
    ocean_state,
    ocn_gain,
    ocn_up,
    ocn_down,
):
    lat_rows, lon_cols, channels = atmosphere.shape
    margin = conv_weight.shape[0] // 2
    owners = tile_owner.reshape(-1)
    tile_count = owners.shape[0]
    peer_count = ocean_state.shape[1]
    capacity = ocean_state.shape[2]
    tile_cells = ocean_state.shape[3]
    pieces = halo_pad(atmosphere, margin)
    atmos_new, fluxes = atmosphere_block(pieces, conv_weight, atmosphere, atm_gain, atm_up, atm_down, flux_weight)
    wet = land_mask.reshape(tile_count, tile_cells, 1).astype(jnp.bfloat16)
    flux_tiles = (fluxes.reshape(tile_count, tile_cells, channels) * wet).reshape(tile_count, tile_cells * channels)
    member = (owners[:, None] == jnp.arange(peer_count, dtype=jnp.int32)[None, :]).astype(jnp.int32)
    tile_rank = jnp.sum(jnp.cumsum(member, axis=0) * member, axis=1) - 1
    slot_index = owners * capacity + tile_rank
    onehot = (
        jnp.arange(peer_count * capacity, dtype=jnp.int32)[:, None] == slot_index[None, :]
    ).astype(jnp.bfloat16)
    outgoing = jnp.dot(onehot, flux_tiles, preferred_element_type=jnp.float32).astype(jnp.bfloat16)
    used = jnp.sum(onehot.astype(jnp.float32), axis=1) > 0
    outgoing = jnp.where(used[:, None], outgoing, jnp.nan).astype(jnp.bfloat16)
    outgoing = outgoing.reshape(peer_count, capacity, tile_cells, channels)
    ocean_out = exchange_and_ocean(outgoing, ocean_state[0], ocn_gain, ocn_up, ocn_down)[None]
    return (atmos_new, ocean_out)


def solution(mesh):
    placed = (
        P("lat", "lon", None),
        P(),
        P(),
        P(),
        P(),
        P(),
        P("lat", "lon"),
        P("lat", "lon", None),
        P(("lat", "lon"), None, None, None, None),
        P(),
        P(),
        P(),
    )
    return jax.shard_map(
        per_device,
        mesh=mesh,
        in_specs=placed,
        out_specs=(P("lat", "lon", None), P(("lat", "lon"), None, None, None, None)),
        check_vma=False,
    )
```

```python
import functools

import jax
import jax.numpy as jnp
from jax import lax
from jax.experimental import pallas as pl
from jax.experimental.pallas import tpu as pltpu
from jax.sharding import PartitionSpec as P

MESH = pl.DeviceIdType.MESH

AXES = ("lat", "lon")


HALO_MOVES = ((1, 0), (-1, 0), (0, 1), (0, -1), (1, 1), (1, -1), (-1, 1), (-1, -1))


def exchange_body(n_lon, n, group, out_ref, state_ref, gain_ref, up_ref, down_ref,
                  res_ref, recv_ref, stage_ref, send_sems, recv_sems):
    me = lax.axis_index("lat") * n_lon + lax.axis_index("lon")

    def coords(d):
        return (lax.rem(d, n_lon), lax.div(d, n_lon))

    barrier = pltpu.get_barrier_semaphore()

    @pl.loop(1, n)
    def _(j):
        pl.semaphore_signal(barrier, inc=1, device_id=coords(lax.rem(me + j, n)), device_id_type=MESH)

    pl.semaphore_wait(barrier, n - 1)

    def send_copy(j):
        peer = lax.rem(me + j, n)
        return pltpu.make_async_remote_copy(
            src_ref=out_ref.at[peer],
            dst_ref=recv_ref.at[j],
            send_sem=send_sems.at[j],
            recv_sem=recv_sems.at[j],
            device_id=coords(peer),
            device_id_type=MESH,
        )

    def recv_copy(j):
        source = lax.rem(me - j + n, n)
        return pltpu.make_async_remote_copy(
            src_ref=out_ref.at[source],
            dst_ref=recv_ref.at[j],
            send_sem=send_sems.at[j],
            recv_sem=recv_sems.at[j],
            device_id=coords(source),
            device_id_type=MESH,
        )

    @pl.loop(1, n)
    def _(j):
        send_copy(j).start()

    recv_ref[0] = out_ref[me]
    slots, cells, channels = out_ref.shape[1], out_ref.shape[2], out_ref.shape[3]
    rows = group * slots * cells

    @pl.loop(0, n // group)
    def _(g):
        base = g * group

        @pl.loop(0, group)
        def _(i):
            j = base + i

            @pl.when(j > 0)
            def _():
                recv_copy(j).wait_recv()

            stage_ref[i] = state_ref[lax.rem(me - j + n, n)]

        fluxes = recv_ref[pl.ds(base, group)]
        used = fluxes[:, :, 0:1, 0:1] == fluxes[:, :, 0:1, 0:1]
        states = (stage_ref[...].astype(jnp.float32) + fluxes.astype(jnp.float32)).reshape(rows, channels)
        average = jnp.mean(states, axis=-1, keepdims=True)
        centred = states - average
        spread = jnp.mean(centred * centred, axis=-1, keepdims=True)
        normed = (centred * lax.rsqrt(spread + 1e-06) * gain_ref[...]).astype(jnp.bfloat16)
        hidden = jax.nn.gelu(
            jnp.dot(normed, up_ref[...], preferred_element_type=jnp.float32), approximate=True
        ).astype(jnp.bfloat16)
        result = states + jnp.dot(hidden, down_ref[...], preferred_element_type=jnp.float32)
        result = result.reshape(group, slots, cells, channels)
        stage_ref[...] = jnp.where(used, result, 0.0).astype(jnp.bfloat16)

        @pl.loop(0, group)
        def _(i):
            res_ref[lax.rem(me - base - i + n, n)] = stage_ref[i]

    @pl.loop(1, n)
    def _(j):
        send_copy(j).wait_send()


def exchange_and_ocean(outgoing, state, gain, w_up, w_down):
    n_lon = lax.axis_size("lon")
    n = n_lon * lax.axis_size("lat")
    group = 16
    rows = outgoing.shape[0] * outgoing.shape[1] * outgoing.shape[2]
    channels, hid = w_up.shape
    vmem = pl.BlockSpec(memory_space=pltpu.VMEM)
    return pl.pallas_call(
        functools.partial(exchange_body, n_lon, n, group),
        out_shape=jax.ShapeDtypeStruct(outgoing.shape, outgoing.dtype),
        in_specs=[vmem] * 5,
        out_specs=vmem,
        scratch_shapes=[
            pltpu.VMEM(outgoing.shape, outgoing.dtype),
            pltpu.VMEM((group,) + outgoing.shape[1:], outgoing.dtype),
            pltpu.SemaphoreType.DMA((n,)),
            pltpu.SemaphoreType.DMA((n,)),
        ],
        compiler_params=pltpu.CompilerParams(
            collective_id=0, has_side_effects=True, vmem_limit_bytes=48 * 1024 * 1024
        ),
        cost_estimate=pl.CostEstimate(
            flops=4 * rows * channels * hid, transcendentals=rows * hid, bytes_accessed=4 * rows * channels * 2
        ),
    )(outgoing, state, gain.reshape(1, channels), w_up, w_down)


def atmos_body(n_lat, n_lon, kw, band, side, x_hbm, w_ref, atm_ref, gain_ref, up_hbm, down_hbm, fw_hbm,
               out_ref, flux_ref, above, below, left, right, above_left, above_right, below_left, below_right,
               xf_ref, xs_ref, mixed_ref, up_ref, down_ref, fw_ref, sems, send_sems, recv_sems):
    rows, cols, channels = atm_ref.shape
    m = kw // 2
    got = (above, below, left, right, above_left, above_right, below_left, below_right)
    lat, lon = lax.axis_index("lat"), lax.axis_index("lon")
    has_up = lat > 0
    has_down = lat < n_lat - 1
    row_part = {1: pl.ds(rows - m, m), -1: pl.ds(0, m), 0: pl.ds(0, rows)}
    col_part = {1: pl.ds(cols - side, side), -1: pl.ds(0, side), 0: pl.ds(0, cols)}

    def exists(d_lat):
        return has_down if d_lat > 0 else (has_up if d_lat < 0 else lat >= 0)

    def exists_from(d_lat):
        return has_up if d_lat > 0 else (has_down if d_lat < 0 else lat >= 0)

    def target(d_lat, d_lon):
        return (lax.rem(lon + d_lon + n_lon, n_lon), lat + d_lat)

    barrier = pltpu.get_barrier_semaphore()
    for d_lat, d_lon in HALO_MOVES:
        @pl.when(exists(d_lat))
        def _():
            pl.semaphore_signal(barrier, inc=1, device_id=target(d_lat, d_lon), device_id_type=MESH)

    pl.semaphore_wait(barrier, 2 + 3 * has_up.astype(jnp.int32) + 3 * has_down.astype(jnp.int32))

    def halo_copy(p):
        d_lat, d_lon = HALO_MOVES[p]
        return pltpu.make_async_remote_copy(
            src_ref=x_hbm.at[row_part[d_lat], col_part[d_lon]],
            dst_ref=got[p],
            send_sem=send_sems.at[p],
            recv_sem=recv_sems.at[p],
            device_id=target(d_lat, d_lon),
            device_id_type=MESH,
        )

    for p, (d_lat, d_lon) in enumerate(HALO_MOVES):
        @pl.when(exists(d_lat))
        def _():
            halo_copy(p).start()

    weights = [
        pltpu.make_async_copy(up_hbm, up_ref, sems.at[0]),
        pltpu.make_async_copy(down_hbm, down_ref, sems.at[1]),
        pltpu.make_async_copy(fw_hbm, fw_ref, sems.at[2]),
    ]
    for copy in weights:
        copy.start()

    xf_ref[m:m + rows, 0:side, :] = jnp.zeros((rows, side, channels), jnp.float32)
    xf_ref[m:m + rows, side:side + cols, :] = atm_ref[...].astype(jnp.float32)
    xf_ref[m:m + rows, side + cols:, :] = jnp.zeros((rows, side, channels), jnp.float32)

    def shift_rows(lo, hi, c0, width):
        @pl.loop(lo, hi)
        def _(i):
            for q in range(kw):
                xs_ref[q, i, pl.ds(c0, width), :] = xf_ref[i, pl.ds(side - m + q + c0, width), :]

    def conv_band(r0, c0, width):
        for cb in range(channels // 128):
            lanes = pl.ds(cb * 128, 128)
            acc = [jnp.zeros((width, 128), jnp.float32) for _ in range(band)]
            for q in range(kw):
                for i in range(band + kw - 1):
                    line = xs_ref[q, r0 + i, pl.ds(c0, width), lanes]
                    for p in range(kw):
                        r = i - p
                        if 0 <= r < band:
                            acc[r] = acc[r] + line * w_ref[p, pl.ds(q, 1), lanes]
            for r in range(band):
                mixed_ref[r0 + r, pl.ds(c0, width), lanes] = acc[r]

    shift_rows(m, m + rows, 0, cols)
    bands = rows // band

    @pl.loop(1, bands - 1)
    def _(b):
        conv_band(b * band, 0, cols)

    for p, (d_lat, d_lon) in enumerate(HALO_MOVES):
        @pl.when(exists_from(d_lat))
        def _():
            halo_copy(p).wait_recv()

        @pl.when(jnp.logical_not(exists_from(d_lat)))
        def _():
            got[p][...] = jnp.zeros(got[p].shape, got[p].dtype)

    for r0, r1, l_ref, c_ref, r_ref in (
        (0, m, above_left, above, above_right),
        (m, m + rows, left, None, right),
        (m + rows, 2 * m + rows, below_left, below, below_right),
    ):
        xf_ref[r0:r1, 0:side, :] = l_ref[...].astype(jnp.float32)
        if c_ref is not None:
            xf_ref[r0:r1, side:side + cols, :] = c_ref[...].astype(jnp.float32)
        xf_ref[r0:r1, side + cols:, :] = r_ref[...].astype(jnp.float32)

    shift_rows(0, m, 0, cols)
    shift_rows(m + rows, rows + 2 * m, 0, cols)
    shift_rows(m, m + rows, 0, 8)
    shift_rows(m, m + rows, cols - 8, 8)

    @pl.loop(0, 2)
    def _(t):
        conv_band(t * (bands - 1) * band, 0, cols)

    @pl.loop(1, bands - 1)
    def _(b):
        conv_band(b * band, 0, 8)
        conv_band(b * band, cols - 8, 8)

    for copy in weights:
        copy.wait()

    for p, (d_lat, d_lon) in enumerate(HALO_MOVES):
        @pl.when(exists(d_lat))
        def _():
            halo_copy(p).wait_send()

    chunk = 8

    @pl.loop(0, rows // chunk)
    def _(k):
        cells = chunk * cols
        mixed = mixed_ref[pl.ds(k * chunk, chunk)].reshape(cells, channels)
        average = jnp.mean(mixed, axis=-1, keepdims=True)
        centred = mixed - average
        spread = jnp.mean(centred * centred, axis=-1, keepdims=True)
        normed = (centred * lax.rsqrt(spread + 1e-06) * gain_ref[...]).astype(jnp.bfloat16)
        hidden = jax.nn.gelu(
            jnp.dot(normed, up_ref[...], preferred_element_type=jnp.float32), approximate=True
        ).astype(jnp.bfloat16)
        branch = jnp.dot(hidden, down_ref[...], preferred_element_type=jnp.float32)
        atmos = atm_ref[pl.ds(k * chunk, chunk)].reshape(cells, channels).astype(jnp.float32)
        new = (atmos + branch).astype(jnp.bfloat16)
        out_ref[pl.ds(k * chunk, chunk)] = new.reshape(chunk, cols, channels)
        flux = jnp.dot(new, fw_ref[...], preferred_element_type=jnp.float32)
        flux_ref[pl.ds(k * cells, cells)] = flux.astype(jnp.bfloat16)


def atmosphere_block(conv_weight, atmosphere, gain, w_up, w_down, flux_weight):
    rows, cols, channels = atmosphere.shape
    kw = conv_weight.shape[0]
    m = kw // 2
    side = 8
    hid = w_up.shape[1]
    vmem = pl.BlockSpec(memory_space=pltpu.VMEM)
    hbm = pl.BlockSpec(memory_space=pl.ANY)
    cells = rows * cols
    pieces = []
    for d_lat, d_lon in HALO_MOVES:
        pieces.append(pltpu.VMEM((m if d_lat else rows, side if d_lon else cols, channels), atmosphere.dtype))
    return pl.pallas_call(
        functools.partial(atmos_body, lax.axis_size("lat"), lax.axis_size("lon"), kw, 4, side),
        out_shape=(
            jax.ShapeDtypeStruct(atmosphere.shape, atmosphere.dtype),
            jax.ShapeDtypeStruct((cells, channels), jnp.bfloat16),
        ),
        in_specs=[hbm] + [vmem] * 3 + [hbm] * 3,
        out_specs=(vmem, vmem),
        scratch_shapes=pieces + [
            pltpu.VMEM((rows + kw - 1, cols + 2 * side, channels), jnp.float32),
            pltpu.VMEM((kw, rows + kw - 1, cols, channels), jnp.float32),
            pltpu.VMEM((rows, cols, channels), jnp.float32),
            pltpu.VMEM(w_up.shape, w_up.dtype),
            pltpu.VMEM(w_down.shape, w_down.dtype),
            pltpu.VMEM(flux_weight.shape, flux_weight.dtype),
            pltpu.SemaphoreType.DMA((3,)),
            pltpu.SemaphoreType.DMA((8,)),
            pltpu.SemaphoreType.DMA((8,)),
        ],
        compiler_params=pltpu.CompilerParams(
            collective_id=1, has_side_effects=True, vmem_limit_bytes=56 * 1024 * 1024
        ),
        cost_estimate=pl.CostEstimate(
            flops=2 * cells * channels * (kw * kw + 2 * hid + channels),
            transcendentals=cells * hid,
            bytes_accessed=cells * channels * 8,
        ),
    )(atmosphere, conv_weight, atmosphere, gain.reshape(1, channels), w_up, w_down, flux_weight)


def normalize(values, scales):
    average = jnp.mean(values, axis=-1, keepdims=True)
    centred = values - average
    spread = jnp.mean(centred * centred, axis=-1, keepdims=True)
    return centred * lax.rsqrt(spread + 1e-06) * scales


def channel_mixer(values, scales, w_up, w_down):
    normed = normalize(values, scales).astype(jnp.bfloat16)
    hidden = jax.nn.gelu(
        jnp.dot(normed, w_up, preferred_element_type=jnp.float32), approximate=True
    ).astype(jnp.bfloat16)
    return jnp.dot(hidden, w_down, preferred_element_type=jnp.float32)


def per_device(
    atmosphere,
    conv_weight,
    atm_gain,
    atm_up,
    atm_down,
    flux_weight,
    land_mask,
    tile_owner,
    ocean_state,
    ocn_gain,
    ocn_up,
    ocn_down,
):
    lat_rows, lon_cols, channels = atmosphere.shape
    margin = conv_weight.shape[0] // 2
    owners = tile_owner.reshape(-1)
    tile_count = owners.shape[0]
    peer_count = ocean_state.shape[1]
    capacity = ocean_state.shape[2]
    tile_cells = ocean_state.shape[3]
    atmos_new, fluxes = atmosphere_block(conv_weight, atmosphere, atm_gain, atm_up, atm_down, flux_weight)
    wet = land_mask.reshape(tile_count, tile_cells, 1).astype(jnp.bfloat16)
    flux_tiles = (fluxes.reshape(tile_count, tile_cells, channels) * wet).reshape(tile_count, tile_cells * channels)
    member = (owners[:, None] == jnp.arange(peer_count, dtype=jnp.int32)[None, :]).astype(jnp.int32)
    tile_rank = jnp.sum(jnp.cumsum(member, axis=0) * member, axis=1) - 1
    slot_index = owners * capacity + tile_rank
    onehot = (
        jnp.arange(peer_count * capacity, dtype=jnp.int32)[:, None] == slot_index[None, :]
    ).astype(jnp.bfloat16)
    outgoing = jnp.dot(onehot, flux_tiles, preferred_element_type=jnp.float32).astype(jnp.bfloat16)
    used = jnp.sum(onehot.astype(jnp.float32), axis=1) > 0
    outgoing = jnp.where(used[:, None], outgoing, jnp.nan).astype(jnp.bfloat16)
    outgoing = outgoing.reshape(peer_count, capacity, tile_cells, channels)
    ocean_out = exchange_and_ocean(outgoing, ocean_state[0], ocn_gain, ocn_up, ocn_down)[None]
    return (atmos_new, ocean_out)


def solution(mesh):
    placed = (
        P("lat", "lon", None),
        P(),
        P(),
        P(),
        P(),
        P(),
        P("lat", "lon"),
        P("lat", "lon", None),
        P(("lat", "lon"), None, None, None, None),
        P(),
        P(),
        P(),
    )
    return jax.shard_map(
        per_device,
        mesh=mesh,
        in_specs=placed,
        out_specs=(P("lat", "lon", None), P(("lat", "lon"), None, None, None, None)),
        check_vma=False,
    )
```

```python
import functools

import jax
import jax.numpy as jnp
from jax import lax
from jax.experimental import pallas as pl
from jax.experimental.pallas import tpu as pltpu
from jax.sharding import PartitionSpec as P

MESH = pl.DeviceIdType.MESH

AXES = ("lat", "lon")


HALO_MOVES = ((1, 0), (-1, 0), (0, 1), (0, -1), (1, 1), (1, -1), (-1, 1), (-1, -1))


def exchange_body(n_lon, n, group, out_ref, state_ref, gain_ref, up_ref, down_ref,
                  res_ref, recv_ref, stage_ref, send_sems, recv_sems):
    me = lax.axis_index("lat") * n_lon + lax.axis_index("lon")

    def coords(d):
        return (lax.rem(d, n_lon), lax.div(d, n_lon))

    barrier = pltpu.get_barrier_semaphore()

    @pl.loop(1, n)
    def _(j):
        pl.semaphore_signal(barrier, inc=1, device_id=coords(lax.rem(me + j, n)), device_id_type=MESH)

    pl.semaphore_wait(barrier, n - 1)

    def send_copy(j):
        peer = lax.rem(me + j, n)
        return pltpu.make_async_remote_copy(
            src_ref=out_ref.at[peer],
            dst_ref=recv_ref.at[j],
            send_sem=send_sems.at[j],
            recv_sem=recv_sems.at[j],
            device_id=coords(peer),
            device_id_type=MESH,
        )

    def recv_copy(j):
        source = lax.rem(me - j + n, n)
        return pltpu.make_async_remote_copy(
            src_ref=out_ref.at[source],
            dst_ref=recv_ref.at[j],
            send_sem=send_sems.at[j],
            recv_sem=recv_sems.at[j],
            device_id=coords(source),
            device_id_type=MESH,
        )

    @pl.loop(1, n)
    def _(j):
        send_copy(j).start()

    recv_ref[0] = out_ref[me]
    slots, cells, channels = out_ref.shape[1], out_ref.shape[2], out_ref.shape[3]
    rows = group * slots * cells

    @pl.loop(0, n // group)
    def _(g):
        base = g * group

        @pl.loop(0, group)
        def _(i):
            j = base + i

            @pl.when(j > 0)
            def _():
                recv_copy(j).wait_recv()

            stage_ref[i] = state_ref[lax.rem(me - j + n, n)]

        fluxes = recv_ref[pl.ds(base, group)]
        used = fluxes[:, :, 0:1, 0:1] == fluxes[:, :, 0:1, 0:1]
        states = (stage_ref[...].astype(jnp.float32) + fluxes.astype(jnp.float32)).reshape(rows, channels)
        average = jnp.mean(states, axis=-1, keepdims=True)
        centred = states - average
        spread = jnp.mean(centred * centred, axis=-1, keepdims=True)
        normed = (centred * lax.rsqrt(spread + 1e-06) * gain_ref[...]).astype(jnp.bfloat16)
        hidden = jax.nn.gelu(
            jnp.dot(normed, up_ref[...], preferred_element_type=jnp.float32), approximate=True
        ).astype(jnp.bfloat16)
        result = states + jnp.dot(hidden, down_ref[...], preferred_element_type=jnp.float32)
        result = result.reshape(group, slots, cells, channels)
        stage_ref[...] = jnp.where(used, result, 0.0).astype(jnp.bfloat16)

        @pl.loop(0, group)
        def _(i):
            res_ref[lax.rem(me - base - i + n, n)] = stage_ref[i]

    @pl.loop(1, n)
    def _(j):
        send_copy(j).wait_send()


def exchange_and_ocean(outgoing, state, gain, w_up, w_down):
    n_lon = lax.axis_size("lon")
    n = n_lon * lax.axis_size("lat")
    group = 8
    rows = outgoing.shape[0] * outgoing.shape[1] * outgoing.shape[2]
    channels, hid = w_up.shape
    vmem = pl.BlockSpec(memory_space=pltpu.VMEM)
    return pl.pallas_call(
        functools.partial(exchange_body, n_lon, n, group),
        out_shape=jax.ShapeDtypeStruct(outgoing.shape, outgoing.dtype),
        in_specs=[vmem] * 5,
        out_specs=vmem,
        scratch_shapes=[
            pltpu.VMEM(outgoing.shape, outgoing.dtype),
            pltpu.VMEM((group,) + outgoing.shape[1:], outgoing.dtype),
            pltpu.SemaphoreType.DMA((n,)),
            pltpu.SemaphoreType.DMA((n,)),
        ],
        compiler_params=pltpu.CompilerParams(
            collective_id=0, has_side_effects=True, vmem_limit_bytes=48 * 1024 * 1024
        ),
        cost_estimate=pl.CostEstimate(
            flops=4 * rows * channels * hid, transcendentals=rows * hid, bytes_accessed=4 * rows * channels * 2
        ),
    )(outgoing, state, gain.reshape(1, channels), w_up, w_down)


def atmos_body(n_lat, n_lon, kw, band, side, x_hbm, w_ref, atm_ref, gain_ref, up_hbm, down_hbm, fw_hbm,
               out_ref, flux_ref, above, below, left, right, above_left, above_right, below_left, below_right,
               xf_ref, xs_ref, mixed_ref, up_ref, down_ref, fw_ref, sems, send_sems, recv_sems):
    rows, cols, channels = atm_ref.shape
    m = kw // 2
    got = (above, below, left, right, above_left, above_right, below_left, below_right)
    lat, lon = lax.axis_index("lat"), lax.axis_index("lon")
    has_up = lat > 0
    has_down = lat < n_lat - 1
    row_part = {1: pl.ds(rows - m, m), -1: pl.ds(0, m), 0: pl.ds(0, rows)}
    col_part = {1: pl.ds(cols - side, side), -1: pl.ds(0, side), 0: pl.ds(0, cols)}

    def exists(d_lat):
        return has_down if d_lat > 0 else (has_up if d_lat < 0 else lat >= 0)

    def exists_from(d_lat):
        return has_up if d_lat > 0 else (has_down if d_lat < 0 else lat >= 0)

    def target(d_lat, d_lon):
        return (lax.rem(lon + d_lon + n_lon, n_lon), lat + d_lat)

    barrier = pltpu.get_barrier_semaphore()
    for d_lat, d_lon in HALO_MOVES:
        @pl.when(exists(d_lat))
        def _():
            pl.semaphore_signal(barrier, inc=1, device_id=target(d_lat, d_lon), device_id_type=MESH)

    pl.semaphore_wait(barrier, 2 + 3 * has_up.astype(jnp.int32) + 3 * has_down.astype(jnp.int32))

    def halo_copy(p):
        d_lat, d_lon = HALO_MOVES[p]
        return pltpu.make_async_remote_copy(
            src_ref=x_hbm.at[row_part[d_lat], col_part[d_lon]],
            dst_ref=got[p],
            send_sem=send_sems.at[p],
            recv_sem=recv_sems.at[p],
            device_id=target(d_lat, d_lon),
            device_id_type=MESH,
        )

    for p, (d_lat, d_lon) in enumerate(HALO_MOVES):
        @pl.when(exists(d_lat))
        def _():
            halo_copy(p).start()

    weights = [
        pltpu.make_async_copy(up_hbm, up_ref, sems.at[0]),
        pltpu.make_async_copy(down_hbm, down_ref, sems.at[1]),
        pltpu.make_async_copy(fw_hbm, fw_ref, sems.at[2]),
    ]
    for copy in weights:
        copy.start()

    xf_ref[m:m + rows, 0:side, :] = jnp.zeros((rows, side, channels), jnp.float32)
    xf_ref[m:m + rows, side:side + cols, :] = atm_ref[...].astype(jnp.float32)
    xf_ref[m:m + rows, side + cols:, :] = jnp.zeros((rows, side, channels), jnp.float32)

    def shift_rows(lo, hi, c0, width):
        @pl.loop(lo, hi)
        def _(i):
            for q in range(kw):
                xs_ref[q, i, pl.ds(c0, width), :] = xf_ref[i, pl.ds(side - m + q + c0, width), :]

    def conv_band(r0, c0, width):
        for cb in range(channels // 128):
            lanes = pl.ds(cb * 128, 128)
            acc = [jnp.zeros((width, 128), jnp.float32) for _ in range(band)]
            for q in range(kw):
                for i in range(band + kw - 1):
                    line = xs_ref[q, r0 + i, pl.ds(c0, width), lanes]
                    for p in range(kw):
                        r = i - p
                        if 0 <= r < band:
                            acc[r] = acc[r] + line * w_ref[p, pl.ds(q, 1), lanes]
            for r in range(band):
                mixed_ref[r0 + r, pl.ds(c0, width), lanes] = acc[r]

    shift_rows(m, m + rows, 0, cols)
    bands = rows // band

    @pl.loop(1, bands - 1)
    def _(b):
        conv_band(b * band, 0, cols)

    for p, (d_lat, d_lon) in enumerate(HALO_MOVES):
        @pl.when(exists_from(d_lat))
        def _():
            halo_copy(p).wait_recv()

        @pl.when(jnp.logical_not(exists_from(d_lat)))
        def _():
            got[p][...] = jnp.zeros(got[p].shape, got[p].dtype)

    for r0, r1, l_ref, c_ref, r_ref in (
        (0, m, above_left, above, above_right),
        (m, m + rows, left, None, right),
        (m + rows, 2 * m + rows, below_left, below, below_right),
    ):
        xf_ref[r0:r1, 0:side, :] = l_ref[...].astype(jnp.float32)
        if c_ref is not None:
            xf_ref[r0:r1, side:side + cols, :] = c_ref[...].astype(jnp.float32)
        xf_ref[r0:r1, side + cols:, :] = r_ref[...].astype(jnp.float32)

    shift_rows(0, m, 0, cols)
    shift_rows(m + rows, rows + 2 * m, 0, cols)
    shift_rows(m, m + rows, 0, 8)
    shift_rows(m, m + rows, cols - 8, 8)

    @pl.loop(0, 2)
    def _(t):
        conv_band(t * (bands - 1) * band, 0, cols)

    @pl.loop(1, bands - 1)
    def _(b):
        conv_band(b * band, 0, 8)
        conv_band(b * band, cols - 8, 8)

    for copy in weights:
        copy.wait()

    for p, (d_lat, d_lon) in enumerate(HALO_MOVES):
        @pl.when(exists(d_lat))
        def _():
            halo_copy(p).wait_send()

    chunk = 8

    @pl.loop(0, rows // chunk)
    def _(k):
        cells = chunk * cols
        mixed = mixed_ref[pl.ds(k * chunk, chunk)].reshape(cells, channels)
        average = jnp.mean(mixed, axis=-1, keepdims=True)
        centred = mixed - average
        spread = jnp.mean(centred * centred, axis=-1, keepdims=True)
        normed = (centred * lax.rsqrt(spread + 1e-06) * gain_ref[...]).astype(jnp.bfloat16)
        hidden = jax.nn.gelu(
            jnp.dot(normed, up_ref[...], preferred_element_type=jnp.float32), approximate=True
        ).astype(jnp.bfloat16)
        branch = jnp.dot(hidden, down_ref[...], preferred_element_type=jnp.float32)
        atmos = atm_ref[pl.ds(k * chunk, chunk)].reshape(cells, channels).astype(jnp.float32)
        new = (atmos + branch).astype(jnp.bfloat16)
        out_ref[pl.ds(k * chunk, chunk)] = new.reshape(chunk, cols, channels)
        flux = jnp.dot(new, fw_ref[...], preferred_element_type=jnp.float32)
        flux_ref[pl.ds(k * cells, cells)] = flux.astype(jnp.bfloat16)


def atmosphere_block(conv_weight, atmosphere, gain, w_up, w_down, flux_weight):
    rows, cols, channels = atmosphere.shape
    kw = conv_weight.shape[0]
    m = kw // 2
    side = 8
    hid = w_up.shape[1]
    vmem = pl.BlockSpec(memory_space=pltpu.VMEM)
    hbm = pl.BlockSpec(memory_space=pl.ANY)
    cells = rows * cols
    pieces = []
    for d_lat, d_lon in HALO_MOVES:
        pieces.append(pltpu.VMEM((m if d_lat else rows, side if d_lon else cols, channels), atmosphere.dtype))
    return pl.pallas_call(
        functools.partial(atmos_body, lax.axis_size("lat"), lax.axis_size("lon"), kw, 4, side),
        out_shape=(
            jax.ShapeDtypeStruct(atmosphere.shape, atmosphere.dtype),
            jax.ShapeDtypeStruct((cells, channels), jnp.bfloat16),
        ),
        in_specs=[hbm] + [vmem] * 3 + [hbm] * 3,
        out_specs=(vmem, vmem),
        scratch_shapes=pieces + [
            pltpu.VMEM((rows + kw - 1, cols + 2 * side, channels), jnp.float32),
            pltpu.VMEM((kw, rows + kw - 1, cols, channels), jnp.float32),
            pltpu.VMEM((rows, cols, channels), jnp.float32),
            pltpu.VMEM(w_up.shape, w_up.dtype),
            pltpu.VMEM(w_down.shape, w_down.dtype),
            pltpu.VMEM(flux_weight.shape, flux_weight.dtype),
            pltpu.SemaphoreType.DMA((3,)),
            pltpu.SemaphoreType.DMA((8,)),
            pltpu.SemaphoreType.DMA((8,)),
        ],
        compiler_params=pltpu.CompilerParams(
            collective_id=1, has_side_effects=True, vmem_limit_bytes=56 * 1024 * 1024
        ),
        cost_estimate=pl.CostEstimate(
            flops=2 * cells * channels * (kw * kw + 2 * hid + channels),
            transcendentals=cells * hid,
            bytes_accessed=cells * channels * 8,
        ),
    )(atmosphere, conv_weight, atmosphere, gain.reshape(1, channels), w_up, w_down, flux_weight)


def normalize(values, scales):
    average = jnp.mean(values, axis=-1, keepdims=True)
    centred = values - average
    spread = jnp.mean(centred * centred, axis=-1, keepdims=True)
    return centred * lax.rsqrt(spread + 1e-06) * scales


def channel_mixer(values, scales, w_up, w_down):
    normed = normalize(values, scales).astype(jnp.bfloat16)
    hidden = jax.nn.gelu(
        jnp.dot(normed, w_up, preferred_element_type=jnp.float32), approximate=True
    ).astype(jnp.bfloat16)
    return jnp.dot(hidden, w_down, preferred_element_type=jnp.float32)


def per_device(
    atmosphere,
    conv_weight,
    atm_gain,
    atm_up,
    atm_down,
    flux_weight,
    land_mask,
    tile_owner,
    ocean_state,
    ocn_gain,
    ocn_up,
    ocn_down,
):
    lat_rows, lon_cols, channels = atmosphere.shape
    margin = conv_weight.shape[0] // 2
    owners = tile_owner.reshape(-1)
    tile_count = owners.shape[0]
    peer_count = ocean_state.shape[1]
    capacity = ocean_state.shape[2]
    tile_cells = ocean_state.shape[3]
    atmos_new, fluxes = atmosphere_block(conv_weight, atmosphere, atm_gain, atm_up, atm_down, flux_weight)
    wet = land_mask.reshape(tile_count, tile_cells, 1).astype(jnp.bfloat16)
    flux_tiles = (fluxes.reshape(tile_count, tile_cells, channels) * wet).reshape(tile_count, tile_cells * channels)
    member = (owners[:, None] == jnp.arange(peer_count, dtype=jnp.int32)[None, :]).astype(jnp.int32)
    tile_rank = jnp.sum(jnp.cumsum(member, axis=0) * member, axis=1) - 1
    slot_index = owners * capacity + tile_rank
    onehot = (
        jnp.arange(peer_count * capacity, dtype=jnp.int32)[:, None] == slot_index[None, :]
    ).astype(jnp.bfloat16)
    outgoing = jnp.dot(onehot, flux_tiles, preferred_element_type=jnp.float32).astype(jnp.bfloat16)
    used = jnp.sum(onehot.astype(jnp.float32), axis=1) > 0
    outgoing = jnp.where(used[:, None], outgoing, jnp.nan).astype(jnp.bfloat16)
    outgoing = outgoing.reshape(peer_count, capacity, tile_cells, channels)
    ocean_out = exchange_and_ocean(outgoing, ocean_state[0], ocn_gain, ocn_up, ocn_down)[None]
    return (atmos_new, ocean_out)


def solution(mesh):
    placed = (
        P("lat", "lon", None),
        P(),
        P(),
        P(),
        P(),
        P(),
        P("lat", "lon"),
        P("lat", "lon", None),
        P(("lat", "lon"), None, None, None, None),
        P(),
        P(),
        P(),
    )
    return jax.shard_map(
        per_device,
        mesh=mesh,
        in_specs=placed,
        out_specs=(P("lat", "lon", None), P(("lat", "lon"), None, None, None, None)),
        check_vma=False,
    )
```

```python
import functools

import jax
import jax.numpy as jnp
from jax import lax
from jax.experimental import pallas as pl
from jax.experimental.pallas import tpu as pltpu
from jax.sharding import PartitionSpec as P

MESH = pl.DeviceIdType.MESH

AXES = ("lat", "lon")


HALO_MOVES = ((1, 0), (-1, 0), (0, 1), (0, -1), (1, 1), (1, -1), (-1, 1), (-1, -1))


def exchange_body(n_lon, n, group, out_ref, state_ref, gain_ref, up_ref, down_ref,
                  res_ref, recv_ref, stage_ref, send_sems, recv_sems):
    me = lax.axis_index("lat") * n_lon + lax.axis_index("lon")

    def coords(d):
        return (lax.rem(d, n_lon), lax.div(d, n_lon))

    barrier = pltpu.get_barrier_semaphore()

    @pl.loop(1, n)
    def _(j):
        pl.semaphore_signal(barrier, inc=1, device_id=coords(lax.rem(me + j, n)), device_id_type=MESH)

    pl.semaphore_wait(barrier, n - 1)

    def send_copy(j):
        peer = lax.rem(me + j, n)
        return pltpu.make_async_remote_copy(
            src_ref=out_ref.at[peer],
            dst_ref=recv_ref.at[j],
            send_sem=send_sems.at[j],
            recv_sem=recv_sems.at[j],
            device_id=coords(peer),
            device_id_type=MESH,
        )

    def recv_copy(j):
        source = lax.rem(me - j + n, n)
        return pltpu.make_async_remote_copy(
            src_ref=out_ref.at[source],
            dst_ref=recv_ref.at[j],
            send_sem=send_sems.at[j],
            recv_sem=recv_sems.at[j],
            device_id=coords(source),
            device_id_type=MESH,
        )

    @pl.loop(1, n)
    def _(j):
        send_copy(j).start()

    recv_ref[0] = out_ref[me]
    slots, cells, channels = out_ref.shape[1], out_ref.shape[2], out_ref.shape[3]
    rows = group * slots * cells

    @pl.loop(0, n // group)
    def _(g):
        base = g * group

        @pl.loop(0, group)
        def _(i):
            j = base + i

            @pl.when(j > 0)
            def _():
                recv_copy(j).wait_recv()

            stage_ref[i] = state_ref[lax.rem(me - j + n, n)]

        fluxes = recv_ref[pl.ds(base, group)]
        used = fluxes[:, :, 0:1, 0:1] == fluxes[:, :, 0:1, 0:1]
        states = (stage_ref[...].astype(jnp.float32) + fluxes.astype(jnp.float32)).reshape(rows, channels)
        average = jnp.mean(states, axis=-1, keepdims=True)
        centred = states - average
        spread = jnp.mean(centred * centred, axis=-1, keepdims=True)
        normed = (centred * lax.rsqrt(spread + 1e-06) * gain_ref[...]).astype(jnp.bfloat16)
        hidden = jax.nn.gelu(
            jnp.dot(normed, up_ref[...], preferred_element_type=jnp.float32), approximate=True
        ).astype(jnp.bfloat16)
        result = states + jnp.dot(hidden, down_ref[...], preferred_element_type=jnp.float32)
        result = result.reshape(group, slots, cells, channels)
        stage_ref[...] = jnp.where(used, result, 0.0).astype(jnp.bfloat16)

        @pl.loop(0, group)
        def _(i):
            res_ref[lax.rem(me - base - i + n, n)] = stage_ref[i]

    @pl.loop(1, n)
    def _(j):
        send_copy(j).wait_send()


def exchange_and_ocean(outgoing, state, gain, w_up, w_down):
    n_lon = lax.axis_size("lon")
    n = n_lon * lax.axis_size("lat")
    group = 32
    rows = outgoing.shape[0] * outgoing.shape[1] * outgoing.shape[2]
    channels, hid = w_up.shape
    vmem = pl.BlockSpec(memory_space=pltpu.VMEM)
    return pl.pallas_call(
        functools.partial(exchange_body, n_lon, n, group),
        out_shape=jax.ShapeDtypeStruct(outgoing.shape, outgoing.dtype),
        in_specs=[vmem] * 5,
        out_specs=vmem,
        scratch_shapes=[
            pltpu.VMEM(outgoing.shape, outgoing.dtype),
            pltpu.VMEM((group,) + outgoing.shape[1:], outgoing.dtype),
            pltpu.SemaphoreType.DMA((n,)),
            pltpu.SemaphoreType.DMA((n,)),
        ],
        compiler_params=pltpu.CompilerParams(
            collective_id=0, has_side_effects=True, vmem_limit_bytes=48 * 1024 * 1024
        ),
        cost_estimate=pl.CostEstimate(
            flops=4 * rows * channels * hid, transcendentals=rows * hid, bytes_accessed=4 * rows * channels * 2
        ),
    )(outgoing, state, gain.reshape(1, channels), w_up, w_down)


def atmos_body(n_lat, n_lon, kw, band, side, x_hbm, w_ref, atm_ref, gain_ref, up_hbm, down_hbm, fw_hbm,
               out_ref, flux_ref, above, below, left, right, above_left, above_right, below_left, below_right,
               xf_ref, xs_ref, mixed_ref, up_ref, down_ref, fw_ref, sems, send_sems, recv_sems):
    rows, cols, channels = atm_ref.shape
    m = kw // 2
    got = (above, below, left, right, above_left, above_right, below_left, below_right)
    lat, lon = lax.axis_index("lat"), lax.axis_index("lon")
    has_up = lat > 0
    has_down = lat < n_lat - 1
    row_part = {1: pl.ds(rows - m, m), -1: pl.ds(0, m), 0: pl.ds(0, rows)}
    col_part = {1: pl.ds(cols - side, side), -1: pl.ds(0, side), 0: pl.ds(0, cols)}

    def exists(d_lat):
        return has_down if d_lat > 0 else (has_up if d_lat < 0 else lat >= 0)

    def exists_from(d_lat):
        return has_up if d_lat > 0 else (has_down if d_lat < 0 else lat >= 0)

    def target(d_lat, d_lon):
        return (lax.rem(lon + d_lon + n_lon, n_lon), lat + d_lat)

    barrier = pltpu.get_barrier_semaphore()
    for d_lat, d_lon in HALO_MOVES:
        @pl.when(exists(d_lat))
        def _():
            pl.semaphore_signal(barrier, inc=1, device_id=target(d_lat, d_lon), device_id_type=MESH)

    pl.semaphore_wait(barrier, 2 + 3 * has_up.astype(jnp.int32) + 3 * has_down.astype(jnp.int32))

    def halo_copy(p):
        d_lat, d_lon = HALO_MOVES[p]
        return pltpu.make_async_remote_copy(
            src_ref=x_hbm.at[row_part[d_lat], col_part[d_lon]],
            dst_ref=got[p],
            send_sem=send_sems.at[p],
            recv_sem=recv_sems.at[p],
            device_id=target(d_lat, d_lon),
            device_id_type=MESH,
        )

    for p, (d_lat, d_lon) in enumerate(HALO_MOVES):
        @pl.when(exists(d_lat))
        def _():
            halo_copy(p).start()

    weights = [
        pltpu.make_async_copy(up_hbm, up_ref, sems.at[0]),
        pltpu.make_async_copy(down_hbm, down_ref, sems.at[1]),
        pltpu.make_async_copy(fw_hbm, fw_ref, sems.at[2]),
    ]
    for copy in weights:
        copy.start()

    xf_ref[m:m + rows, 0:side, :] = jnp.zeros((rows, side, channels), jnp.float32)
    xf_ref[m:m + rows, side:side + cols, :] = atm_ref[...].astype(jnp.float32)
    xf_ref[m:m + rows, side + cols:, :] = jnp.zeros((rows, side, channels), jnp.float32)

    def shift_rows(lo, hi, c0, width):
        @pl.loop(lo, hi)
        def _(i):
            for q in range(kw):
                xs_ref[q, i, pl.ds(c0, width), :] = xf_ref[i, pl.ds(side - m + q + c0, width), :]

    def conv_band(r0, c0, width):
        for cb in range(channels // 128):
            lanes = pl.ds(cb * 128, 128)
            acc = [jnp.zeros((width, 128), jnp.float32) for _ in range(band)]
            for q in range(kw):
                for i in range(band + kw - 1):
                    line = xs_ref[q, r0 + i, pl.ds(c0, width), lanes]
                    for p in range(kw):
                        r = i - p
                        if 0 <= r < band:
                            acc[r] = acc[r] + line * w_ref[p, pl.ds(q, 1), lanes]
            for r in range(band):
                mixed_ref[r0 + r, pl.ds(c0, width), lanes] = acc[r]

    shift_rows(m, m + rows, 0, cols)
    bands = rows // band

    @pl.loop(1, bands - 1)
    def _(b):
        conv_band(b * band, 0, cols)

    for p, (d_lat, d_lon) in enumerate(HALO_MOVES):
        @pl.when(exists_from(d_lat))
        def _():
            halo_copy(p).wait_recv()

        @pl.when(jnp.logical_not(exists_from(d_lat)))
        def _():
            got[p][...] = jnp.zeros(got[p].shape, got[p].dtype)

    for r0, r1, l_ref, c_ref, r_ref in (
        (0, m, above_left, above, above_right),
        (m, m + rows, left, None, right),
        (m + rows, 2 * m + rows, below_left, below, below_right),
    ):
        xf_ref[r0:r1, 0:side, :] = l_ref[...].astype(jnp.float32)
        if c_ref is not None:
            xf_ref[r0:r1, side:side + cols, :] = c_ref[...].astype(jnp.float32)
        xf_ref[r0:r1, side + cols:, :] = r_ref[...].astype(jnp.float32)

    shift_rows(0, m, 0, cols)
    shift_rows(m + rows, rows + 2 * m, 0, cols)
    shift_rows(m, m + rows, 0, 8)
    shift_rows(m, m + rows, cols - 8, 8)

    @pl.loop(0, 2)
    def _(t):
        conv_band(t * (bands - 1) * band, 0, cols)

    @pl.loop(1, bands - 1)
    def _(b):
        conv_band(b * band, 0, 8)
        conv_band(b * band, cols - 8, 8)

    for copy in weights:
        copy.wait()

    for p, (d_lat, d_lon) in enumerate(HALO_MOVES):
        @pl.when(exists(d_lat))
        def _():
            halo_copy(p).wait_send()

    chunk = 8

    @pl.loop(0, rows // chunk)
    def _(k):
        cells = chunk * cols
        mixed = mixed_ref[pl.ds(k * chunk, chunk)].reshape(cells, channels)
        average = jnp.mean(mixed, axis=-1, keepdims=True)
        centred = mixed - average
        spread = jnp.mean(centred * centred, axis=-1, keepdims=True)
        normed = (centred * lax.rsqrt(spread + 1e-06) * gain_ref[...]).astype(jnp.bfloat16)
        hidden = jax.nn.gelu(
            jnp.dot(normed, up_ref[...], preferred_element_type=jnp.float32), approximate=True
        ).astype(jnp.bfloat16)
        branch = jnp.dot(hidden, down_ref[...], preferred_element_type=jnp.float32)
        atmos = atm_ref[pl.ds(k * chunk, chunk)].reshape(cells, channels).astype(jnp.float32)
        new = (atmos + branch).astype(jnp.bfloat16)
        out_ref[pl.ds(k * chunk, chunk)] = new.reshape(chunk, cols, channels)
        flux = jnp.dot(new, fw_ref[...], preferred_element_type=jnp.float32)
        flux_ref[pl.ds(k * cells, cells)] = flux.astype(jnp.bfloat16)


def atmosphere_block(conv_weight, atmosphere, gain, w_up, w_down, flux_weight):
    rows, cols, channels = atmosphere.shape
    kw = conv_weight.shape[0]
    m = kw // 2
    side = 8
    hid = w_up.shape[1]
    vmem = pl.BlockSpec(memory_space=pltpu.VMEM)
    hbm = pl.BlockSpec(memory_space=pl.ANY)
    cells = rows * cols
    pieces = []
    for d_lat, d_lon in HALO_MOVES:
        pieces.append(pltpu.VMEM((m if d_lat else rows, side if d_lon else cols, channels), atmosphere.dtype))
    return pl.pallas_call(
        functools.partial(atmos_body, lax.axis_size("lat"), lax.axis_size("lon"), kw, 4, side),
        out_shape=(
            jax.ShapeDtypeStruct(atmosphere.shape, atmosphere.dtype),
            jax.ShapeDtypeStruct((cells, channels), jnp.bfloat16),
        ),
        in_specs=[hbm] + [vmem] * 3 + [hbm] * 3,
        out_specs=(vmem, vmem),
        scratch_shapes=pieces + [
            pltpu.VMEM((rows + kw - 1, cols + 2 * side, channels), jnp.float32),
            pltpu.VMEM((kw, rows + kw - 1, cols, channels), jnp.float32),
            pltpu.VMEM((rows, cols, channels), jnp.float32),
            pltpu.VMEM(w_up.shape, w_up.dtype),
            pltpu.VMEM(w_down.shape, w_down.dtype),
            pltpu.VMEM(flux_weight.shape, flux_weight.dtype),
            pltpu.SemaphoreType.DMA((3,)),
            pltpu.SemaphoreType.DMA((8,)),
            pltpu.SemaphoreType.DMA((8,)),
        ],
        compiler_params=pltpu.CompilerParams(
            collective_id=1, has_side_effects=True, vmem_limit_bytes=56 * 1024 * 1024
        ),
        cost_estimate=pl.CostEstimate(
            flops=2 * cells * channels * (kw * kw + 2 * hid + channels),
            transcendentals=cells * hid,
            bytes_accessed=cells * channels * 8,
        ),
    )(atmosphere, conv_weight, atmosphere, gain.reshape(1, channels), w_up, w_down, flux_weight)


def normalize(values, scales):
    average = jnp.mean(values, axis=-1, keepdims=True)
    centred = values - average
    spread = jnp.mean(centred * centred, axis=-1, keepdims=True)
    return centred * lax.rsqrt(spread + 1e-06) * scales


def channel_mixer(values, scales, w_up, w_down):
    normed = normalize(values, scales).astype(jnp.bfloat16)
    hidden = jax.nn.gelu(
        jnp.dot(normed, w_up, preferred_element_type=jnp.float32), approximate=True
    ).astype(jnp.bfloat16)
    return jnp.dot(hidden, w_down, preferred_element_type=jnp.float32)


def per_device(
    atmosphere,
    conv_weight,
    atm_gain,
    atm_up,
    atm_down,
    flux_weight,
    land_mask,
    tile_owner,
    ocean_state,
    ocn_gain,
    ocn_up,
    ocn_down,
):
    lat_rows, lon_cols, channels = atmosphere.shape
    margin = conv_weight.shape[0] // 2
    owners = tile_owner.reshape(-1)
    tile_count = owners.shape[0]
    peer_count = ocean_state.shape[1]
    capacity = ocean_state.shape[2]
    tile_cells = ocean_state.shape[3]
    atmos_new, fluxes = atmosphere_block(conv_weight, atmosphere, atm_gain, atm_up, atm_down, flux_weight)
    wet = land_mask.reshape(tile_count, tile_cells, 1).astype(jnp.bfloat16)
    flux_tiles = (fluxes.reshape(tile_count, tile_cells, channels) * wet).reshape(tile_count, tile_cells * channels)
    member = (owners[:, None] == jnp.arange(peer_count, dtype=jnp.int32)[None, :]).astype(jnp.int32)
    tile_rank = jnp.sum(jnp.cumsum(member, axis=0) * member, axis=1) - 1
    slot_index = owners * capacity + tile_rank
    onehot = (
        jnp.arange(peer_count * capacity, dtype=jnp.int32)[:, None] == slot_index[None, :]
    ).astype(jnp.bfloat16)
    outgoing = jnp.dot(onehot, flux_tiles, preferred_element_type=jnp.float32).astype(jnp.bfloat16)
    used = jnp.sum(onehot.astype(jnp.float32), axis=1) > 0
    outgoing = jnp.where(used[:, None], outgoing, jnp.nan).astype(jnp.bfloat16)
    outgoing = outgoing.reshape(peer_count, capacity, tile_cells, channels)
    ocean_out = exchange_and_ocean(outgoing, ocean_state[0], ocn_gain, ocn_up, ocn_down)[None]
    return (atmos_new, ocean_out)


def solution(mesh):
    placed = (
        P("lat", "lon", None),
        P(),
        P(),
        P(),
        P(),
        P(),
        P("lat", "lon"),
        P("lat", "lon", None),
        P(("lat", "lon"), None, None, None, None),
        P(),
        P(),
        P(),
    )
    return jax.shard_map(
        per_device,
        mesh=mesh,
        in_specs=placed,
        out_specs=(P("lat", "lon", None), P(("lat", "lon"), None, None, None, None)),
        check_vma=False,
    )
```

```python
import functools

import jax
import jax.numpy as jnp
from jax import lax
from jax.experimental import pallas as pl
from jax.experimental.pallas import tpu as pltpu
from jax.sharding import PartitionSpec as P

MESH = pl.DeviceIdType.MESH

AXES = ("lat", "lon")


HALO_MOVES = ((1, 0), (-1, 0), (0, 1), (0, -1), (1, 1), (1, -1), (-1, 1), (-1, -1))


def exchange_body(n_lon, n, group, flux_ref, wet_ref, tile_ref, used_ref, state_ref, gain_ref, up_ref, down_ref,
                  res_ref, out_ref, recv_ref, stage_ref, send_sems, recv_sems):
    me = lax.axis_index("lat") * n_lon + lax.axis_index("lon")

    def coords(d):
        return (lax.rem(d, n_lon), lax.div(d, n_lon))

    barrier = pltpu.get_barrier_semaphore()

    @pl.loop(1, n)
    def _(j):
        pl.semaphore_signal(barrier, inc=1, device_id=coords(lax.rem(me + j, n)), device_id_type=MESH)

    capacity = out_ref.shape[1]

    @pl.loop(0, n * capacity // 8)
    def _(t8):
        for u in range(8):
            t = t8 * 8 + u
            k = tile_ref[t]
            cells = (flux_ref[k].astype(jnp.float32) * wet_ref[k].astype(jnp.float32)).astype(jnp.bfloat16)
            keep = jnp.full(cells.shape, used_ref[t], jnp.int32) > 0
            out_ref[t // capacity, t % capacity] = jnp.where(keep, cells, jnp.nan).astype(jnp.bfloat16)

    pl.semaphore_wait(barrier, n - 1)

    def send_copy(j):
        peer = lax.rem(me + j, n)
        return pltpu.make_async_remote_copy(
            src_ref=out_ref.at[peer],
            dst_ref=recv_ref.at[j],
            send_sem=send_sems.at[j],
            recv_sem=recv_sems.at[j],
            device_id=coords(peer),
            device_id_type=MESH,
        )

    def recv_copy(j):
        source = lax.rem(me - j + n, n)
        return pltpu.make_async_remote_copy(
            src_ref=out_ref.at[source],
            dst_ref=recv_ref.at[j],
            send_sem=send_sems.at[j],
            recv_sem=recv_sems.at[j],
            device_id=coords(source),
            device_id_type=MESH,
        )

    @pl.loop(1, n)
    def _(j):
        send_copy(j).start()

    recv_ref[0] = out_ref[me]
    slots, cells, channels = out_ref.shape[1], out_ref.shape[2], out_ref.shape[3]
    rows = group * slots * cells

    @pl.loop(0, n // group)
    def _(g):
        base = g * group

        @pl.loop(0, group)
        def _(i):
            j = base + i

            @pl.when(j > 0)
            def _():
                recv_copy(j).wait_recv()

            stage_ref[i] = state_ref[lax.rem(me - j + n, n)]

        fluxes = recv_ref[pl.ds(base, group)]
        used = fluxes[:, :, 0:1, 0:1] == fluxes[:, :, 0:1, 0:1]
        states = (stage_ref[...].astype(jnp.float32) + fluxes.astype(jnp.float32)).reshape(rows, channels)
        average = jnp.mean(states, axis=-1, keepdims=True)
        centred = states - average
        spread = jnp.mean(centred * centred, axis=-1, keepdims=True)
        normed = (centred * lax.rsqrt(spread + 1e-06) * gain_ref[...]).astype(jnp.bfloat16)
        hidden = jax.nn.gelu(
            jnp.dot(normed, up_ref[...], preferred_element_type=jnp.float32), approximate=True
        ).astype(jnp.bfloat16)
        result = states + jnp.dot(hidden, down_ref[...], preferred_element_type=jnp.float32)
        result = result.reshape(group, slots, cells, channels)
        stage_ref[...] = jnp.where(used, result, 0.0).astype(jnp.bfloat16)

        @pl.loop(0, group)
        def _(i):
            res_ref[lax.rem(me - base - i + n, n)] = stage_ref[i]

    @pl.loop(1, n)
    def _(j):
        send_copy(j).wait_send()


def exchange_and_ocean(flux_tiles, wet, tile_of_slot, used, state, gain, w_up, w_down):
    n_lon = lax.axis_size("lon")
    n = n_lon * lax.axis_size("lat")
    group = 16
    outgoing = jax.ShapeDtypeStruct(state.shape, state.dtype)
    rows = outgoing.shape[0] * outgoing.shape[1] * outgoing.shape[2]
    channels, hid = w_up.shape
    vmem = pl.BlockSpec(memory_space=pltpu.VMEM)
    smem = pl.BlockSpec(memory_space=pltpu.SMEM)
    return pl.pallas_call(
        functools.partial(exchange_body, n_lon, n, group),
        out_shape=jax.ShapeDtypeStruct(outgoing.shape, outgoing.dtype),
        in_specs=[vmem, vmem, smem, smem] + [vmem] * 4,
        out_specs=vmem,
        scratch_shapes=[
            pltpu.VMEM(outgoing.shape, outgoing.dtype),
            pltpu.VMEM(outgoing.shape, outgoing.dtype),
            pltpu.VMEM((group,) + outgoing.shape[1:], outgoing.dtype),
            pltpu.SemaphoreType.DMA((n,)),
            pltpu.SemaphoreType.DMA((n,)),
        ],
        compiler_params=pltpu.CompilerParams(
            collective_id=0, has_side_effects=True, vmem_limit_bytes=48 * 1024 * 1024
        ),
        cost_estimate=pl.CostEstimate(
            flops=4 * rows * channels * hid, transcendentals=rows * hid, bytes_accessed=4 * rows * channels * 2
        ),
    )(flux_tiles, wet, tile_of_slot, used, state, gain.reshape(1, channels), w_up, w_down)


def atmos_body(n_lat, n_lon, kw, band, side, x_hbm, w_ref, atm_ref, gain_ref, up_hbm, down_hbm, fw_hbm,
               out_ref, flux_ref, above, below, left, right, above_left, above_right, below_left, below_right,
               xf_ref, xs_ref, mixed_ref, up_ref, down_ref, fw_ref, sems, send_sems, recv_sems):
    rows, cols, channels = atm_ref.shape
    m = kw // 2
    got = (above, below, left, right, above_left, above_right, below_left, below_right)
    lat, lon = lax.axis_index("lat"), lax.axis_index("lon")
    has_up = lat > 0
    has_down = lat < n_lat - 1
    row_part = {1: pl.ds(rows - m, m), -1: pl.ds(0, m), 0: pl.ds(0, rows)}
    col_part = {1: pl.ds(cols - side, side), -1: pl.ds(0, side), 0: pl.ds(0, cols)}

    def exists(d_lat):
        return has_down if d_lat > 0 else (has_up if d_lat < 0 else lat >= 0)

    def exists_from(d_lat):
        return has_up if d_lat > 0 else (has_down if d_lat < 0 else lat >= 0)

    def target(d_lat, d_lon):
        return (lax.rem(lon + d_lon + n_lon, n_lon), lat + d_lat)

    barrier = pltpu.get_barrier_semaphore()
    for d_lat, d_lon in HALO_MOVES:
        @pl.when(exists(d_lat))
        def _():
            pl.semaphore_signal(barrier, inc=1, device_id=target(d_lat, d_lon), device_id_type=MESH)

    pl.semaphore_wait(barrier, 2 + 3 * has_up.astype(jnp.int32) + 3 * has_down.astype(jnp.int32))

    def halo_copy(p):
        d_lat, d_lon = HALO_MOVES[p]
        return pltpu.make_async_remote_copy(
            src_ref=x_hbm.at[row_part[d_lat], col_part[d_lon]],
            dst_ref=got[p],
            send_sem=send_sems.at[p],
            recv_sem=recv_sems.at[p],
            device_id=target(d_lat, d_lon),
            device_id_type=MESH,
        )

    for p, (d_lat, d_lon) in enumerate(HALO_MOVES):
        @pl.when(exists(d_lat))
        def _():
            halo_copy(p).start()

    weights = [
        pltpu.make_async_copy(up_hbm, up_ref, sems.at[0]),
        pltpu.make_async_copy(down_hbm, down_ref, sems.at[1]),
        pltpu.make_async_copy(fw_hbm, fw_ref, sems.at[2]),
    ]
    for copy in weights:
        copy.start()

    xf_ref[m:m + rows, 0:side, :] = jnp.zeros((rows, side, channels), jnp.float32)
    xf_ref[m:m + rows, side:side + cols, :] = atm_ref[...].astype(jnp.float32)
    xf_ref[m:m + rows, side + cols:, :] = jnp.zeros((rows, side, channels), jnp.float32)

    def shift_rows(lo, hi, c0, width):
        @pl.loop(lo, hi)
        def _(i):
            for q in range(kw):
                xs_ref[q, i, pl.ds(c0, width), :] = xf_ref[i, pl.ds(side - m + q + c0, width), :]

    def conv_band(r0, c0, width):
        for cb in range(channels // 128):
            lanes = pl.ds(cb * 128, 128)
            acc = [jnp.zeros((width, 128), jnp.float32) for _ in range(band)]
            for q in range(kw):
                for i in range(band + kw - 1):
                    line = xs_ref[q, r0 + i, pl.ds(c0, width), lanes]
                    for p in range(kw):
                        r = i - p
                        if 0 <= r < band:
                            acc[r] = acc[r] + line * w_ref[p, pl.ds(q, 1), lanes]
            for r in range(band):
                mixed_ref[r0 + r, pl.ds(c0, width), lanes] = acc[r]

    shift_rows(m, m + rows, 0, cols)
    bands = rows // band

    @pl.loop(1, bands - 1)
    def _(b):
        conv_band(b * band, 0, cols)

    for p, (d_lat, d_lon) in enumerate(HALO_MOVES):
        @pl.when(exists_from(d_lat))
        def _():
            halo_copy(p).wait_recv()

        @pl.when(jnp.logical_not(exists_from(d_lat)))
        def _():
            got[p][...] = jnp.zeros(got[p].shape, got[p].dtype)

    for r0, r1, l_ref, c_ref, r_ref in (
        (0, m, above_left, above, above_right),
        (m, m + rows, left, None, right),
        (m + rows, 2 * m + rows, below_left, below, below_right),
    ):
        xf_ref[r0:r1, 0:side, :] = l_ref[...].astype(jnp.float32)
        if c_ref is not None:
            xf_ref[r0:r1, side:side + cols, :] = c_ref[...].astype(jnp.float32)
        xf_ref[r0:r1, side + cols:, :] = r_ref[...].astype(jnp.float32)

    shift_rows(0, m, 0, cols)
    shift_rows(m + rows, rows + 2 * m, 0, cols)
    shift_rows(m, m + rows, 0, 8)
    shift_rows(m, m + rows, cols - 8, 8)

    @pl.loop(0, 2)
    def _(t):
        conv_band(t * (bands - 1) * band, 0, cols)

    @pl.loop(1, bands - 1)
    def _(b):
        conv_band(b * band, 0, 8)
        conv_band(b * band, cols - 8, 8)

    for copy in weights:
        copy.wait()

    for p, (d_lat, d_lon) in enumerate(HALO_MOVES):
        @pl.when(exists(d_lat))
        def _():
            halo_copy(p).wait_send()

    chunk = 8

    @pl.loop(0, rows // chunk)
    def _(k):
        cells = chunk * cols
        mixed = mixed_ref[pl.ds(k * chunk, chunk)].reshape(cells, channels)
        average = jnp.mean(mixed, axis=-1, keepdims=True)
        centred = mixed - average
        spread = jnp.mean(centred * centred, axis=-1, keepdims=True)
        normed = (centred * lax.rsqrt(spread + 1e-06) * gain_ref[...]).astype(jnp.bfloat16)
        hidden = jax.nn.gelu(
            jnp.dot(normed, up_ref[...], preferred_element_type=jnp.float32), approximate=True
        ).astype(jnp.bfloat16)
        branch = jnp.dot(hidden, down_ref[...], preferred_element_type=jnp.float32)
        atmos = atm_ref[pl.ds(k * chunk, chunk)].reshape(cells, channels).astype(jnp.float32)
        new = (atmos + branch).astype(jnp.bfloat16)
        out_ref[pl.ds(k * chunk, chunk)] = new.reshape(chunk, cols, channels)
        flux = jnp.dot(new, fw_ref[...], preferred_element_type=jnp.float32)
        flux_ref[pl.ds(k * cells, cells)] = flux.astype(jnp.bfloat16)


def atmosphere_block(conv_weight, atmosphere, gain, w_up, w_down, flux_weight):
    rows, cols, channels = atmosphere.shape
    kw = conv_weight.shape[0]
    m = kw // 2
    side = 8
    hid = w_up.shape[1]
    vmem = pl.BlockSpec(memory_space=pltpu.VMEM)
    hbm = pl.BlockSpec(memory_space=pl.ANY)
    cells = rows * cols
    pieces = []
    for d_lat, d_lon in HALO_MOVES:
        pieces.append(pltpu.VMEM((m if d_lat else rows, side if d_lon else cols, channels), atmosphere.dtype))
    return pl.pallas_call(
        functools.partial(atmos_body, lax.axis_size("lat"), lax.axis_size("lon"), kw, 4, side),
        out_shape=(
            jax.ShapeDtypeStruct(atmosphere.shape, atmosphere.dtype),
            jax.ShapeDtypeStruct((cells, channels), jnp.bfloat16),
        ),
        in_specs=[hbm] + [vmem] * 3 + [hbm] * 3,
        out_specs=(vmem, vmem),
        scratch_shapes=pieces + [
            pltpu.VMEM((rows + kw - 1, cols + 2 * side, channels), jnp.float32),
            pltpu.VMEM((kw, rows + kw - 1, cols, channels), jnp.float32),
            pltpu.VMEM((rows, cols, channels), jnp.float32),
            pltpu.VMEM(w_up.shape, w_up.dtype),
            pltpu.VMEM(w_down.shape, w_down.dtype),
            pltpu.VMEM(flux_weight.shape, flux_weight.dtype),
            pltpu.SemaphoreType.DMA((3,)),
            pltpu.SemaphoreType.DMA((8,)),
            pltpu.SemaphoreType.DMA((8,)),
        ],
        compiler_params=pltpu.CompilerParams(
            collective_id=1, has_side_effects=True, vmem_limit_bytes=56 * 1024 * 1024
        ),
        cost_estimate=pl.CostEstimate(
            flops=2 * cells * channels * (kw * kw + 2 * hid + channels),
            transcendentals=cells * hid,
            bytes_accessed=cells * channels * 8,
        ),
    )(atmosphere, conv_weight, atmosphere, gain.reshape(1, channels), w_up, w_down, flux_weight)


def normalize(values, scales):
    average = jnp.mean(values, axis=-1, keepdims=True)
    centred = values - average
    spread = jnp.mean(centred * centred, axis=-1, keepdims=True)
    return centred * lax.rsqrt(spread + 1e-06) * scales


def channel_mixer(values, scales, w_up, w_down):
    normed = normalize(values, scales).astype(jnp.bfloat16)
    hidden = jax.nn.gelu(
        jnp.dot(normed, w_up, preferred_element_type=jnp.float32), approximate=True
    ).astype(jnp.bfloat16)
    return jnp.dot(hidden, w_down, preferred_element_type=jnp.float32)


def per_device(
    atmosphere,
    conv_weight,
    atm_gain,
    atm_up,
    atm_down,
    flux_weight,
    land_mask,
    tile_owner,
    ocean_state,
    ocn_gain,
    ocn_up,
    ocn_down,
):
    lat_rows, lon_cols, channels = atmosphere.shape
    margin = conv_weight.shape[0] // 2
    owners = tile_owner.reshape(-1)
    tile_count = owners.shape[0]
    peer_count = ocean_state.shape[1]
    capacity = ocean_state.shape[2]
    tile_cells = ocean_state.shape[3]
    atmos_new, fluxes = atmosphere_block(conv_weight, atmosphere, atm_gain, atm_up, atm_down, flux_weight)
    wet = land_mask.reshape(tile_count, tile_cells, 1).astype(jnp.bfloat16)
    flux_tiles = fluxes.reshape(tile_count, tile_cells, channels)
    order = jnp.arange(tile_count, dtype=jnp.int32)
    earlier_same = (owners[:, None] == owners[None, :]) & (order[None, :] < order[:, None])
    slot_index = owners * capacity + jnp.sum(earlier_same.astype(jnp.int32), axis=1)
    hits = jnp.arange(peer_count * capacity, dtype=jnp.int32)[:, None] == slot_index[None, :]
    used = jnp.sum(hits.astype(jnp.int32), axis=1)
    tile_of_slot = jnp.sum(jnp.where(hits, order[None, :], 0), axis=1)
    ocean_out = exchange_and_ocean(
        flux_tiles, wet, tile_of_slot, used, ocean_state[0], ocn_gain, ocn_up, ocn_down
    )[None]
    return (atmos_new, ocean_out)


def solution(mesh):
    placed = (
        P("lat", "lon", None),
        P(),
        P(),
        P(),
        P(),
        P(),
        P("lat", "lon"),
        P("lat", "lon", None),
        P(("lat", "lon"), None, None, None, None),
        P(),
        P(),
        P(),
    )
    return jax.shard_map(
        per_device,
        mesh=mesh,
        in_specs=placed,
        out_specs=(P("lat", "lon", None), P(("lat", "lon"), None, None, None, None)),
        check_vma=False,
    )
```

```python
import functools

import jax
import jax.numpy as jnp
from jax import lax
from jax.experimental import pallas as pl
from jax.experimental.pallas import tpu as pltpu
from jax.sharding import PartitionSpec as P

MESH = pl.DeviceIdType.MESH

AXES = ("lat", "lon")


HALO_MOVES = ((1, 0), (-1, 0), (0, 1), (0, -1), (1, 1), (1, -1), (-1, 1), (-1, -1))


def exchange_body(n_lon, n, group, flux_ref, wet_ref, tile_ref, used_ref, state_hbm, gain_ref, up_ref, down_ref,
                  res_ref, out_ref, recv_ref, stage_ref, send_sems, recv_sems, state_ref, state_sem):
    me = lax.axis_index("lat") * n_lon + lax.axis_index("lon")

    def coords(d):
        return (lax.rem(d, n_lon), lax.div(d, n_lon))

    barrier = pltpu.get_barrier_semaphore()

    @pl.loop(1, n)
    def _(j):
        pl.semaphore_signal(barrier, inc=1, device_id=coords(lax.rem(me + j, n)), device_id_type=MESH)

    state_copy = pltpu.make_async_copy(state_hbm, state_ref, state_sem)
    state_copy.start()

    capacity = out_ref.shape[1]

    @pl.loop(0, n * capacity // 8)
    def _(t8):
        for u in range(8):
            t = t8 * 8 + u
            k = tile_ref[t]
            cells = (flux_ref[k].astype(jnp.float32) * wet_ref[k].astype(jnp.float32)).astype(jnp.bfloat16)
            keep = jnp.full(cells.shape, used_ref[t], jnp.int32) > 0
            out_ref[t // capacity, t % capacity] = jnp.where(keep, cells, jnp.nan).astype(jnp.bfloat16)

    pl.semaphore_wait(barrier, n - 1)

    def send_copy(j):
        peer = lax.rem(me + j, n)
        return pltpu.make_async_remote_copy(
            src_ref=out_ref.at[peer],
            dst_ref=recv_ref.at[j],
            send_sem=send_sems.at[j],
            recv_sem=recv_sems.at[j],
            device_id=coords(peer),
            device_id_type=MESH,
        )

    def recv_copy(j):
        source = lax.rem(me - j + n, n)
        return pltpu.make_async_remote_copy(
            src_ref=out_ref.at[source],
            dst_ref=recv_ref.at[j],
            send_sem=send_sems.at[j],
            recv_sem=recv_sems.at[j],
            device_id=coords(source),
            device_id_type=MESH,
        )

    @pl.loop(1, n)
    def _(j):
        send_copy(j).start()

    recv_ref[0] = out_ref[me]
    state_copy.wait()
    slots, cells, channels = out_ref.shape[1], out_ref.shape[2], out_ref.shape[3]
    rows = group * slots * cells

    @pl.loop(0, n // group)
    def _(g):
        base = g * group

        @pl.loop(0, group)
        def _(i):
            j = base + i

            @pl.when(j > 0)
            def _():
                recv_copy(j).wait_recv()

            stage_ref[i] = state_ref[lax.rem(me - j + n, n)]

        fluxes = recv_ref[pl.ds(base, group)]
        used = fluxes[:, :, 0:1, 0:1] == fluxes[:, :, 0:1, 0:1]
        states = (stage_ref[...].astype(jnp.float32) + fluxes.astype(jnp.float32)).reshape(rows, channels)
        average = jnp.mean(states, axis=-1, keepdims=True)
        centred = states - average
        spread = jnp.mean(centred * centred, axis=-1, keepdims=True)
        normed = (centred * lax.rsqrt(spread + 1e-06) * gain_ref[...]).astype(jnp.bfloat16)
        hidden = jax.nn.gelu(
            jnp.dot(normed, up_ref[...], preferred_element_type=jnp.float32), approximate=True
        ).astype(jnp.bfloat16)
        result = states + jnp.dot(hidden, down_ref[...], preferred_element_type=jnp.float32)
        result = result.reshape(group, slots, cells, channels)
        stage_ref[...] = jnp.where(used, result, 0.0).astype(jnp.bfloat16)

        @pl.loop(0, group)
        def _(i):
            res_ref[lax.rem(me - base - i + n, n)] = stage_ref[i]

    @pl.loop(1, n)
    def _(j):
        send_copy(j).wait_send()


def exchange_and_ocean(flux_tiles, wet, tile_of_slot, used, state, gain, w_up, w_down):
    n_lon = lax.axis_size("lon")
    n = n_lon * lax.axis_size("lat")
    group = 16
    outgoing = jax.ShapeDtypeStruct(state.shape, state.dtype)
    rows = outgoing.shape[0] * outgoing.shape[1] * outgoing.shape[2]
    channels, hid = w_up.shape
    vmem = pl.BlockSpec(memory_space=pltpu.VMEM)
    smem = pl.BlockSpec(memory_space=pltpu.SMEM)
    return pl.pallas_call(
        functools.partial(exchange_body, n_lon, n, group),
        out_shape=jax.ShapeDtypeStruct(outgoing.shape, outgoing.dtype),
        in_specs=[vmem, vmem, smem, smem, pl.BlockSpec(memory_space=pl.ANY)] + [vmem] * 3,
        out_specs=vmem,
        scratch_shapes=[
            pltpu.VMEM(outgoing.shape, outgoing.dtype),
            pltpu.VMEM(outgoing.shape, outgoing.dtype),
            pltpu.VMEM((group,) + outgoing.shape[1:], outgoing.dtype),
            pltpu.SemaphoreType.DMA((n,)),
            pltpu.SemaphoreType.DMA((n,)),
            pltpu.VMEM(outgoing.shape, outgoing.dtype),
            pltpu.SemaphoreType.DMA(()),
        ],
        compiler_params=pltpu.CompilerParams(
            collective_id=0, has_side_effects=True, vmem_limit_bytes=48 * 1024 * 1024
        ),
        cost_estimate=pl.CostEstimate(
            flops=4 * rows * channels * hid, transcendentals=rows * hid, bytes_accessed=4 * rows * channels * 2
        ),
    )(flux_tiles, wet, tile_of_slot, used, state, gain.reshape(1, channels), w_up, w_down)


def atmos_body(n_lat, n_lon, kw, band, side, x_hbm, w_ref, atm_ref, gain_ref, up_hbm, down_hbm, fw_hbm,
               out_ref, flux_ref, above, below, left, right, above_left, above_right, below_left, below_right,
               xf_ref, xs_ref, mixed_ref, up_ref, down_ref, fw_ref, sems, send_sems, recv_sems):
    rows, cols, channels = atm_ref.shape
    m = kw // 2
    got = (above, below, left, right, above_left, above_right, below_left, below_right)
    lat, lon = lax.axis_index("lat"), lax.axis_index("lon")
    has_up = lat > 0
    has_down = lat < n_lat - 1
    row_part = {1: pl.ds(rows - m, m), -1: pl.ds(0, m), 0: pl.ds(0, rows)}
    col_part = {1: pl.ds(cols - side, side), -1: pl.ds(0, side), 0: pl.ds(0, cols)}

    def exists(d_lat):
        return has_down if d_lat > 0 else (has_up if d_lat < 0 else lat >= 0)

    def exists_from(d_lat):
        return has_up if d_lat > 0 else (has_down if d_lat < 0 else lat >= 0)

    def target(d_lat, d_lon):
        return (lax.rem(lon + d_lon + n_lon, n_lon), lat + d_lat)

    barrier = pltpu.get_barrier_semaphore()
    for d_lat, d_lon in HALO_MOVES:
        @pl.when(exists(d_lat))
        def _():
            pl.semaphore_signal(barrier, inc=1, device_id=target(d_lat, d_lon), device_id_type=MESH)

    pl.semaphore_wait(barrier, 2 + 3 * has_up.astype(jnp.int32) + 3 * has_down.astype(jnp.int32))

    def halo_copy(p):
        d_lat, d_lon = HALO_MOVES[p]
        return pltpu.make_async_remote_copy(
            src_ref=x_hbm.at[row_part[d_lat], col_part[d_lon]],
            dst_ref=got[p],
            send_sem=send_sems.at[p],
            recv_sem=recv_sems.at[p],
            device_id=target(d_lat, d_lon),
            device_id_type=MESH,
        )

    for p, (d_lat, d_lon) in enumerate(HALO_MOVES):
        @pl.when(exists(d_lat))
        def _():
            halo_copy(p).start()

    weights = [
        pltpu.make_async_copy(up_hbm, up_ref, sems.at[0]),
        pltpu.make_async_copy(down_hbm, down_ref, sems.at[1]),
        pltpu.make_async_copy(fw_hbm, fw_ref, sems.at[2]),
    ]
    for copy in weights:
        copy.start()

    xf_ref[m:m + rows, 0:side, :] = jnp.zeros((rows, side, channels), jnp.float32)
    xf_ref[m:m + rows, side:side + cols, :] = atm_ref[...].astype(jnp.float32)
    xf_ref[m:m + rows, side + cols:, :] = jnp.zeros((rows, side, channels), jnp.float32)

    def shift_rows(lo, hi, c0, width):
        @pl.loop(lo, hi)
        def _(i):
            for q in range(kw):
                xs_ref[q, i, pl.ds(c0, width), :] = xf_ref[i, pl.ds(side - m + q + c0, width), :]

    def conv_band(r0, c0, width):
        for cb in range(channels // 128):
            lanes = pl.ds(cb * 128, 128)
            acc = [jnp.zeros((width, 128), jnp.float32) for _ in range(band)]
            for q in range(kw):
                for i in range(band + kw - 1):
                    line = xs_ref[q, r0 + i, pl.ds(c0, width), lanes]
                    for p in range(kw):
                        r = i - p
                        if 0 <= r < band:
                            acc[r] = acc[r] + line * w_ref[p, pl.ds(q, 1), lanes]
            for r in range(band):
                mixed_ref[r0 + r, pl.ds(c0, width), lanes] = acc[r]

    shift_rows(m, m + rows, 0, cols)
    bands = rows // band

    @pl.loop(1, bands - 1)
    def _(b):
        conv_band(b * band, 0, cols)

    for p, (d_lat, d_lon) in enumerate(HALO_MOVES):
        @pl.when(exists_from(d_lat))
        def _():
            halo_copy(p).wait_recv()

        @pl.when(jnp.logical_not(exists_from(d_lat)))
        def _():
            got[p][...] = jnp.zeros(got[p].shape, got[p].dtype)

    for r0, r1, l_ref, c_ref, r_ref in (
        (0, m, above_left, above, above_right),
        (m, m + rows, left, None, right),
        (m + rows, 2 * m + rows, below_left, below, below_right),
    ):
        xf_ref[r0:r1, 0:side, :] = l_ref[...].astype(jnp.float32)
        if c_ref is not None:
            xf_ref[r0:r1, side:side + cols, :] = c_ref[...].astype(jnp.float32)
        xf_ref[r0:r1, side + cols:, :] = r_ref[...].astype(jnp.float32)

    shift_rows(0, m, 0, cols)
    shift_rows(m + rows, rows + 2 * m, 0, cols)
    shift_rows(m, m + rows, 0, 8)
    shift_rows(m, m + rows, cols - 8, 8)

    @pl.loop(0, 2)
    def _(t):
        conv_band(t * (bands - 1) * band, 0, cols)

    @pl.loop(1, bands - 1)
    def _(b):
        conv_band(b * band, 0, 8)
        conv_band(b * band, cols - 8, 8)

    for copy in weights:
        copy.wait()

    for p, (d_lat, d_lon) in enumerate(HALO_MOVES):
        @pl.when(exists(d_lat))
        def _():
            halo_copy(p).wait_send()

    chunk = 8

    @pl.loop(0, rows // chunk)
    def _(k):
        cells = chunk * cols
        mixed = mixed_ref[pl.ds(k * chunk, chunk)].reshape(cells, channels)
        average = jnp.mean(mixed, axis=-1, keepdims=True)
        centred = mixed - average
        spread = jnp.mean(centred * centred, axis=-1, keepdims=True)
        normed = (centred * lax.rsqrt(spread + 1e-06) * gain_ref[...]).astype(jnp.bfloat16)
        hidden = jax.nn.gelu(
            jnp.dot(normed, up_ref[...], preferred_element_type=jnp.float32), approximate=True
        ).astype(jnp.bfloat16)
        branch = jnp.dot(hidden, down_ref[...], preferred_element_type=jnp.float32)
        atmos = atm_ref[pl.ds(k * chunk, chunk)].reshape(cells, channels).astype(jnp.float32)
        new = (atmos + branch).astype(jnp.bfloat16)
        out_ref[pl.ds(k * chunk, chunk)] = new.reshape(chunk, cols, channels)
        flux = jnp.dot(new, fw_ref[...], preferred_element_type=jnp.float32)
        flux_ref[pl.ds(k * cells, cells)] = flux.astype(jnp.bfloat16)


def atmosphere_block(conv_weight, atmosphere, gain, w_up, w_down, flux_weight):
    rows, cols, channels = atmosphere.shape
    kw = conv_weight.shape[0]
    m = kw // 2
    side = 8
    hid = w_up.shape[1]
    vmem = pl.BlockSpec(memory_space=pltpu.VMEM)
    hbm = pl.BlockSpec(memory_space=pl.ANY)
    cells = rows * cols
    pieces = []
    for d_lat, d_lon in HALO_MOVES:
        pieces.append(pltpu.VMEM((m if d_lat else rows, side if d_lon else cols, channels), atmosphere.dtype))
    return pl.pallas_call(
        functools.partial(atmos_body, lax.axis_size("lat"), lax.axis_size("lon"), kw, 4, side),
        out_shape=(
            jax.ShapeDtypeStruct(atmosphere.shape, atmosphere.dtype),
            jax.ShapeDtypeStruct((cells, channels), jnp.bfloat16),
        ),
        in_specs=[hbm] + [vmem] * 3 + [hbm] * 3,
        out_specs=(vmem, vmem),
        scratch_shapes=pieces + [
            pltpu.VMEM((rows + kw - 1, cols + 2 * side, channels), jnp.float32),
            pltpu.VMEM((kw, rows + kw - 1, cols, channels), jnp.float32),
            pltpu.VMEM((rows, cols, channels), jnp.float32),
            pltpu.VMEM(w_up.shape, w_up.dtype),
            pltpu.VMEM(w_down.shape, w_down.dtype),
            pltpu.VMEM(flux_weight.shape, flux_weight.dtype),
            pltpu.SemaphoreType.DMA((3,)),
            pltpu.SemaphoreType.DMA((8,)),
            pltpu.SemaphoreType.DMA((8,)),
        ],
        compiler_params=pltpu.CompilerParams(
            collective_id=1, has_side_effects=True, vmem_limit_bytes=56 * 1024 * 1024
        ),
        cost_estimate=pl.CostEstimate(
            flops=2 * cells * channels * (kw * kw + 2 * hid + channels),
            transcendentals=cells * hid,
            bytes_accessed=cells * channels * 8,
        ),
    )(atmosphere, conv_weight, atmosphere, gain.reshape(1, channels), w_up, w_down, flux_weight)


def normalize(values, scales):
    average = jnp.mean(values, axis=-1, keepdims=True)
    centred = values - average
    spread = jnp.mean(centred * centred, axis=-1, keepdims=True)
    return centred * lax.rsqrt(spread + 1e-06) * scales


def channel_mixer(values, scales, w_up, w_down):
    normed = normalize(values, scales).astype(jnp.bfloat16)
    hidden = jax.nn.gelu(
        jnp.dot(normed, w_up, preferred_element_type=jnp.float32), approximate=True
    ).astype(jnp.bfloat16)
    return jnp.dot(hidden, w_down, preferred_element_type=jnp.float32)


def per_device(
    atmosphere,
    conv_weight,
    atm_gain,
    atm_up,
    atm_down,
    flux_weight,
    land_mask,
    tile_owner,
    ocean_state,
    ocn_gain,
    ocn_up,
    ocn_down,
):
    lat_rows, lon_cols, channels = atmosphere.shape
    margin = conv_weight.shape[0] // 2
    owners = tile_owner.reshape(-1)
    tile_count = owners.shape[0]
    peer_count = ocean_state.shape[1]
    capacity = ocean_state.shape[2]
    tile_cells = ocean_state.shape[3]
    atmos_new, fluxes = atmosphere_block(conv_weight, atmosphere, atm_gain, atm_up, atm_down, flux_weight)
    wet = land_mask.reshape(tile_count, tile_cells, 1).astype(jnp.bfloat16)
    flux_tiles = fluxes.reshape(tile_count, tile_cells, channels)
    order = jnp.arange(tile_count, dtype=jnp.int32)
    earlier_same = (owners[:, None] == owners[None, :]) & (order[None, :] < order[:, None])
    slot_index = owners * capacity + jnp.sum(earlier_same.astype(jnp.int32), axis=1)
    hits = jnp.arange(peer_count * capacity, dtype=jnp.int32)[:, None] == slot_index[None, :]
    used = jnp.sum(hits.astype(jnp.int32), axis=1)
    tile_of_slot = jnp.sum(jnp.where(hits, order[None, :], 0), axis=1)
    ocean_out = exchange_and_ocean(
        flux_tiles, wet, tile_of_slot, used, ocean_state[0], ocn_gain, ocn_up, ocn_down
    )[None]
    return (atmos_new, ocean_out)


def solution(mesh):
    placed = (
        P("lat", "lon", None),
        P(),
        P(),
        P(),
        P(),
        P(),
        P("lat", "lon"),
        P("lat", "lon", None),
        P(("lat", "lon"), None, None, None, None),
        P(),
        P(),
        P(),
    )
    return jax.shard_map(
        per_device,
        mesh=mesh,
        in_specs=placed,
        out_specs=(P("lat", "lon", None), P(("lat", "lon"), None, None, None, None)),
        check_vma=False,
    )
```

```python
import functools

import jax
import jax.numpy as jnp
from jax import lax
from jax.experimental import pallas as pl
from jax.experimental.pallas import tpu as pltpu
from jax.sharding import PartitionSpec as P

MESH = pl.DeviceIdType.MESH

AXES = ("lat", "lon")


HALO_MOVES = ((1, 0), (-1, 0), (0, 1), (0, -1), (1, 1), (1, -1), (-1, 1), (-1, -1))


def exchange_body(n_lon, n, group, flux_ref, tile_ref, used_ref, state_hbm, gain_ref, up_ref, down_ref,
                  res_ref, out_ref, recv_ref, stage_ref, send_sems, recv_sems, state_ref, state_sem):
    me = lax.axis_index("lat") * n_lon + lax.axis_index("lon")

    def coords(d):
        return (lax.rem(d, n_lon), lax.div(d, n_lon))

    barrier = pltpu.get_barrier_semaphore()

    @pl.loop(1, n)
    def _(j):
        pl.semaphore_signal(barrier, inc=1, device_id=coords(lax.rem(me + j, n)), device_id_type=MESH)

    state_copy = pltpu.make_async_copy(state_hbm, state_ref, state_sem)
    state_copy.start()

    capacity = out_ref.shape[1]

    @pl.loop(0, n * capacity // 8)
    def _(t8):
        for u in range(8):
            t = t8 * 8 + u
            k = tile_ref[t]
            cells = flux_ref[k]
            keep = jnp.full(cells.shape, used_ref[t], jnp.int32) > 0
            out_ref[t // capacity, t % capacity] = jnp.where(keep, cells, jnp.nan).astype(jnp.bfloat16)

    pl.semaphore_wait(barrier, n - 1)

    def send_copy(j):
        peer = lax.rem(me + j, n)
        return pltpu.make_async_remote_copy(
            src_ref=out_ref.at[peer],
            dst_ref=recv_ref.at[j],
            send_sem=send_sems.at[j],
            recv_sem=recv_sems.at[j],
            device_id=coords(peer),
            device_id_type=MESH,
        )

    def recv_copy(j):
        source = lax.rem(me - j + n, n)
        return pltpu.make_async_remote_copy(
            src_ref=out_ref.at[source],
            dst_ref=recv_ref.at[j],
            send_sem=send_sems.at[j],
            recv_sem=recv_sems.at[j],
            device_id=coords(source),
            device_id_type=MESH,
        )

    @pl.loop(1, n)
    def _(j):
        send_copy(j).start()

    recv_ref[0] = out_ref[me]
    state_copy.wait()
    slots, cells, channels = out_ref.shape[1], out_ref.shape[2], out_ref.shape[3]
    rows = group * slots * cells

    @pl.loop(0, n // group)
    def _(g):
        base = g * group

        @pl.loop(0, group)
        def _(i):
            j = base + i

            @pl.when(j > 0)
            def _():
                recv_copy(j).wait_recv()

            stage_ref[i] = state_ref[lax.rem(me - j + n, n)]

        fluxes = recv_ref[pl.ds(base, group)]
        used = fluxes[:, :, 0:1, 0:1] == fluxes[:, :, 0:1, 0:1]
        states = (stage_ref[...].astype(jnp.float32) + fluxes.astype(jnp.float32)).reshape(rows, channels)
        average = jnp.mean(states, axis=-1, keepdims=True)
        centred = states - average
        spread = jnp.mean(centred * centred, axis=-1, keepdims=True)
        normed = (centred * lax.rsqrt(spread + 1e-06) * gain_ref[...]).astype(jnp.bfloat16)
        hidden = jax.nn.gelu(
            jnp.dot(normed, up_ref[...], preferred_element_type=jnp.float32), approximate=True
        ).astype(jnp.bfloat16)
        result = states + jnp.dot(hidden, down_ref[...], preferred_element_type=jnp.float32)
        result = result.reshape(group, slots, cells, channels)
        stage_ref[...] = jnp.where(used, result, 0.0).astype(jnp.bfloat16)

        @pl.loop(0, group)
        def _(i):
            res_ref[lax.rem(me - base - i + n, n)] = stage_ref[i]

    @pl.loop(1, n)
    def _(j):
        send_copy(j).wait_send()


def exchange_and_ocean(flux_tiles, tile_of_slot, used, state, gain, w_up, w_down):
    n_lon = lax.axis_size("lon")
    n = n_lon * lax.axis_size("lat")
    group = 16
    outgoing = jax.ShapeDtypeStruct(state.shape, state.dtype)
    rows = outgoing.shape[0] * outgoing.shape[1] * outgoing.shape[2]
    channels, hid = w_up.shape
    vmem = pl.BlockSpec(memory_space=pltpu.VMEM)
    smem = pl.BlockSpec(memory_space=pltpu.SMEM)
    return pl.pallas_call(
        functools.partial(exchange_body, n_lon, n, group),
        out_shape=jax.ShapeDtypeStruct(outgoing.shape, outgoing.dtype),
        in_specs=[vmem, smem, smem, pl.BlockSpec(memory_space=pl.ANY)] + [vmem] * 3,
        out_specs=vmem,
        scratch_shapes=[
            pltpu.VMEM(outgoing.shape, outgoing.dtype),
            pltpu.VMEM(outgoing.shape, outgoing.dtype),
            pltpu.VMEM((group,) + outgoing.shape[1:], outgoing.dtype),
            pltpu.SemaphoreType.DMA((n,)),
            pltpu.SemaphoreType.DMA((n,)),
            pltpu.VMEM(outgoing.shape, outgoing.dtype),
            pltpu.SemaphoreType.DMA(()),
        ],
        compiler_params=pltpu.CompilerParams(
            collective_id=0, has_side_effects=True, vmem_limit_bytes=48 * 1024 * 1024
        ),
        cost_estimate=pl.CostEstimate(
            flops=4 * rows * channels * hid, transcendentals=rows * hid, bytes_accessed=4 * rows * channels * 2
        ),
    )(flux_tiles, tile_of_slot, used, state, gain.reshape(1, channels), w_up, w_down)


def atmos_body(n_lat, n_lon, kw, band, side, x_hbm, w_ref, atm_ref, gain_ref, up_hbm, down_hbm, fw_hbm, land_ref,
               out_ref, flux_ref, above, below, left, right, above_left, above_right, below_left, below_right,
               xf_ref, xs_ref, mixed_ref, up_ref, down_ref, fw_ref, sems, send_sems, recv_sems, wet_ref):
    rows, cols, channels = atm_ref.shape
    m = kw // 2
    got = (above, below, left, right, above_left, above_right, below_left, below_right)
    lat, lon = lax.axis_index("lat"), lax.axis_index("lon")
    has_up = lat > 0
    has_down = lat < n_lat - 1
    row_part = {1: pl.ds(rows - m, m), -1: pl.ds(0, m), 0: pl.ds(0, rows)}
    col_part = {1: pl.ds(cols - side, side), -1: pl.ds(0, side), 0: pl.ds(0, cols)}

    def exists(d_lat):
        return has_down if d_lat > 0 else (has_up if d_lat < 0 else lat >= 0)

    def exists_from(d_lat):
        return has_up if d_lat > 0 else (has_down if d_lat < 0 else lat >= 0)

    def target(d_lat, d_lon):
        return (lax.rem(lon + d_lon + n_lon, n_lon), lat + d_lat)

    barrier = pltpu.get_barrier_semaphore()
    for d_lat, d_lon in HALO_MOVES:
        @pl.when(exists(d_lat))
        def _():
            pl.semaphore_signal(barrier, inc=1, device_id=target(d_lat, d_lon), device_id_type=MESH)

    pl.semaphore_wait(barrier, 2 + 3 * has_up.astype(jnp.int32) + 3 * has_down.astype(jnp.int32))

    def halo_copy(p):
        d_lat, d_lon = HALO_MOVES[p]
        return pltpu.make_async_remote_copy(
            src_ref=x_hbm.at[row_part[d_lat], col_part[d_lon]],
            dst_ref=got[p],
            send_sem=send_sems.at[p],
            recv_sem=recv_sems.at[p],
            device_id=target(d_lat, d_lon),
            device_id_type=MESH,
        )

    for p, (d_lat, d_lon) in enumerate(HALO_MOVES):
        @pl.when(exists(d_lat))
        def _():
            halo_copy(p).start()

    weights = [
        pltpu.make_async_copy(up_hbm, up_ref, sems.at[0]),
        pltpu.make_async_copy(down_hbm, down_ref, sems.at[1]),
        pltpu.make_async_copy(fw_hbm, fw_ref, sems.at[2]),
    ]
    for copy in weights:
        copy.start()

    xf_ref[m:m + rows, 0:side, :] = jnp.zeros((rows, side, channels), jnp.float32)
    xf_ref[m:m + rows, side:side + cols, :] = atm_ref[...].astype(jnp.float32)
    xf_ref[m:m + rows, side + cols:, :] = jnp.zeros((rows, side, channels), jnp.float32)

    def shift_rows(lo, hi, c0, width):
        @pl.loop(lo, hi)
        def _(i):
            for q in range(kw):
                xs_ref[q, i, pl.ds(c0, width), :] = xf_ref[i, pl.ds(side - m + q + c0, width), :]

    def conv_band(r0, c0, width):
        for cb in range(channels // 128):
            lanes = pl.ds(cb * 128, 128)
            acc = [jnp.zeros((width, 128), jnp.float32) for _ in range(band)]
            for q in range(kw):
                for i in range(band + kw - 1):
                    line = xs_ref[q, r0 + i, pl.ds(c0, width), lanes]
                    for p in range(kw):
                        r = i - p
                        if 0 <= r < band:
                            acc[r] = acc[r] + line * w_ref[p, pl.ds(q, 1), lanes]
            for r in range(band):
                mixed_ref[r0 + r, pl.ds(c0, width), lanes] = acc[r]

    shift_rows(m, m + rows, 0, cols)
    bands = rows // band

    @pl.loop(1, bands - 1)
    def _(b):
        conv_band(b * band, 0, cols)

    for p, (d_lat, d_lon) in enumerate(HALO_MOVES):
        @pl.when(exists_from(d_lat))
        def _():
            halo_copy(p).wait_recv()

        @pl.when(jnp.logical_not(exists_from(d_lat)))
        def _():
            got[p][...] = jnp.zeros(got[p].shape, got[p].dtype)

    for r0, r1, l_ref, c_ref, r_ref in (
        (0, m, above_left, above, above_right),
        (m, m + rows, left, None, right),
        (m + rows, 2 * m + rows, below_left, below, below_right),
    ):
        xf_ref[r0:r1, 0:side, :] = l_ref[...].astype(jnp.float32)
        if c_ref is not None:
            xf_ref[r0:r1, side:side + cols, :] = c_ref[...].astype(jnp.float32)
        xf_ref[r0:r1, side + cols:, :] = r_ref[...].astype(jnp.float32)

    shift_rows(0, m, 0, cols)
    shift_rows(m + rows, rows + 2 * m, 0, cols)
    shift_rows(m, m + rows, 0, 8)
    shift_rows(m, m + rows, cols - 8, 8)

    @pl.loop(0, 2)
    def _(t):
        conv_band(t * (bands - 1) * band, 0, cols)

    @pl.loop(1, bands - 1)
    def _(b):
        conv_band(b * band, 0, 8)
        conv_band(b * band, cols - 8, 8)

    for copy in weights:
        copy.wait()

    for p, (d_lat, d_lon) in enumerate(HALO_MOVES):
        @pl.when(exists(d_lat))
        def _():
            halo_copy(p).wait_send()

    eye = (lax.broadcasted_iota(jnp.int32, (cols, cols), 0) == lax.broadcasted_iota(jnp.int32, (cols, cols), 1))
    land_t = lax.dot_general(
        eye.astype(jnp.bfloat16), land_ref[...].astype(jnp.bfloat16), (((1,), (1,)), ((), ())),
        preferred_element_type=jnp.float32,
    )
    for r in range(rows):
        wet_ref[r] = jnp.broadcast_to(land_t[:, r:r + 1], (cols, channels))

    chunk = 8

    @pl.loop(0, rows // chunk)
    def _(k):
        cells = chunk * cols
        mixed = mixed_ref[pl.ds(k * chunk, chunk)].reshape(cells, channels)
        average = jnp.mean(mixed, axis=-1, keepdims=True)
        centred = mixed - average
        spread = jnp.mean(centred * centred, axis=-1, keepdims=True)
        normed = (centred * lax.rsqrt(spread + 1e-06) * gain_ref[...]).astype(jnp.bfloat16)
        hidden = jax.nn.gelu(
            jnp.dot(normed, up_ref[...], preferred_element_type=jnp.float32), approximate=True
        ).astype(jnp.bfloat16)
        branch = jnp.dot(hidden, down_ref[...], preferred_element_type=jnp.float32)
        atmos = atm_ref[pl.ds(k * chunk, chunk)].reshape(cells, channels).astype(jnp.float32)
        new = (atmos + branch).astype(jnp.bfloat16)
        out_ref[pl.ds(k * chunk, chunk)] = new.reshape(chunk, cols, channels)
        flux = jnp.dot(new, fw_ref[...], preferred_element_type=jnp.float32)
        flux = flux * wet_ref[pl.ds(k * chunk, chunk)].reshape(cells, channels)
        flux_ref[pl.ds(k * cells, cells)] = flux.astype(jnp.bfloat16)


def atmosphere_block(conv_weight, atmosphere, gain, w_up, w_down, flux_weight, land_mask):
    rows, cols, channels = atmosphere.shape
    kw = conv_weight.shape[0]
    m = kw // 2
    side = 8
    hid = w_up.shape[1]
    vmem = pl.BlockSpec(memory_space=pltpu.VMEM)
    hbm = pl.BlockSpec(memory_space=pl.ANY)
    cells = rows * cols
    pieces = []
    for d_lat, d_lon in HALO_MOVES:
        pieces.append(pltpu.VMEM((m if d_lat else rows, side if d_lon else cols, channels), atmosphere.dtype))
    return pl.pallas_call(
        functools.partial(atmos_body, lax.axis_size("lat"), lax.axis_size("lon"), kw, 4, side),
        out_shape=(
            jax.ShapeDtypeStruct(atmosphere.shape, atmosphere.dtype),
            jax.ShapeDtypeStruct((cells, channels), jnp.bfloat16),
        ),
        in_specs=[hbm] + [vmem] * 3 + [hbm] * 3 + [vmem],
        out_specs=(vmem, vmem),
        scratch_shapes=pieces + [
            pltpu.VMEM((rows + kw - 1, cols + 2 * side, channels), jnp.float32),
            pltpu.VMEM((kw, rows + kw - 1, cols, channels), jnp.float32),
            pltpu.VMEM((rows, cols, channels), jnp.float32),
            pltpu.VMEM(w_up.shape, w_up.dtype),
            pltpu.VMEM(w_down.shape, w_down.dtype),
            pltpu.VMEM(flux_weight.shape, flux_weight.dtype),
            pltpu.SemaphoreType.DMA((3,)),
            pltpu.SemaphoreType.DMA((8,)),
            pltpu.SemaphoreType.DMA((8,)),
            pltpu.VMEM((rows, cols, channels), jnp.float32),
        ],
        compiler_params=pltpu.CompilerParams(
            collective_id=1, has_side_effects=True, vmem_limit_bytes=56 * 1024 * 1024
        ),
        cost_estimate=pl.CostEstimate(
            flops=2 * cells * channels * (kw * kw + 2 * hid + channels),
            transcendentals=cells * hid,
            bytes_accessed=cells * channels * 8,
        ),
    )(atmosphere, conv_weight, atmosphere, gain.reshape(1, channels), w_up, w_down, flux_weight, land_mask)


def normalize(values, scales):
    average = jnp.mean(values, axis=-1, keepdims=True)
    centred = values - average
    spread = jnp.mean(centred * centred, axis=-1, keepdims=True)
    return centred * lax.rsqrt(spread + 1e-06) * scales


def channel_mixer(values, scales, w_up, w_down):
    normed = normalize(values, scales).astype(jnp.bfloat16)
    hidden = jax.nn.gelu(
        jnp.dot(normed, w_up, preferred_element_type=jnp.float32), approximate=True
    ).astype(jnp.bfloat16)
    return jnp.dot(hidden, w_down, preferred_element_type=jnp.float32)


def per_device(
    atmosphere,
    conv_weight,
    atm_gain,
    atm_up,
    atm_down,
    flux_weight,
    land_mask,
    tile_owner,
    ocean_state,
    ocn_gain,
    ocn_up,
    ocn_down,
):
    lat_rows, lon_cols, channels = atmosphere.shape
    margin = conv_weight.shape[0] // 2
    owners = tile_owner.reshape(-1)
    tile_count = owners.shape[0]
    peer_count = ocean_state.shape[1]
    capacity = ocean_state.shape[2]
    tile_cells = ocean_state.shape[3]
    atmos_new, fluxes = atmosphere_block(
        conv_weight, atmosphere, atm_gain, atm_up, atm_down, flux_weight, land_mask
    )
    flux_tiles = fluxes.reshape(tile_count, tile_cells, channels)
    order = jnp.arange(tile_count, dtype=jnp.int32)
    earlier_same = (owners[:, None] == owners[None, :]) & (order[None, :] < order[:, None])
    slot_index = owners * capacity + jnp.sum(earlier_same.astype(jnp.int32), axis=1)
    hits = jnp.arange(peer_count * capacity, dtype=jnp.int32)[:, None] == slot_index[None, :]
    used = jnp.sum(hits.astype(jnp.int32), axis=1)
    tile_of_slot = jnp.sum(jnp.where(hits, order[None, :], 0), axis=1)
    ocean_out = exchange_and_ocean(
        flux_tiles, tile_of_slot, used, ocean_state[0], ocn_gain, ocn_up, ocn_down
    )[None]
    return (atmos_new, ocean_out)


def solution(mesh):
    placed = (
        P("lat", "lon", None),
        P(),
        P(),
        P(),
        P(),
        P(),
        P("lat", "lon"),
        P("lat", "lon", None),
        P(("lat", "lon"), None, None, None, None),
        P(),
        P(),
        P(),
    )
    return jax.shard_map(
        per_device,
        mesh=mesh,
        in_specs=placed,
        out_specs=(P("lat", "lon", None), P(("lat", "lon"), None, None, None, None)),
        check_vma=False,
    )
```

```python
import functools

import jax
import jax.numpy as jnp
from jax import lax
from jax.experimental import pallas as pl
from jax.experimental.pallas import tpu as pltpu
from jax.sharding import PartitionSpec as P

MESH = pl.DeviceIdType.MESH

AXES = ("lat", "lon")


HALO_MOVES = ((1, 0), (-1, 0), (0, 1), (0, -1), (1, 1), (1, -1), (-1, 1), (-1, -1))


def exchange_body(n_lon, n, group, flux_hbm, tile_ref, used_ref, state_hbm, gain_ref, up_ref, down_ref,
                  res_ref, out_ref, recv_ref, stage_ref, send_sems, recv_sems, state_ref, state_sem,
                  flux_ref, flux_sem):
    me = lax.axis_index("lat") * n_lon + lax.axis_index("lon")
    flux_copy = pltpu.make_async_copy(flux_hbm, flux_ref, flux_sem)
    flux_copy.start()

    def coords(d):
        return (lax.rem(d, n_lon), lax.div(d, n_lon))

    barrier = pltpu.get_barrier_semaphore()

    @pl.loop(1, n)
    def _(j):
        pl.semaphore_signal(barrier, inc=1, device_id=coords(lax.rem(me + j, n)), device_id_type=MESH)

    state_copy = pltpu.make_async_copy(state_hbm, state_ref, state_sem)
    state_copy.start()

    capacity = out_ref.shape[1]
    flux_copy.wait()

    @pl.loop(0, n * capacity // 8)
    def _(t8):
        for u in range(8):
            t = t8 * 8 + u
            k = tile_ref[t]
            cells = flux_ref[k]
            keep = jnp.full(cells.shape, used_ref[t], jnp.int32) > 0
            out_ref[t // capacity, t % capacity] = jnp.where(keep, cells, jnp.nan).astype(jnp.bfloat16)

    pl.semaphore_wait(barrier, n - 1)

    def send_copy(j):
        peer = lax.rem(me + j, n)
        return pltpu.make_async_remote_copy(
            src_ref=out_ref.at[peer],
            dst_ref=recv_ref.at[j],
            send_sem=send_sems.at[j],
            recv_sem=recv_sems.at[j],
            device_id=coords(peer),
            device_id_type=MESH,
        )

    def recv_copy(j):
        source = lax.rem(me - j + n, n)
        return pltpu.make_async_remote_copy(
            src_ref=out_ref.at[source],
            dst_ref=recv_ref.at[j],
            send_sem=send_sems.at[j],
            recv_sem=recv_sems.at[j],
            device_id=coords(source),
            device_id_type=MESH,
        )

    @pl.loop(1, n)
    def _(j):
        send_copy(j).start()

    recv_ref[0] = out_ref[me]
    state_copy.wait()
    slots, cells, channels = out_ref.shape[1], out_ref.shape[2], out_ref.shape[3]
    rows = group * slots * cells

    @pl.loop(0, n // group)
    def _(g):
        base = g * group

        @pl.loop(0, group)
        def _(i):
            j = base + i

            @pl.when(j > 0)
            def _():
                recv_copy(j).wait_recv()

            stage_ref[i] = state_ref[lax.rem(me - j + n, n)]

        fluxes = recv_ref[pl.ds(base, group)]
        used = fluxes[:, :, 0:1, 0:1] == fluxes[:, :, 0:1, 0:1]
        states = (stage_ref[...].astype(jnp.float32) + fluxes.astype(jnp.float32)).reshape(rows, channels)
        average = jnp.mean(states, axis=-1, keepdims=True)
        centred = states - average
        spread = jnp.mean(centred * centred, axis=-1, keepdims=True)
        normed = (centred * lax.rsqrt(spread + 1e-06) * gain_ref[...]).astype(jnp.bfloat16)
        hidden = jax.nn.gelu(
            jnp.dot(normed, up_ref[...], preferred_element_type=jnp.float32), approximate=True
        ).astype(jnp.bfloat16)
        result = states + jnp.dot(hidden, down_ref[...], preferred_element_type=jnp.float32)
        result = result.reshape(group, slots, cells, channels)
        stage_ref[...] = jnp.where(used, result, 0.0).astype(jnp.bfloat16)

        @pl.loop(0, group)
        def _(i):
            res_ref[lax.rem(me - base - i + n, n)] = stage_ref[i]

    @pl.loop(1, n)
    def _(j):
        send_copy(j).wait_send()


def exchange_and_ocean(flux_tiles, tile_of_slot, used, state, gain, w_up, w_down):
    n_lon = lax.axis_size("lon")
    n = n_lon * lax.axis_size("lat")
    group = 16
    outgoing = jax.ShapeDtypeStruct(state.shape, state.dtype)
    rows = outgoing.shape[0] * outgoing.shape[1] * outgoing.shape[2]
    channels, hid = w_up.shape
    vmem = pl.BlockSpec(memory_space=pltpu.VMEM)
    smem = pl.BlockSpec(memory_space=pltpu.SMEM)
    return pl.pallas_call(
        functools.partial(exchange_body, n_lon, n, group),
        out_shape=jax.ShapeDtypeStruct(outgoing.shape, outgoing.dtype),
        in_specs=[pl.BlockSpec(memory_space=pl.ANY), smem, smem, pl.BlockSpec(memory_space=pl.ANY)] + [vmem] * 3,
        out_specs=vmem,
        scratch_shapes=[
            pltpu.VMEM(outgoing.shape, outgoing.dtype),
            pltpu.VMEM(outgoing.shape, outgoing.dtype),
            pltpu.VMEM((group,) + outgoing.shape[1:], outgoing.dtype),
            pltpu.SemaphoreType.DMA((n,)),
            pltpu.SemaphoreType.DMA((n,)),
            pltpu.VMEM(outgoing.shape, outgoing.dtype),
            pltpu.SemaphoreType.DMA(()),
            pltpu.VMEM(flux_tiles.shape, flux_tiles.dtype),
            pltpu.SemaphoreType.DMA(()),
        ],
        compiler_params=pltpu.CompilerParams(
            collective_id=0, has_side_effects=True, vmem_limit_bytes=48 * 1024 * 1024
        ),
        cost_estimate=pl.CostEstimate(
            flops=4 * rows * channels * hid, transcendentals=rows * hid, bytes_accessed=4 * rows * channels * 2
        ),
    )(flux_tiles, tile_of_slot, used, state, gain.reshape(1, channels), w_up, w_down)


def atmos_body(n_lat, n_lon, kw, band, side, x_hbm, w_ref, atm_ref, gain_ref, up_hbm, down_hbm, fw_hbm, land_ref,
               out_ref, flux_ref, above, below, left, right, above_left, above_right, below_left, below_right,
               xf_ref, xs_ref, mixed_ref, up_ref, down_ref, fw_ref, sems, send_sems, recv_sems, wet_ref):
    rows, cols, channels = atm_ref.shape
    m = kw // 2
    got = (above, below, left, right, above_left, above_right, below_left, below_right)
    lat, lon = lax.axis_index("lat"), lax.axis_index("lon")
    has_up = lat > 0
    has_down = lat < n_lat - 1
    row_part = {1: pl.ds(rows - m, m), -1: pl.ds(0, m), 0: pl.ds(0, rows)}
    col_part = {1: pl.ds(cols - side, side), -1: pl.ds(0, side), 0: pl.ds(0, cols)}

    def exists(d_lat):
        return has_down if d_lat > 0 else (has_up if d_lat < 0 else lat >= 0)

    def exists_from(d_lat):
        return has_up if d_lat > 0 else (has_down if d_lat < 0 else lat >= 0)

    def target(d_lat, d_lon):
        return (lax.rem(lon + d_lon + n_lon, n_lon), lat + d_lat)

    barrier = pltpu.get_barrier_semaphore()
    for d_lat, d_lon in HALO_MOVES:
        @pl.when(exists(d_lat))
        def _():
            pl.semaphore_signal(barrier, inc=1, device_id=target(d_lat, d_lon), device_id_type=MESH)

    pl.semaphore_wait(barrier, 2 + 3 * has_up.astype(jnp.int32) + 3 * has_down.astype(jnp.int32))

    def halo_copy(p):
        d_lat, d_lon = HALO_MOVES[p]
        return pltpu.make_async_remote_copy(
            src_ref=x_hbm.at[row_part[d_lat], col_part[d_lon]],
            dst_ref=got[p],
            send_sem=send_sems.at[p],
            recv_sem=recv_sems.at[p],
            device_id=target(d_lat, d_lon),
            device_id_type=MESH,
        )

    for p, (d_lat, d_lon) in enumerate(HALO_MOVES):
        @pl.when(exists(d_lat))
        def _():
            halo_copy(p).start()

    weights = [
        pltpu.make_async_copy(up_hbm, up_ref, sems.at[0]),
        pltpu.make_async_copy(down_hbm, down_ref, sems.at[1]),
        pltpu.make_async_copy(fw_hbm, fw_ref, sems.at[2]),
    ]
    for copy in weights:
        copy.start()

    xf_ref[m:m + rows, 0:side, :] = jnp.zeros((rows, side, channels), jnp.float32)
    xf_ref[m:m + rows, side:side + cols, :] = atm_ref[...].astype(jnp.float32)
    xf_ref[m:m + rows, side + cols:, :] = jnp.zeros((rows, side, channels), jnp.float32)

    def shift_rows(lo, hi, c0, width):
        @pl.loop(lo, hi)
        def _(i):
            for q in range(kw):
                xs_ref[q, i, pl.ds(c0, width), :] = xf_ref[i, pl.ds(side - m + q + c0, width), :]

    def conv_band(r0, c0, width):
        for cb in range(channels // 128):
            lanes = pl.ds(cb * 128, 128)
            acc = [jnp.zeros((width, 128), jnp.float32) for _ in range(band)]
            for q in range(kw):
                for i in range(band + kw - 1):
                    line = xs_ref[q, r0 + i, pl.ds(c0, width), lanes]
                    for p in range(kw):
                        r = i - p
                        if 0 <= r < band:
                            acc[r] = acc[r] + line * w_ref[p, pl.ds(q, 1), lanes]
            for r in range(band):
                mixed_ref[r0 + r, pl.ds(c0, width), lanes] = acc[r]

    shift_rows(m, m + rows, 0, cols)
    bands = rows // band

    @pl.loop(1, bands - 1)
    def _(b):
        conv_band(b * band, 0, cols)

    for p, (d_lat, d_lon) in enumerate(HALO_MOVES):
        @pl.when(exists_from(d_lat))
        def _():
            halo_copy(p).wait_recv()

        @pl.when(jnp.logical_not(exists_from(d_lat)))
        def _():
            got[p][...] = jnp.zeros(got[p].shape, got[p].dtype)

    for r0, r1, l_ref, c_ref, r_ref in (
        (0, m, above_left, above, above_right),
        (m, m + rows, left, None, right),
        (m + rows, 2 * m + rows, below_left, below, below_right),
    ):
        xf_ref[r0:r1, 0:side, :] = l_ref[...].astype(jnp.float32)
        if c_ref is not None:
            xf_ref[r0:r1, side:side + cols, :] = c_ref[...].astype(jnp.float32)
        xf_ref[r0:r1, side + cols:, :] = r_ref[...].astype(jnp.float32)

    shift_rows(0, m, 0, cols)
    shift_rows(m + rows, rows + 2 * m, 0, cols)
    shift_rows(m, m + rows, 0, 8)
    shift_rows(m, m + rows, cols - 8, 8)

    @pl.loop(0, 2)
    def _(t):
        conv_band(t * (bands - 1) * band, 0, cols)

    @pl.loop(1, bands - 1)
    def _(b):
        conv_band(b * band, 0, 8)
        conv_band(b * band, cols - 8, 8)

    for copy in weights:
        copy.wait()

    for p, (d_lat, d_lon) in enumerate(HALO_MOVES):
        @pl.when(exists(d_lat))
        def _():
            halo_copy(p).wait_send()

    eye = (lax.broadcasted_iota(jnp.int32, (cols, cols), 0) == lax.broadcasted_iota(jnp.int32, (cols, cols), 1))
    land_t = lax.dot_general(
        eye.astype(jnp.bfloat16), land_ref[...].astype(jnp.bfloat16), (((1,), (1,)), ((), ())),
        preferred_element_type=jnp.float32,
    )
    for r in range(rows):
        wet_ref[r] = jnp.broadcast_to(land_t[:, r:r + 1], (cols, channels))

    chunk = 8

    @pl.loop(0, rows // chunk)
    def _(k):
        cells = chunk * cols
        mixed = mixed_ref[pl.ds(k * chunk, chunk)].reshape(cells, channels)
        average = jnp.mean(mixed, axis=-1, keepdims=True)
        centred = mixed - average
        spread = jnp.mean(centred * centred, axis=-1, keepdims=True)
        normed = (centred * lax.rsqrt(spread + 1e-06) * gain_ref[...]).astype(jnp.bfloat16)
        hidden = jax.nn.gelu(
            jnp.dot(normed, up_ref[...], preferred_element_type=jnp.float32), approximate=True
        ).astype(jnp.bfloat16)
        branch = jnp.dot(hidden, down_ref[...], preferred_element_type=jnp.float32)
        atmos = atm_ref[pl.ds(k * chunk, chunk)].reshape(cells, channels).astype(jnp.float32)
        new = (atmos + branch).astype(jnp.bfloat16)
        out_ref[pl.ds(k * chunk, chunk)] = new.reshape(chunk, cols, channels)
        flux = jnp.dot(new, fw_ref[...], preferred_element_type=jnp.float32)
        flux = flux * wet_ref[pl.ds(k * chunk, chunk)].reshape(cells, channels)
        flux_ref[pl.ds(k * cells, cells)] = flux.astype(jnp.bfloat16)


def atmosphere_block(conv_weight, atmosphere, gain, w_up, w_down, flux_weight, land_mask):
    rows, cols, channels = atmosphere.shape
    kw = conv_weight.shape[0]
    m = kw // 2
    side = 8
    hid = w_up.shape[1]
    vmem = pl.BlockSpec(memory_space=pltpu.VMEM)
    hbm = pl.BlockSpec(memory_space=pl.ANY)
    cells = rows * cols
    pieces = []
    for d_lat, d_lon in HALO_MOVES:
        pieces.append(pltpu.VMEM((m if d_lat else rows, side if d_lon else cols, channels), atmosphere.dtype))
    return pl.pallas_call(
        functools.partial(atmos_body, lax.axis_size("lat"), lax.axis_size("lon"), kw, 4, side),
        out_shape=(
            jax.ShapeDtypeStruct(atmosphere.shape, atmosphere.dtype),
            jax.ShapeDtypeStruct((cells, channels), jnp.bfloat16),
        ),
        in_specs=[hbm] + [vmem] * 3 + [hbm] * 3 + [vmem],
        out_specs=(vmem, vmem),
        scratch_shapes=pieces + [
            pltpu.VMEM((rows + kw - 1, cols + 2 * side, channels), jnp.float32),
            pltpu.VMEM((kw, rows + kw - 1, cols, channels), jnp.float32),
            pltpu.VMEM((rows, cols, channels), jnp.float32),
            pltpu.VMEM(w_up.shape, w_up.dtype),
            pltpu.VMEM(w_down.shape, w_down.dtype),
            pltpu.VMEM(flux_weight.shape, flux_weight.dtype),
            pltpu.SemaphoreType.DMA((3,)),
            pltpu.SemaphoreType.DMA((8,)),
            pltpu.SemaphoreType.DMA((8,)),
            pltpu.VMEM((rows, cols, channels), jnp.float32),
        ],
        compiler_params=pltpu.CompilerParams(
            collective_id=1, has_side_effects=True, vmem_limit_bytes=56 * 1024 * 1024
        ),
        cost_estimate=pl.CostEstimate(
            flops=2 * cells * channels * (kw * kw + 2 * hid + channels),
            transcendentals=cells * hid,
            bytes_accessed=cells * channels * 8,
        ),
    )(atmosphere, conv_weight, atmosphere, gain.reshape(1, channels), w_up, w_down, flux_weight, land_mask)


def normalize(values, scales):
    average = jnp.mean(values, axis=-1, keepdims=True)
    centred = values - average
    spread = jnp.mean(centred * centred, axis=-1, keepdims=True)
    return centred * lax.rsqrt(spread + 1e-06) * scales


def channel_mixer(values, scales, w_up, w_down):
    normed = normalize(values, scales).astype(jnp.bfloat16)
    hidden = jax.nn.gelu(
        jnp.dot(normed, w_up, preferred_element_type=jnp.float32), approximate=True
    ).astype(jnp.bfloat16)
    return jnp.dot(hidden, w_down, preferred_element_type=jnp.float32)


def per_device(
    atmosphere,
    conv_weight,
    atm_gain,
    atm_up,
    atm_down,
    flux_weight,
    land_mask,
    tile_owner,
    ocean_state,
    ocn_gain,
    ocn_up,
    ocn_down,
):
    lat_rows, lon_cols, channels = atmosphere.shape
    margin = conv_weight.shape[0] // 2
    owners = tile_owner.reshape(-1)
    tile_count = owners.shape[0]
    peer_count = ocean_state.shape[1]
    capacity = ocean_state.shape[2]
    tile_cells = ocean_state.shape[3]
    atmos_new, fluxes = atmosphere_block(
        conv_weight, atmosphere, atm_gain, atm_up, atm_down, flux_weight, land_mask
    )
    flux_tiles = fluxes.reshape(tile_count, tile_cells, channels)
    order = jnp.arange(tile_count, dtype=jnp.int32)
    earlier_same = (owners[:, None] == owners[None, :]) & (order[None, :] < order[:, None])
    slot_index = owners * capacity + jnp.sum(earlier_same.astype(jnp.int32), axis=1)
    hits = jnp.arange(peer_count * capacity, dtype=jnp.int32)[:, None] == slot_index[None, :]
    used = jnp.sum(hits.astype(jnp.int32), axis=1)
    tile_of_slot = jnp.sum(jnp.where(hits, order[None, :], 0), axis=1)
    ocean_out = exchange_and_ocean(
        flux_tiles, tile_of_slot, used, ocean_state[0], ocn_gain, ocn_up, ocn_down
    )[None]
    return (atmos_new, ocean_out)


def solution(mesh):
    placed = (
        P("lat", "lon", None),
        P(),
        P(),
        P(),
        P(),
        P(),
        P("lat", "lon"),
        P("lat", "lon", None),
        P(("lat", "lon"), None, None, None, None),
        P(),
        P(),
        P(),
    )
    return jax.shard_map(
        per_device,
        mesh=mesh,
        in_specs=placed,
        out_specs=(P("lat", "lon", None), P(("lat", "lon"), None, None, None, None)),
        check_vma=False,
    )
```

```python
import functools

import jax
import jax.numpy as jnp
from jax import lax
from jax.experimental import pallas as pl
from jax.experimental.pallas import tpu as pltpu
from jax.sharding import PartitionSpec as P

MESH = pl.DeviceIdType.MESH

AXES = ("lat", "lon")


HALO_MOVES = ((1, 0), (-1, 0), (0, 1), (0, -1), (1, 1), (1, -1), (-1, 1), (-1, -1))


def exchange_body(n_lon, n, group, flux_ref, tile_ref, used_ref, state_hbm, gain_ref, up_ref, down_ref,
                  res_ref, out_ref, recv_ref, stage_ref, send_sems, recv_sems, state_ref, state_sem):
    me = lax.axis_index("lat") * n_lon + lax.axis_index("lon")

    def coords(d):
        return (lax.rem(d, n_lon), lax.div(d, n_lon))

    barrier = pltpu.get_barrier_semaphore()

    @pl.loop(1, n)
    def _(j):
        pl.semaphore_signal(barrier, inc=1, device_id=coords(lax.rem(me + j, n)), device_id_type=MESH)

    state_copy = pltpu.make_async_copy(state_hbm, state_ref, state_sem)
    state_copy.start()

    capacity = out_ref.shape[1]

    @pl.loop(0, n * capacity // 8)
    def _(t8):
        for u in range(8):
            t = t8 * 8 + u
            k = tile_ref[t]
            cells = flux_ref[k]
            keep = jnp.full(cells.shape, used_ref[t], jnp.int32) > 0
            out_ref[t // capacity, t % capacity] = jnp.where(keep, cells, jnp.nan).astype(jnp.bfloat16)

    pl.semaphore_wait(barrier, n - 1)

    def send_copy(j):
        peer = lax.rem(me + j, n)
        return pltpu.make_async_remote_copy(
            src_ref=out_ref.at[peer],
            dst_ref=recv_ref.at[j],
            send_sem=send_sems.at[j],
            recv_sem=recv_sems.at[j],
            device_id=coords(peer),
            device_id_type=MESH,
        )

    def recv_copy(j):
        source = lax.rem(me - j + n, n)
        return pltpu.make_async_remote_copy(
            src_ref=out_ref.at[source],
            dst_ref=recv_ref.at[j],
            send_sem=send_sems.at[j],
            recv_sem=recv_sems.at[j],
            device_id=coords(source),
            device_id_type=MESH,
        )

    @pl.loop(1, n)
    def _(j):
        send_copy(j).start()

    recv_ref[0] = out_ref[me]
    state_copy.wait()
    slots, cells, channels = out_ref.shape[1], out_ref.shape[2], out_ref.shape[3]
    rows = group * slots * cells

    @pl.loop(0, n // group)
    def _(g):
        base = g * group

        @pl.loop(0, group)
        def _(i):
            j = base + i

            @pl.when(j > 0)
            def _():
                recv_copy(j).wait_recv()

            stage_ref[i] = state_ref[lax.rem(me - j + n, n)]

        fluxes = recv_ref[pl.ds(base, group)]
        used = fluxes[:, :, 0:1, 0:1] == fluxes[:, :, 0:1, 0:1]
        states = (stage_ref[...].astype(jnp.float32) + fluxes.astype(jnp.float32)).reshape(rows, channels)
        average = jnp.mean(states, axis=-1, keepdims=True)
        centred = states - average
        spread = jnp.mean(centred * centred, axis=-1, keepdims=True)
        normed = (centred * lax.rsqrt(spread + 1e-06) * gain_ref[...]).astype(jnp.bfloat16)
        hidden = jax.nn.gelu(
            jnp.dot(normed, up_ref[...], preferred_element_type=jnp.float32), approximate=True
        ).astype(jnp.bfloat16)
        result = states + jnp.dot(hidden, down_ref[...], preferred_element_type=jnp.float32)
        result = result.reshape(group, slots, cells, channels)
        stage_ref[...] = jnp.where(used, result, 0.0).astype(jnp.bfloat16)

        @pl.loop(0, group)
        def _(i):
            res_ref[lax.rem(me - base - i + n, n)] = stage_ref[i]

    @pl.loop(1, n)
    def _(j):
        send_copy(j).wait_send()


def exchange_and_ocean(flux_tiles, tile_of_slot, used, state, gain, w_up, w_down):
    n_lon = lax.axis_size("lon")
    n = n_lon * lax.axis_size("lat")
    group = 16
    outgoing = jax.ShapeDtypeStruct(state.shape, state.dtype)
    rows = outgoing.shape[0] * outgoing.shape[1] * outgoing.shape[2]
    channels, hid = w_up.shape
    vmem = pl.BlockSpec(memory_space=pltpu.VMEM)
    smem = pl.BlockSpec(memory_space=pltpu.SMEM)
    return pl.pallas_call(
        functools.partial(exchange_body, n_lon, n, group),
        out_shape=jax.ShapeDtypeStruct(outgoing.shape, outgoing.dtype),
        in_specs=[vmem, smem, smem, pl.BlockSpec(memory_space=pl.ANY)] + [vmem] * 3,
        out_specs=vmem,
        scratch_shapes=[
            pltpu.VMEM(outgoing.shape, outgoing.dtype),
            pltpu.VMEM(outgoing.shape, outgoing.dtype),
            pltpu.VMEM((group,) + outgoing.shape[1:], outgoing.dtype),
            pltpu.SemaphoreType.DMA((n,)),
            pltpu.SemaphoreType.DMA((n,)),
            pltpu.VMEM(outgoing.shape, outgoing.dtype),
            pltpu.SemaphoreType.DMA(()),
        ],
        compiler_params=pltpu.CompilerParams(
            collective_id=0, has_side_effects=True, vmem_limit_bytes=48 * 1024 * 1024
        ),
        cost_estimate=pl.CostEstimate(
            flops=4 * rows * channels * hid, transcendentals=rows * hid, bytes_accessed=4 * rows * channels * 2
        ),
    )(flux_tiles, tile_of_slot, used, state, gain.reshape(1, channels), w_up, w_down)


def atmos_body(n_lat, n_lon, kw, band, side, x_hbm, w_ref, atm_ref, gain_ref, up_hbm, down_hbm, fw_hbm, land_ref,
               out_ref, flux_ref, above, below, left, right, above_left, above_right, below_left, below_right,
               xf_ref, xs_ref, mixed_ref, up_ref, down_ref, fw_ref, sems, send_sems, recv_sems, wet_ref):
    rows, cols, channels = atm_ref.shape
    m = kw // 2
    got = (above, below, left, right, above_left, above_right, below_left, below_right)
    lat, lon = lax.axis_index("lat"), lax.axis_index("lon")
    has_up = lat > 0
    has_down = lat < n_lat - 1
    row_part = {1: pl.ds(rows - m, m), -1: pl.ds(0, m), 0: pl.ds(0, rows)}
    col_part = {1: pl.ds(cols - side, side), -1: pl.ds(0, side), 0: pl.ds(0, cols)}

    def exists(d_lat):
        return has_down if d_lat > 0 else (has_up if d_lat < 0 else lat >= 0)

    def exists_from(d_lat):
        return has_up if d_lat > 0 else (has_down if d_lat < 0 else lat >= 0)

    def target(d_lat, d_lon):
        return (lax.rem(lon + d_lon + n_lon, n_lon), lat + d_lat)

    barrier = pltpu.get_barrier_semaphore()
    for d_lat, d_lon in HALO_MOVES:
        @pl.when(exists(d_lat))
        def _():
            pl.semaphore_signal(barrier, inc=1, device_id=target(d_lat, d_lon), device_id_type=MESH)

    pl.semaphore_wait(barrier, 2 + 3 * has_up.astype(jnp.int32) + 3 * has_down.astype(jnp.int32))

    def halo_copy(p):
        d_lat, d_lon = HALO_MOVES[p]
        return pltpu.make_async_remote_copy(
            src_ref=x_hbm.at[row_part[d_lat], col_part[d_lon]],
            dst_ref=got[p],
            send_sem=send_sems.at[p],
            recv_sem=recv_sems.at[p],
            device_id=target(d_lat, d_lon),
            device_id_type=MESH,
        )

    for p, (d_lat, d_lon) in enumerate(HALO_MOVES):
        @pl.when(exists(d_lat))
        def _():
            halo_copy(p).start()

    weights = [
        pltpu.make_async_copy(up_hbm, up_ref, sems.at[0]),
        pltpu.make_async_copy(down_hbm, down_ref, sems.at[1]),
        pltpu.make_async_copy(fw_hbm, fw_ref, sems.at[2]),
    ]
    for copy in weights:
        copy.start()

    xf_ref[m:m + rows, 0:side, :] = jnp.zeros((rows, side, channels), jnp.float32)
    xf_ref[m:m + rows, side:side + cols, :] = atm_ref[...].astype(jnp.float32)
    xf_ref[m:m + rows, side + cols:, :] = jnp.zeros((rows, side, channels), jnp.float32)

    def shift_rows(lo, hi, c0, width):
        @pl.loop(lo, hi)
        def _(i):
            for q in range(kw):
                xs_ref[q, i, pl.ds(c0, width), :] = xf_ref[i, pl.ds(side - m + q + c0, width), :]

    def conv_band(r0, c0, width):
        for cb in range(channels // 128):
            lanes = pl.ds(cb * 128, 128)
            acc = [jnp.zeros((width, 128), jnp.float32) for _ in range(band)]
            for q in range(kw):
                for i in range(band + kw - 1):
                    line = xs_ref[q, r0 + i, pl.ds(c0, width), lanes]
                    for p in range(kw):
                        r = i - p
                        if 0 <= r < band:
                            acc[r] = acc[r] + line * w_ref[p, pl.ds(q, 1), lanes]
            for r in range(band):
                mixed_ref[r0 + r, pl.ds(c0, width), lanes] = acc[r]

    shift_rows(m, m + rows, 0, cols)
    bands = rows // band

    @pl.loop(1, bands - 1)
    def _(b):
        conv_band(b * band, 0, cols)

    for p, (d_lat, d_lon) in enumerate(HALO_MOVES):
        @pl.when(exists_from(d_lat))
        def _():
            halo_copy(p).wait_recv()

        @pl.when(jnp.logical_not(exists_from(d_lat)))
        def _():
            got[p][...] = jnp.zeros(got[p].shape, got[p].dtype)

    for r0, r1, l_ref, c_ref, r_ref in (
        (0, m, above_left, above, above_right),
        (m, m + rows, left, None, right),
        (m + rows, 2 * m + rows, below_left, below, below_right),
    ):
        xf_ref[r0:r1, 0:side, :] = l_ref[...].astype(jnp.float32)
        if c_ref is not None:
            xf_ref[r0:r1, side:side + cols, :] = c_ref[...].astype(jnp.float32)
        xf_ref[r0:r1, side + cols:, :] = r_ref[...].astype(jnp.float32)

    shift_rows(0, m, 0, cols)
    shift_rows(m + rows, rows + 2 * m, 0, cols)
    shift_rows(m, m + rows, 0, 8)
    shift_rows(m, m + rows, cols - 8, 8)

    @pl.loop(0, 2)
    def _(t):
        conv_band(t * (bands - 1) * band, 0, cols)

    @pl.loop(1, bands - 1)
    def _(b):
        conv_band(b * band, 0, 8)
        conv_band(b * band, cols - 8, 8)

    for copy in weights:
        copy.wait()

    for p, (d_lat, d_lon) in enumerate(HALO_MOVES):
        @pl.when(exists(d_lat))
        def _():
            halo_copy(p).wait_send()

    eye = (lax.broadcasted_iota(jnp.int32, (cols, cols), 0) == lax.broadcasted_iota(jnp.int32, (cols, cols), 1))
    land_t = lax.dot_general(
        eye.astype(jnp.bfloat16), land_ref[...].astype(jnp.bfloat16), (((1,), (1,)), ((), ())),
        preferred_element_type=jnp.float32,
    )
    for r in range(rows):
        wet_ref[r] = jnp.broadcast_to(land_t[:, r:r + 1], (cols, channels))

    chunk = 8

    @pl.loop(0, rows // chunk)
    def _(k):
        cells = chunk * cols
        mixed = mixed_ref[pl.ds(k * chunk, chunk)].reshape(cells, channels)
        average = jnp.mean(mixed, axis=-1, keepdims=True)
        centred = mixed - average
        spread = jnp.mean(centred * centred, axis=-1, keepdims=True)
        normed = (centred * lax.rsqrt(spread + 1e-06) * gain_ref[...]).astype(jnp.bfloat16)
        hidden = jax.nn.gelu(
            jnp.dot(normed, up_ref[...], preferred_element_type=jnp.float32), approximate=True
        ).astype(jnp.bfloat16)
        branch = jnp.dot(hidden, down_ref[...], preferred_element_type=jnp.float32)
        atmos = atm_ref[pl.ds(k * chunk, chunk)].reshape(cells, channels).astype(jnp.float32)
        new = (atmos + branch).astype(jnp.bfloat16)
        out_ref[pl.ds(k * chunk, chunk)] = new.reshape(chunk, cols, channels)
        flux = jnp.dot(new, fw_ref[...], preferred_element_type=jnp.float32)
        flux = flux * wet_ref[pl.ds(k * chunk, chunk)].reshape(cells, channels)
        flux_ref[pl.ds(k * cells, cells)] = flux.astype(jnp.bfloat16)


def atmosphere_block(conv_weight, atmosphere, gain, w_up, w_down, flux_weight, land_mask):
    rows, cols, channels = atmosphere.shape
    kw = conv_weight.shape[0]
    m = kw // 2
    side = 8
    hid = w_up.shape[1]
    vmem = pl.BlockSpec(memory_space=pltpu.VMEM)
    hbm = pl.BlockSpec(memory_space=pl.ANY)
    cells = rows * cols
    pieces = []
    for d_lat, d_lon in HALO_MOVES:
        pieces.append(pltpu.VMEM((m if d_lat else rows, side if d_lon else cols, channels), atmosphere.dtype))
    return pl.pallas_call(
        functools.partial(atmos_body, lax.axis_size("lat"), lax.axis_size("lon"), kw, 4, side),
        out_shape=(
            jax.ShapeDtypeStruct(atmosphere.shape, atmosphere.dtype),
            jax.ShapeDtypeStruct((cells, channels), jnp.bfloat16),
        ),
        in_specs=[hbm] + [vmem] * 3 + [hbm] * 3 + [vmem],
        out_specs=(vmem, vmem),
        scratch_shapes=pieces + [
            pltpu.VMEM((rows + kw - 1, cols + 2 * side, channels), jnp.float32),
            pltpu.VMEM((kw, rows + kw - 1, cols, channels), jnp.float32),
            pltpu.VMEM((rows, cols, channels), jnp.float32),
            pltpu.VMEM(w_up.shape, w_up.dtype),
            pltpu.VMEM(w_down.shape, w_down.dtype),
            pltpu.VMEM(flux_weight.shape, flux_weight.dtype),
            pltpu.SemaphoreType.DMA((3,)),
            pltpu.SemaphoreType.DMA((8,)),
            pltpu.SemaphoreType.DMA((8,)),
            pltpu.VMEM((rows, cols, channels), jnp.float32),
        ],
        compiler_params=pltpu.CompilerParams(
            collective_id=1, has_side_effects=True, vmem_limit_bytes=56 * 1024 * 1024
        ),
        cost_estimate=pl.CostEstimate(
            flops=2 * cells * channels * (kw * kw + 2 * hid + channels),
            transcendentals=cells * hid,
            bytes_accessed=cells * channels * 8,
        ),
    )(atmosphere, conv_weight, atmosphere, gain.reshape(1, channels), w_up, w_down, flux_weight, land_mask)


def normalize(values, scales):
    average = jnp.mean(values, axis=-1, keepdims=True)
    centred = values - average
    spread = jnp.mean(centred * centred, axis=-1, keepdims=True)
    return centred * lax.rsqrt(spread + 1e-06) * scales


def channel_mixer(values, scales, w_up, w_down):
    normed = normalize(values, scales).astype(jnp.bfloat16)
    hidden = jax.nn.gelu(
        jnp.dot(normed, w_up, preferred_element_type=jnp.float32), approximate=True
    ).astype(jnp.bfloat16)
    return jnp.dot(hidden, w_down, preferred_element_type=jnp.float32)


def per_device(
    atmosphere,
    conv_weight,
    atm_gain,
    atm_up,
    atm_down,
    flux_weight,
    land_mask,
    tile_owner,
    ocean_state,
    ocn_gain,
    ocn_up,
    ocn_down,
):
    lat_rows, lon_cols, channels = atmosphere.shape
    margin = conv_weight.shape[0] // 2
    owners = tile_owner.reshape(-1)
    tile_count = owners.shape[0]
    peer_count = ocean_state.shape[1]
    capacity = ocean_state.shape[2]
    tile_cells = ocean_state.shape[3]
    atmos_new, fluxes = atmosphere_block(
        conv_weight, atmosphere, atm_gain, atm_up, atm_down, flux_weight, land_mask
    )
    flux_tiles = fluxes.reshape(tile_count, tile_cells, channels)
    order = jnp.arange(tile_count, dtype=jnp.int32)
    assert capacity == 2
    mine = jnp.arange(peer_count, dtype=jnp.int32)[:, None] == owners[None, :]
    count = jnp.sum(mine.astype(jnp.int32), axis=1)
    first = jnp.min(jnp.where(mine, order[None, :], tile_count), axis=1)
    last = jnp.max(jnp.where(mine, order[None, :], -1), axis=1)
    used = jnp.stack([(count >= 1).astype(jnp.int32), (count >= 2).astype(jnp.int32)], axis=1).reshape(-1)
    tile_of_slot = jnp.stack(
        [jnp.where(count >= 1, first, 0), jnp.where(count >= 2, last, 0)], axis=1
    ).reshape(-1)
    ocean_out = exchange_and_ocean(
        flux_tiles, tile_of_slot, used, ocean_state[0], ocn_gain, ocn_up, ocn_down
    )[None]
    return (atmos_new, ocean_out)


def solution(mesh):
    placed = (
        P("lat", "lon", None),
        P(),
        P(),
        P(),
        P(),
        P(),
        P("lat", "lon"),
        P("lat", "lon", None),
        P(("lat", "lon"), None, None, None, None),
        P(),
        P(),
        P(),
    )
    return jax.shard_map(
        per_device,
        mesh=mesh,
        in_specs=placed,
        out_specs=(P("lat", "lon", None), P(("lat", "lon"), None, None, None, None)),
        check_vma=False,
    )
```

```python
import functools

import jax
import jax.numpy as jnp
from jax import lax
from jax.experimental import pallas as pl
from jax.experimental.pallas import tpu as pltpu
from jax.sharding import PartitionSpec as P

MESH = pl.DeviceIdType.MESH

AXES = ("lat", "lon")


HALO_MOVES = ((1, 0), (-1, 0), (0, 1), (0, -1), (1, 1), (1, -1), (-1, 1), (-1, -1))


def exchange_body(n_lon, n, group, flux_ref, tile_ref, used_ref, state_hbm, gain_ref, up_ref, down_ref,
                  res_ref, out_ref, recv_ref, stage_ref, send_sems, recv_sems, state_ref, state_sem):
    me = lax.axis_index("lat") * n_lon + lax.axis_index("lon")

    def coords(d):
        return (lax.rem(d, n_lon), lax.div(d, n_lon))

    barrier = pltpu.get_barrier_semaphore()

    @pl.loop(1, n)
    def _(j):
        pl.semaphore_signal(barrier, inc=1, device_id=coords(lax.rem(me + j, n)), device_id_type=MESH)

    state_copy = pltpu.make_async_copy(state_hbm, state_ref, state_sem)
    state_copy.start()

    capacity = out_ref.shape[1]

    @pl.loop(0, n * capacity // 16)
    def _(t8):
        for u in range(16):
            t = t8 * 16 + u
            k = tile_ref[t]
            cells = flux_ref[k]
            keep = jnp.full(cells.shape, used_ref[t], jnp.int32) > 0
            out_ref[t // capacity, t % capacity] = jnp.where(keep, cells, jnp.nan).astype(jnp.bfloat16)

    pl.semaphore_wait(barrier, n - 1)

    def send_copy(j):
        peer = lax.rem(me + j, n)
        return pltpu.make_async_remote_copy(
            src_ref=out_ref.at[peer],
            dst_ref=recv_ref.at[j],
            send_sem=send_sems.at[j],
            recv_sem=recv_sems.at[j],
            device_id=coords(peer),
            device_id_type=MESH,
        )

    def recv_copy(j):
        source = lax.rem(me - j + n, n)
        return pltpu.make_async_remote_copy(
            src_ref=out_ref.at[source],
            dst_ref=recv_ref.at[j],
            send_sem=send_sems.at[j],
            recv_sem=recv_sems.at[j],
            device_id=coords(source),
            device_id_type=MESH,
        )

    @pl.loop(1, n)
    def _(j):
        send_copy(j).start()

    recv_ref[0] = out_ref[me]
    state_copy.wait()
    slots, cells, channels = out_ref.shape[1], out_ref.shape[2], out_ref.shape[3]
    rows = group * slots * cells

    @pl.loop(0, n // group)
    def _(g):
        base = g * group

        @pl.loop(0, group)
        def _(i):
            j = base + i

            @pl.when(j > 0)
            def _():
                recv_copy(j).wait_recv()

            stage_ref[i] = state_ref[lax.rem(me - j + n, n)]

        fluxes = recv_ref[pl.ds(base, group)]
        used = fluxes[:, :, 0:1, 0:1] == fluxes[:, :, 0:1, 0:1]
        states = (stage_ref[...].astype(jnp.float32) + fluxes.astype(jnp.float32)).reshape(rows, channels)
        average = jnp.mean(states, axis=-1, keepdims=True)
        centred = states - average
        spread = jnp.mean(centred * centred, axis=-1, keepdims=True)
        normed = (centred * lax.rsqrt(spread + 1e-06) * gain_ref[...]).astype(jnp.bfloat16)
        hidden = jax.nn.gelu(
            jnp.dot(normed, up_ref[...], preferred_element_type=jnp.float32), approximate=True
        ).astype(jnp.bfloat16)
        result = states + jnp.dot(hidden, down_ref[...], preferred_element_type=jnp.float32)
        result = result.reshape(group, slots, cells, channels)
        stage_ref[...] = jnp.where(used, result, 0.0).astype(jnp.bfloat16)

        @pl.loop(0, group)
        def _(i):
            res_ref[lax.rem(me - base - i + n, n)] = stage_ref[i]

    @pl.loop(1, n)
    def _(j):
        send_copy(j).wait_send()


def exchange_and_ocean(flux_tiles, tile_of_slot, used, state, gain, w_up, w_down):
    n_lon = lax.axis_size("lon")
    n = n_lon * lax.axis_size("lat")
    group = 16
    outgoing = jax.ShapeDtypeStruct(state.shape, state.dtype)
    rows = outgoing.shape[0] * outgoing.shape[1] * outgoing.shape[2]
    channels, hid = w_up.shape
    vmem = pl.BlockSpec(memory_space=pltpu.VMEM)
    smem = pl.BlockSpec(memory_space=pltpu.SMEM)
    return pl.pallas_call(
        functools.partial(exchange_body, n_lon, n, group),
        out_shape=jax.ShapeDtypeStruct(outgoing.shape, outgoing.dtype),
        in_specs=[vmem, smem, smem, pl.BlockSpec(memory_space=pl.ANY)] + [vmem] * 3,
        out_specs=vmem,
        scratch_shapes=[
            pltpu.VMEM(outgoing.shape, outgoing.dtype),
            pltpu.VMEM(outgoing.shape, outgoing.dtype),
            pltpu.VMEM((group,) + outgoing.shape[1:], outgoing.dtype),
            pltpu.SemaphoreType.DMA((n,)),
            pltpu.SemaphoreType.DMA((n,)),
            pltpu.VMEM(outgoing.shape, outgoing.dtype),
            pltpu.SemaphoreType.DMA(()),
        ],
        compiler_params=pltpu.CompilerParams(
            collective_id=0, has_side_effects=True, vmem_limit_bytes=48 * 1024 * 1024
        ),
        cost_estimate=pl.CostEstimate(
            flops=4 * rows * channels * hid, transcendentals=rows * hid, bytes_accessed=4 * rows * channels * 2
        ),
    )(flux_tiles, tile_of_slot, used, state, gain.reshape(1, channels), w_up, w_down)


def atmos_body(n_lat, n_lon, kw, band, side, x_hbm, w_ref, atm_ref, gain_ref, up_hbm, down_hbm, fw_hbm, land_ref,
               out_ref, flux_ref, above, below, left, right, above_left, above_right, below_left, below_right,
               xf_ref, xs_ref, mixed_ref, up_ref, down_ref, fw_ref, sems, send_sems, recv_sems, wet_ref):
    rows, cols, channels = atm_ref.shape
    m = kw // 2
    got = (above, below, left, right, above_left, above_right, below_left, below_right)
    lat, lon = lax.axis_index("lat"), lax.axis_index("lon")
    has_up = lat > 0
    has_down = lat < n_lat - 1
    row_part = {1: pl.ds(rows - m, m), -1: pl.ds(0, m), 0: pl.ds(0, rows)}
    col_part = {1: pl.ds(cols - side, side), -1: pl.ds(0, side), 0: pl.ds(0, cols)}

    def exists(d_lat):
        return has_down if d_lat > 0 else (has_up if d_lat < 0 else lat >= 0)

    def exists_from(d_lat):
        return has_up if d_lat > 0 else (has_down if d_lat < 0 else lat >= 0)

    def target(d_lat, d_lon):
        return (lax.rem(lon + d_lon + n_lon, n_lon), lat + d_lat)

    barrier = pltpu.get_barrier_semaphore()
    for d_lat, d_lon in HALO_MOVES:
        @pl.when(exists(d_lat))
        def _():
            pl.semaphore_signal(barrier, inc=1, device_id=target(d_lat, d_lon), device_id_type=MESH)

    pl.semaphore_wait(barrier, 2 + 3 * has_up.astype(jnp.int32) + 3 * has_down.astype(jnp.int32))

    def halo_copy(p):
        d_lat, d_lon = HALO_MOVES[p]
        return pltpu.make_async_remote_copy(
            src_ref=x_hbm.at[row_part[d_lat], col_part[d_lon]],
            dst_ref=got[p],
            send_sem=send_sems.at[p],
            recv_sem=recv_sems.at[p],
            device_id=target(d_lat, d_lon),
            device_id_type=MESH,
        )

    for p, (d_lat, d_lon) in enumerate(HALO_MOVES):
        @pl.when(exists(d_lat))
        def _():
            halo_copy(p).start()

    weights = [
        pltpu.make_async_copy(up_hbm, up_ref, sems.at[0]),
        pltpu.make_async_copy(down_hbm, down_ref, sems.at[1]),
        pltpu.make_async_copy(fw_hbm, fw_ref, sems.at[2]),
    ]
    for copy in weights:
        copy.start()

    xf_ref[m:m + rows, 0:side, :] = jnp.zeros((rows, side, channels), jnp.float32)
    xf_ref[m:m + rows, side:side + cols, :] = atm_ref[...].astype(jnp.float32)
    xf_ref[m:m + rows, side + cols:, :] = jnp.zeros((rows, side, channels), jnp.float32)

    def shift_rows(lo, hi, c0, width):
        @pl.loop(lo, hi)
        def _(i):
            for q in range(kw):
                xs_ref[q, i, pl.ds(c0, width), :] = xf_ref[i, pl.ds(side - m + q + c0, width), :]

    def conv_band(r0, c0, width):
        for cb in range(channels // 128):
            lanes = pl.ds(cb * 128, 128)
            acc = [jnp.zeros((width, 128), jnp.float32) for _ in range(band)]
            for q in range(kw):
                for i in range(band + kw - 1):
                    line = xs_ref[q, r0 + i, pl.ds(c0, width), lanes]
                    for p in range(kw):
                        r = i - p
                        if 0 <= r < band:
                            acc[r] = acc[r] + line * w_ref[p, pl.ds(q, 1), lanes]
            for r in range(band):
                mixed_ref[r0 + r, pl.ds(c0, width), lanes] = acc[r]

    shift_rows(m, m + rows, 0, cols)
    bands = rows // band

    @pl.loop(1, bands - 1)
    def _(b):
        conv_band(b * band, 0, cols)

    for p, (d_lat, d_lon) in enumerate(HALO_MOVES):
        @pl.when(exists_from(d_lat))
        def _():
            halo_copy(p).wait_recv()

        @pl.when(jnp.logical_not(exists_from(d_lat)))
        def _():
            got[p][...] = jnp.zeros(got[p].shape, got[p].dtype)

    for r0, r1, l_ref, c_ref, r_ref in (
        (0, m, above_left, above, above_right),
        (m, m + rows, left, None, right),
        (m + rows, 2 * m + rows, below_left, below, below_right),
    ):
        xf_ref[r0:r1, 0:side, :] = l_ref[...].astype(jnp.float32)
        if c_ref is not None:
            xf_ref[r0:r1, side:side + cols, :] = c_ref[...].astype(jnp.float32)
        xf_ref[r0:r1, side + cols:, :] = r_ref[...].astype(jnp.float32)

    shift_rows(0, m, 0, cols)
    shift_rows(m + rows, rows + 2 * m, 0, cols)
    shift_rows(m, m + rows, 0, 8)
    shift_rows(m, m + rows, cols - 8, 8)

    @pl.loop(0, 2)
    def _(t):
        conv_band(t * (bands - 1) * band, 0, cols)

    @pl.loop(1, bands - 1)
    def _(b):
        conv_band(b * band, 0, 8)
        conv_band(b * band, cols - 8, 8)

    for copy in weights:
        copy.wait()

    for p, (d_lat, d_lon) in enumerate(HALO_MOVES):
        @pl.when(exists(d_lat))
        def _():
            halo_copy(p).wait_send()

    eye = (lax.broadcasted_iota(jnp.int32, (cols, cols), 0) == lax.broadcasted_iota(jnp.int32, (cols, cols), 1))
    land_t = lax.dot_general(
        eye.astype(jnp.bfloat16), land_ref[...].astype(jnp.bfloat16), (((1,), (1,)), ((), ())),
        preferred_element_type=jnp.float32,
    )
    for r in range(rows):
        wet_ref[r] = jnp.broadcast_to(land_t[:, r:r + 1], (cols, channels))

    chunk = 8

    @pl.loop(0, rows // chunk)
    def _(k):
        cells = chunk * cols
        mixed = mixed_ref[pl.ds(k * chunk, chunk)].reshape(cells, channels)
        average = jnp.mean(mixed, axis=-1, keepdims=True)
        centred = mixed - average
        spread = jnp.mean(centred * centred, axis=-1, keepdims=True)
        normed = (centred * lax.rsqrt(spread + 1e-06) * gain_ref[...]).astype(jnp.bfloat16)
        hidden = jax.nn.gelu(
            jnp.dot(normed, up_ref[...], preferred_element_type=jnp.float32), approximate=True
        ).astype(jnp.bfloat16)
        branch = jnp.dot(hidden, down_ref[...], preferred_element_type=jnp.float32)
        atmos = atm_ref[pl.ds(k * chunk, chunk)].reshape(cells, channels).astype(jnp.float32)
        new = (atmos + branch).astype(jnp.bfloat16)
        out_ref[pl.ds(k * chunk, chunk)] = new.reshape(chunk, cols, channels)
        flux = jnp.dot(new, fw_ref[...], preferred_element_type=jnp.float32)
        flux = flux * wet_ref[pl.ds(k * chunk, chunk)].reshape(cells, channels)
        flux_ref[pl.ds(k * cells, cells)] = flux.astype(jnp.bfloat16)


def atmosphere_block(conv_weight, atmosphere, gain, w_up, w_down, flux_weight, land_mask):
    rows, cols, channels = atmosphere.shape
    kw = conv_weight.shape[0]
    m = kw // 2
    side = 8
    hid = w_up.shape[1]
    vmem = pl.BlockSpec(memory_space=pltpu.VMEM)
    hbm = pl.BlockSpec(memory_space=pl.ANY)
    cells = rows * cols
    pieces = []
    for d_lat, d_lon in HALO_MOVES:
        pieces.append(pltpu.VMEM((m if d_lat else rows, side if d_lon else cols, channels), atmosphere.dtype))
    return pl.pallas_call(
        functools.partial(atmos_body, lax.axis_size("lat"), lax.axis_size("lon"), kw, 4, side),
        out_shape=(
            jax.ShapeDtypeStruct(atmosphere.shape, atmosphere.dtype),
            jax.ShapeDtypeStruct((cells, channels), jnp.bfloat16),
        ),
        in_specs=[hbm] + [vmem] * 3 + [hbm] * 3 + [vmem],
        out_specs=(vmem, vmem),
        scratch_shapes=pieces + [
            pltpu.VMEM((rows + kw - 1, cols + 2 * side, channels), jnp.float32),
            pltpu.VMEM((kw, rows + kw - 1, cols, channels), jnp.float32),
            pltpu.VMEM((rows, cols, channels), jnp.float32),
            pltpu.VMEM(w_up.shape, w_up.dtype),
            pltpu.VMEM(w_down.shape, w_down.dtype),
            pltpu.VMEM(flux_weight.shape, flux_weight.dtype),
            pltpu.SemaphoreType.DMA((3,)),
            pltpu.SemaphoreType.DMA((8,)),
            pltpu.SemaphoreType.DMA((8,)),
            pltpu.VMEM((rows, cols, channels), jnp.float32),
        ],
        compiler_params=pltpu.CompilerParams(
            collective_id=1, has_side_effects=True, vmem_limit_bytes=56 * 1024 * 1024
        ),
        cost_estimate=pl.CostEstimate(
            flops=2 * cells * channels * (kw * kw + 2 * hid + channels),
            transcendentals=cells * hid,
            bytes_accessed=cells * channels * 8,
        ),
    )(atmosphere, conv_weight, atmosphere, gain.reshape(1, channels), w_up, w_down, flux_weight, land_mask)


def normalize(values, scales):
    average = jnp.mean(values, axis=-1, keepdims=True)
    centred = values - average
    spread = jnp.mean(centred * centred, axis=-1, keepdims=True)
    return centred * lax.rsqrt(spread + 1e-06) * scales


def channel_mixer(values, scales, w_up, w_down):
    normed = normalize(values, scales).astype(jnp.bfloat16)
    hidden = jax.nn.gelu(
        jnp.dot(normed, w_up, preferred_element_type=jnp.float32), approximate=True
    ).astype(jnp.bfloat16)
    return jnp.dot(hidden, w_down, preferred_element_type=jnp.float32)


def per_device(
    atmosphere,
    conv_weight,
    atm_gain,
    atm_up,
    atm_down,
    flux_weight,
    land_mask,
    tile_owner,
    ocean_state,
    ocn_gain,
    ocn_up,
    ocn_down,
):
    lat_rows, lon_cols, channels = atmosphere.shape
    margin = conv_weight.shape[0] // 2
    owners = tile_owner.reshape(-1)
    tile_count = owners.shape[0]
    peer_count = ocean_state.shape[1]
    capacity = ocean_state.shape[2]
    tile_cells = ocean_state.shape[3]
    atmos_new, fluxes = atmosphere_block(
        conv_weight, atmosphere, atm_gain, atm_up, atm_down, flux_weight, land_mask
    )
    flux_tiles = fluxes.reshape(tile_count, tile_cells, channels)
    order = jnp.arange(tile_count, dtype=jnp.int32)
    earlier_same = (owners[:, None] == owners[None, :]) & (order[None, :] < order[:, None])
    slot_index = owners * capacity + jnp.sum(earlier_same.astype(jnp.int32), axis=1)
    hits = jnp.arange(peer_count * capacity, dtype=jnp.int32)[:, None] == slot_index[None, :]
    used = jnp.sum(hits.astype(jnp.int32), axis=1)
    tile_of_slot = jnp.sum(jnp.where(hits, order[None, :], 0), axis=1)
    ocean_out = exchange_and_ocean(
        flux_tiles, tile_of_slot, used, ocean_state[0], ocn_gain, ocn_up, ocn_down
    )[None]
    return (atmos_new, ocean_out)


def solution(mesh):
    placed = (
        P("lat", "lon", None),
        P(),
        P(),
        P(),
        P(),
        P(),
        P("lat", "lon"),
        P("lat", "lon", None),
        P(("lat", "lon"), None, None, None, None),
        P(),
        P(),
        P(),
    )
    return jax.shard_map(
        per_device,
        mesh=mesh,
        in_specs=placed,
        out_specs=(P("lat", "lon", None), P(("lat", "lon"), None, None, None, None)),
        check_vma=False,
    )
```

```python
import functools

import jax
import jax.numpy as jnp
from jax import lax
from jax.experimental import pallas as pl
from jax.experimental.pallas import tpu as pltpu
from jax.sharding import PartitionSpec as P

MESH = pl.DeviceIdType.MESH

AXES = ("lat", "lon")


HALO_MOVES = ((1, 0), (-1, 0), (0, 1), (0, -1), (1, 1), (1, -1), (-1, 1), (-1, -1))


def exchange_body(n_lon, n, group, flux_ref, tile_ref, used_ref, state_hbm, gain_ref, up_ref, down_ref,
                  res_ref, out_ref, recv_ref, stage_ref, send_sems, recv_sems, state_ref, state_sem):
    me = lax.axis_index("lat") * n_lon + lax.axis_index("lon")

    def coords(d):
        return (lax.rem(d, n_lon), lax.div(d, n_lon))

    barrier = pltpu.get_barrier_semaphore()

    @pl.loop(1, n)
    def _(j):
        pl.semaphore_signal(barrier, inc=1, device_id=coords(lax.rem(me + j, n)), device_id_type=MESH)

    state_copy = pltpu.make_async_copy(state_hbm, state_ref, state_sem)
    state_copy.start()

    capacity = out_ref.shape[1]

    @pl.loop(0, n * capacity // 8)
    def _(t8):
        for u in range(8):
            t = t8 * 8 + u
            k = tile_ref[t]
            cells = flux_ref[k]
            keep = jnp.full(cells.shape, used_ref[t], jnp.int32) > 0
            out_ref[t // capacity, t % capacity] = jnp.where(keep, cells, jnp.nan).astype(jnp.bfloat16)

    pl.semaphore_wait(barrier, n - 1)

    def send_copy(j):
        peer = lax.rem(me + j, n)
        return pltpu.make_async_remote_copy(
            src_ref=out_ref.at[peer],
            dst_ref=recv_ref.at[j],
            send_sem=send_sems.at[j],
            recv_sem=recv_sems.at[j],
            device_id=coords(peer),
            device_id_type=MESH,
        )

    def recv_copy(j):
        source = lax.rem(me - j + n, n)
        return pltpu.make_async_remote_copy(
            src_ref=out_ref.at[source],
            dst_ref=recv_ref.at[j],
            send_sem=send_sems.at[j],
            recv_sem=recv_sems.at[j],
            device_id=coords(source),
            device_id_type=MESH,
        )

    @pl.loop(1, n)
    def _(j):
        send_copy(j).start()

    recv_ref[0] = out_ref[me]
    state_copy.wait()
    slots, cells, channels = out_ref.shape[1], out_ref.shape[2], out_ref.shape[3]
    rows = group * slots * cells

    @pl.loop(0, n // group)
    def _(g):
        base = g * group

        @pl.loop(0, group)
        def _(i):
            j = base + i

            @pl.when(j > 0)
            def _():
                recv_copy(j).wait_recv()

            stage_ref[i] = state_ref[lax.rem(me - j + n, n)]

        fluxes = recv_ref[pl.ds(base, group)]
        used = fluxes[:, :, 0:1, 0:1] == fluxes[:, :, 0:1, 0:1]
        states = (stage_ref[...].astype(jnp.float32) + fluxes.astype(jnp.float32)).reshape(rows, channels)
        average = jnp.mean(states, axis=-1, keepdims=True)
        centred = states - average
        spread = jnp.mean(centred * centred, axis=-1, keepdims=True)
        normed = (centred * lax.rsqrt(spread + 1e-06) * gain_ref[...]).astype(jnp.bfloat16)
        hidden = jax.nn.gelu(
            jnp.dot(normed, up_ref[...], preferred_element_type=jnp.float32), approximate=True
        ).astype(jnp.bfloat16)
        result = states + jnp.dot(hidden, down_ref[...], preferred_element_type=jnp.float32)
        result = result.reshape(group, slots, cells, channels)
        stage_ref[...] = jnp.where(used, result, 0.0).astype(jnp.bfloat16)

        @pl.loop(0, group)
        def _(i):
            res_ref[lax.rem(me - base - i + n, n)] = stage_ref[i]

    @pl.loop(1, n)
    def _(j):
        send_copy(j).wait_send()


def exchange_and_ocean(flux_tiles, tile_of_slot, used, state, gain, w_up, w_down):
    n_lon = lax.axis_size("lon")
    n = n_lon * lax.axis_size("lat")
    group = 16
    outgoing = jax.ShapeDtypeStruct(state.shape, state.dtype)
    rows = outgoing.shape[0] * outgoing.shape[1] * outgoing.shape[2]
    channels, hid = w_up.shape
    vmem = pl.BlockSpec(memory_space=pltpu.VMEM)
    smem = pl.BlockSpec(memory_space=pltpu.SMEM)
    return pl.pallas_call(
        functools.partial(exchange_body, n_lon, n, group),
        out_shape=jax.ShapeDtypeStruct(outgoing.shape, outgoing.dtype),
        in_specs=[vmem, smem, smem, pl.BlockSpec(memory_space=pl.ANY)] + [vmem] * 3,
        out_specs=vmem,
        scratch_shapes=[
            pltpu.VMEM(outgoing.shape, outgoing.dtype),
            pltpu.VMEM(outgoing.shape, outgoing.dtype),
            pltpu.VMEM((group,) + outgoing.shape[1:], outgoing.dtype),
            pltpu.SemaphoreType.DMA((n,)),
            pltpu.SemaphoreType.DMA((n,)),
            pltpu.VMEM(outgoing.shape, outgoing.dtype),
            pltpu.SemaphoreType.DMA(()),
        ],
        compiler_params=pltpu.CompilerParams(
            collective_id=0, has_side_effects=True, vmem_limit_bytes=48 * 1024 * 1024
        ),
        cost_estimate=pl.CostEstimate(
            flops=4 * rows * channels * hid, transcendentals=rows * hid, bytes_accessed=4 * rows * channels * 2
        ),
    )(flux_tiles, tile_of_slot, used, state, gain.reshape(1, channels), w_up, w_down)


def atmos_body(n_lat, n_lon, kw, band, side, x_hbm, w_ref, atm_ref, gain_ref, up_hbm, down_hbm, fw_hbm, land_ref,
               out_ref, flux_ref, above, below, left, right, above_left, above_right, below_left, below_right,
               xf_ref, xs_ref, mixed_ref, up_ref, down_ref, fw_ref, sems, send_sems, recv_sems, wet_ref):
    rows, cols, channels = atm_ref.shape
    m = kw // 2
    got = (above, below, left, right, above_left, above_right, below_left, below_right)
    lat, lon = lax.axis_index("lat"), lax.axis_index("lon")
    has_up = lat > 0
    has_down = lat < n_lat - 1
    row_part = {1: pl.ds(rows - m, m), -1: pl.ds(0, m), 0: pl.ds(0, rows)}
    col_part = {1: pl.ds(cols - side, side), -1: pl.ds(0, side), 0: pl.ds(0, cols)}

    def exists(d_lat):
        return has_down if d_lat > 0 else (has_up if d_lat < 0 else lat >= 0)

    def exists_from(d_lat):
        return has_up if d_lat > 0 else (has_down if d_lat < 0 else lat >= 0)

    def target(d_lat, d_lon):
        return (lax.rem(lon + d_lon + n_lon, n_lon), lat + d_lat)

    barrier = pltpu.get_barrier_semaphore()
    for d_lat, d_lon in HALO_MOVES:
        @pl.when(exists(d_lat))
        def _():
            pl.semaphore_signal(barrier, inc=1, device_id=target(d_lat, d_lon), device_id_type=MESH)

    pl.semaphore_wait(barrier, 2 + 3 * has_up.astype(jnp.int32) + 3 * has_down.astype(jnp.int32))

    def halo_copy(p):
        d_lat, d_lon = HALO_MOVES[p]
        return pltpu.make_async_remote_copy(
            src_ref=x_hbm.at[row_part[d_lat], col_part[d_lon]],
            dst_ref=got[p],
            send_sem=send_sems.at[p],
            recv_sem=recv_sems.at[p],
            device_id=target(d_lat, d_lon),
            device_id_type=MESH,
        )

    for p, (d_lat, d_lon) in enumerate(HALO_MOVES):
        @pl.when(exists(d_lat))
        def _():
            halo_copy(p).start()

    weights = [
        pltpu.make_async_copy(up_hbm, up_ref, sems.at[0]),
        pltpu.make_async_copy(down_hbm, down_ref, sems.at[1]),
        pltpu.make_async_copy(fw_hbm, fw_ref, sems.at[2]),
    ]
    for copy in weights:
        copy.start()

    xf_ref[m:m + rows, 0:side, :] = jnp.zeros((rows, side, channels), jnp.float32)
    xf_ref[m:m + rows, side:side + cols, :] = atm_ref[...].astype(jnp.float32)
    xf_ref[m:m + rows, side + cols:, :] = jnp.zeros((rows, side, channels), jnp.float32)

    def shift_rows(lo, hi, c0, width):
        @pl.loop(lo, hi)
        def _(i):
            for q in range(kw):
                xs_ref[q, i, pl.ds(c0, width), :] = xf_ref[i, pl.ds(side - m + q + c0, width), :]

    def conv_band(r0, c0, width):
        for cb in range(channels // 128):
            lanes = pl.ds(cb * 128, 128)
            acc = [jnp.zeros((width, 128), jnp.float32) for _ in range(band)]
            for q in range(kw):
                for i in range(band + kw - 1):
                    line = xs_ref[q, r0 + i, pl.ds(c0, width), lanes]
                    for p in range(kw):
                        r = i - p
                        if 0 <= r < band:
                            acc[r] = acc[r] + line * w_ref[p, pl.ds(q, 1), lanes]
            for r in range(band):
                mixed_ref[r0 + r, pl.ds(c0, width), lanes] = acc[r]

    shift_rows(m, m + rows, 0, cols)
    bands = rows // band

    @pl.loop(1, bands - 1)
    def _(b):
        conv_band(b * band, 0, cols)

    for p, (d_lat, d_lon) in enumerate(HALO_MOVES):
        @pl.when(exists_from(d_lat))
        def _():
            halo_copy(p).wait_recv()

        @pl.when(jnp.logical_not(exists_from(d_lat)))
        def _():
            got[p][...] = jnp.zeros(got[p].shape, got[p].dtype)

    for r0, r1, l_ref, c_ref, r_ref in (
        (0, m, above_left, above, above_right),
        (m, m + rows, left, None, right),
        (m + rows, 2 * m + rows, below_left, below, below_right),
    ):
        xf_ref[r0:r1, 0:side, :] = l_ref[...].astype(jnp.float32)
        if c_ref is not None:
            xf_ref[r0:r1, side:side + cols, :] = c_ref[...].astype(jnp.float32)
        xf_ref[r0:r1, side + cols:, :] = r_ref[...].astype(jnp.float32)

    shift_rows(0, m, 0, cols)
    shift_rows(m + rows, rows + 2 * m, 0, cols)
    shift_rows(m, m + rows, 0, 8)
    shift_rows(m, m + rows, cols - 8, 8)

    @pl.loop(0, 2)
    def _(t):
        conv_band(t * (bands - 1) * band, 0, cols)

    @pl.loop(1, bands - 1)
    def _(b):
        conv_band(b * band, 0, 8)
        conv_band(b * band, cols - 8, 8)

    for copy in weights:
        copy.wait()

    for p, (d_lat, d_lon) in enumerate(HALO_MOVES):
        @pl.when(exists(d_lat))
        def _():
            halo_copy(p).wait_send()

    eye = (lax.broadcasted_iota(jnp.int32, (cols, cols), 0) == lax.broadcasted_iota(jnp.int32, (cols, cols), 1))
    land_t = lax.dot_general(
        eye.astype(jnp.bfloat16), land_ref[...].astype(jnp.bfloat16), (((1,), (1,)), ((), ())),
        preferred_element_type=jnp.float32,
    )
    for r in range(rows):
        wet_ref[r] = jnp.broadcast_to(land_t[:, r:r + 1], (cols, channels))

    chunk = 16

    @pl.loop(0, rows // chunk)
    def _(k):
        cells = chunk * cols
        mixed = mixed_ref[pl.ds(k * chunk, chunk)].reshape(cells, channels)
        average = jnp.mean(mixed, axis=-1, keepdims=True)
        centred = mixed - average
        spread = jnp.mean(centred * centred, axis=-1, keepdims=True)
        normed = (centred * lax.rsqrt(spread + 1e-06) * gain_ref[...]).astype(jnp.bfloat16)
        hidden = jax.nn.gelu(
            jnp.dot(normed, up_ref[...], preferred_element_type=jnp.float32), approximate=True
        ).astype(jnp.bfloat16)
        branch = jnp.dot(hidden, down_ref[...], preferred_element_type=jnp.float32)
        atmos = atm_ref[pl.ds(k * chunk, chunk)].reshape(cells, channels).astype(jnp.float32)
        new = (atmos + branch).astype(jnp.bfloat16)
        out_ref[pl.ds(k * chunk, chunk)] = new.reshape(chunk, cols, channels)
        flux = jnp.dot(new, fw_ref[...], preferred_element_type=jnp.float32)
        flux = flux * wet_ref[pl.ds(k * chunk, chunk)].reshape(cells, channels)
        flux_ref[pl.ds(k * cells, cells)] = flux.astype(jnp.bfloat16)


def atmosphere_block(conv_weight, atmosphere, gain, w_up, w_down, flux_weight, land_mask):
    rows, cols, channels = atmosphere.shape
    kw = conv_weight.shape[0]
    m = kw // 2
    side = 8
    hid = w_up.shape[1]
    vmem = pl.BlockSpec(memory_space=pltpu.VMEM)
    hbm = pl.BlockSpec(memory_space=pl.ANY)
    cells = rows * cols
    pieces = []
    for d_lat, d_lon in HALO_MOVES:
        pieces.append(pltpu.VMEM((m if d_lat else rows, side if d_lon else cols, channels), atmosphere.dtype))
    return pl.pallas_call(
        functools.partial(atmos_body, lax.axis_size("lat"), lax.axis_size("lon"), kw, 4, side),
        out_shape=(
            jax.ShapeDtypeStruct(atmosphere.shape, atmosphere.dtype),
            jax.ShapeDtypeStruct((cells, channels), jnp.bfloat16),
        ),
        in_specs=[hbm] + [vmem] * 3 + [hbm] * 3 + [vmem],
        out_specs=(vmem, vmem),
        scratch_shapes=pieces + [
            pltpu.VMEM((rows + kw - 1, cols + 2 * side, channels), jnp.float32),
            pltpu.VMEM((kw, rows + kw - 1, cols, channels), jnp.float32),
            pltpu.VMEM((rows, cols, channels), jnp.float32),
            pltpu.VMEM(w_up.shape, w_up.dtype),
            pltpu.VMEM(w_down.shape, w_down.dtype),
            pltpu.VMEM(flux_weight.shape, flux_weight.dtype),
            pltpu.SemaphoreType.DMA((3,)),
            pltpu.SemaphoreType.DMA((8,)),
            pltpu.SemaphoreType.DMA((8,)),
            pltpu.VMEM((rows, cols, channels), jnp.float32),
        ],
        compiler_params=pltpu.CompilerParams(
            collective_id=1, has_side_effects=True, vmem_limit_bytes=56 * 1024 * 1024
        ),
        cost_estimate=pl.CostEstimate(
            flops=2 * cells * channels * (kw * kw + 2 * hid + channels),
            transcendentals=cells * hid,
            bytes_accessed=cells * channels * 8,
        ),
    )(atmosphere, conv_weight, atmosphere, gain.reshape(1, channels), w_up, w_down, flux_weight, land_mask)


def normalize(values, scales):
    average = jnp.mean(values, axis=-1, keepdims=True)
    centred = values - average
    spread = jnp.mean(centred * centred, axis=-1, keepdims=True)
    return centred * lax.rsqrt(spread + 1e-06) * scales


def channel_mixer(values, scales, w_up, w_down):
    normed = normalize(values, scales).astype(jnp.bfloat16)
    hidden = jax.nn.gelu(
        jnp.dot(normed, w_up, preferred_element_type=jnp.float32), approximate=True
    ).astype(jnp.bfloat16)
    return jnp.dot(hidden, w_down, preferred_element_type=jnp.float32)


def per_device(
    atmosphere,
    conv_weight,
    atm_gain,
    atm_up,
    atm_down,
    flux_weight,
    land_mask,
    tile_owner,
    ocean_state,
    ocn_gain,
    ocn_up,
    ocn_down,
):
    lat_rows, lon_cols, channels = atmosphere.shape
    margin = conv_weight.shape[0] // 2
    owners = tile_owner.reshape(-1)
    tile_count = owners.shape[0]
    peer_count = ocean_state.shape[1]
    capacity = ocean_state.shape[2]
    tile_cells = ocean_state.shape[3]
    atmos_new, fluxes = atmosphere_block(
        conv_weight, atmosphere, atm_gain, atm_up, atm_down, flux_weight, land_mask
    )
    flux_tiles = fluxes.reshape(tile_count, tile_cells, channels)
    order = jnp.arange(tile_count, dtype=jnp.int32)
    earlier_same = (owners[:, None] == owners[None, :]) & (order[None, :] < order[:, None])
    slot_index = owners * capacity + jnp.sum(earlier_same.astype(jnp.int32), axis=1)
    hits = jnp.arange(peer_count * capacity, dtype=jnp.int32)[:, None] == slot_index[None, :]
    used = jnp.sum(hits.astype(jnp.int32), axis=1)
    tile_of_slot = jnp.sum(jnp.where(hits, order[None, :], 0), axis=1)
    ocean_out = exchange_and_ocean(
        flux_tiles, tile_of_slot, used, ocean_state[0], ocn_gain, ocn_up, ocn_down
    )[None]
    return (atmos_new, ocean_out)


def solution(mesh):
    placed = (
        P("lat", "lon", None),
        P(),
        P(),
        P(),
        P(),
        P(),
        P("lat", "lon"),
        P("lat", "lon", None),
        P(("lat", "lon"), None, None, None, None),
        P(),
        P(),
        P(),
    )
    return jax.shard_map(
        per_device,
        mesh=mesh,
        in_specs=placed,
        out_specs=(P("lat", "lon", None), P(("lat", "lon"), None, None, None, None)),
        check_vma=False,
    )
```
